32 devices in a mesh: dp: 2 (over core), ctx: 16 (over z, y, x).
Axes of the slice: x: 2, y: 2, z: 4, core: 2. Of those that a mesh axis runs over, the one named last changes fastest.
Arguments:
- block_input: bfloat16 [4, 2048, 512], P('dp', 'ctx'), may hold values from -6 to 6
- prefix: int32 [4], P('dp'), may hold values from 204 to 1024
- ln1_gain: bfloat16 [512], P('ctx'), may hold values from 0.099609375 to 1.8984375
- w_qkv: bfloat16 [512, 1536], P('dp', 'ctx'), may hold values from -0.25 to 0.25
- w_out: bfloat16 [512, 512], P('dp', 'ctx'), may hold values from -1 to 1
- ln2_gain: bfloat16 [512], P('ctx'), may hold values from 0.099609375 to 1.8984375
- w_up: bfloat16 [512, 2048], P('dp', 'ctx'), may hold values from -0.25 to 0.25
- w_down: bfloat16 [2048, 512], P('dp', 'ctx'), may hold values from -0.125 to 0.125
- grad_y: bfloat16 [4, 2048, 512], P('dp', 'ctx'), may hold values from -6 to 6
Outputs:
- output: bfloat16 [4, 2048, 512], P('dp', 'ctx')
- grad_x: float32 [4, 2048, 512], P('dp', 'ctx')
- grad_ln1: float32 [512], P('ctx')
- grad_qkv: float32 [512, 1536], P('dp', 'ctx')
- grad_out: float32 [512, 512], P('dp', 'ctx')
- grad_ln2: float32 [512], P('ctx')
- grad_up: float32 [512, 2048], P('dp', 'ctx')
- grad_down: float32 [2048, 512], P('dp', 'ctx')
The draws below stay inside these ranges and needn't reach their ends.
All inputs are finite; a program needn't handle non-finite values.
Results may differ from the reference program's by a relative error of at most 0.02.
Values may be sent and summed in bfloat16 or wider, within the bound.
A program may use at most 192 MiB of HBM per device.

```python
import math
import jax
import jax.numpy as jnp
from jax import lax

D = 512
H = 8
DH = 64
FF = 2048
LEN = 2048
SEQS = 4


def plant(result, rng, smallest, largest):
    longest = result.shape.index(max(result.shape))
    spots = []
    for shift in (0, 1):
        where = [jax.random.randint(jax.random.fold_in(rng, axis), (), 0, length) for axis, length in enumerate(result.shape)]
        where[longest] = (where[longest] + shift) % result.shape[longest]
        spots.append(tuple(where))
    return result.at[spots[0]].set(smallest).at[spots[1]].set(largest)


def steps_of(stream_key, shape, shards, low, high):
    factor_of, own = 1.0, jax.random.fold_in(stream_key, 6)
    for position, parts in shards:
        draws = jnp.exp(jax.random.uniform(jax.random.fold_in(own, position), (parts,), jnp.float32, low / len(shards), high / len(shards)))
        factor_of = factor_of * jnp.repeat(draws, shape[position] // parts).reshape([-1 if axis == position else 1 for axis in range(len(shape))])
    return factor_of


def scatter_about(own_key, extent, scale, most, cuts=(), kind=jnp.bfloat16):
    drawn = scale * jax.random.normal(own_key, extent, jnp.float32)
    if cuts:
        drawn = drawn * steps_of(own_key, extent, cuts, -0.22, 0.18)
    return jnp.clip(drawn, -most, most).astype(kind)


def setup_inputs(seed: int = 0) -> dict:
    seeds = jax.random.split(jax.random.key(seed), 10)
    block_input = scatter_about(seeds[0], (SEQS, LEN, D), 1.0, 6.0, ((0, 2), (1, 16)))
    prefix = plant(jax.random.randint(seeds[1], (SEQS,), LEN // 10, LEN // 2 + 1), jax.random.fold_in(seeds[1], 1), LEN // 10, (LEN // 2 + 1) - 1).astype(jnp.int32)
    ln1_gain = jnp.clip(1.0 + 0.18 * jax.random.normal(seeds[2], (D,), jnp.float32), 0.099609375, 1.8984375).astype(jnp.bfloat16)
    w_qkv = scatter_about(seeds[3], (D, 3 * D), D ** -0.5, 0.25, ((0, 2), (1, 16)))
    w_out = scatter_about(seeds[4], (D, D), (D // 16) ** -0.5, 1.0, ((0, 2), (1, 16)))
    ln2_gain = jnp.clip(1.0 + 0.18 * jax.random.normal(seeds[5], (D,), jnp.float32), 0.099609375, 1.8984375).astype(jnp.bfloat16)
    w_up = scatter_about(seeds[6], (D, FF), D ** -0.5, 0.25, ((0, 2), (1, 16)))
    w_down = scatter_about(seeds[7], (FF, D), FF ** -0.5, 0.125, ((0, 2), (1, 16)))
    grad_y = scatter_about(seeds[8], (SEQS, LEN, D), 1.0, 6.0, ((0, 2), (1, 16)))
    return {"block_input": block_input, "prefix": prefix, "ln1_gain": ln1_gain, "w_qkv": w_qkv, "w_out": w_out, "ln2_gain": ln2_gain, "w_up": w_up, "w_down": w_down, "grad_y": grad_y}


@jax.custom_vjp
def low(v):
    return lax.optimization_barrier(v.astype(jnp.bfloat16)).astype(jnp.float32)

@jax.custom_vjp
def low_back(v):
    return v

def low_keep(v):
    return (low(v), None)

def low_pass(kept, grad):
    return (grad,)

def back_keep(v):
    return (v, None)

def back_low(kept, grad):
    return (low(grad),)
low.defvjp(low_keep, low_pass)
low_back.defvjp(back_keep, back_low)
EPS = 1e-05
HIGH = lax.Precision.HIGHEST

def layer_norm(values, gain):
    centred = values - lax.optimization_barrier(jnp.mean(values, axis=-1, keepdims=True))
    spread = lax.optimization_barrier(jnp.mean(centred * centred, axis=-1, keepdims=True))
    return centred * lax.rsqrt(spread + EPS) * gain

def matmul(left, right):
    return jnp.dot(left, right, precision=HIGH, preferred_element_type=jnp.float32)

def forward_one(inputs, gain_one, w_proj, w_mix, gain_two, w_expand, w_reduce, prefix_len):
    length = inputs.shape[0]
    normed = low(layer_norm(inputs, gain_one))
    projected = low_back(low(matmul(normed, w_proj)))
    queries = projected[:, :D].reshape(length, H, DH)
    keys_all = projected[:, D:2 * D].reshape(length, H, DH)
    values_all = projected[:, 2 * D:].reshape(length, H, DH)
    q_block = math.gcd(length, 512)
    key_pos = jnp.arange(length, dtype=jnp.int32)

    def attend(packed):
        query_rows, first_row = packed
        scores = jnp.einsum('qhd,khd->hqk', query_rows, keys_all, precision=HIGH) * DH ** (-0.5)
        scores = low_back(scores)
        query_pos = first_row + jnp.arange(q_block, dtype=jnp.int32)
        visible = (key_pos[None, :] <= query_pos[:, None]) | (key_pos[None, :] < prefix_len)
        scores = jnp.where(visible[None], scores, -1e+30)
        weights = jax.nn.softmax(scores, axis=-1)
        return jnp.einsum('hqk,khd->qhd', low(weights), values_all, precision=HIGH)
    blocks = queries.reshape(length // q_block, q_block, H, DH)
    firsts = jnp.arange(length // q_block, dtype=jnp.int32) * q_block
    attended = lax.map(jax.checkpoint(attend), (blocks, firsts)).reshape(length, D)
    attended = low_back(low(attended))
    resid = inputs + low_back(matmul(attended, w_mix))
    normed_two = low(layer_norm(resid, gain_two))
    hidden_pre = low_back(matmul(normed_two, w_expand))
    activated = low(jax.nn.gelu(hidden_pre))
    return resid + low_back(matmul(activated, w_reduce))

def reference(block_input, prefix, ln1_gain, w_qkv, w_out, ln2_gain, w_up, w_down, grad_y):
    params = tuple((member.astype(jnp.float32) for member in (ln1_gain, w_qkv, w_out, ln2_gain, w_up, w_down)))

    def per_seq(totals, packed):
        inputs, prefix_len, cotangent = packed

        def apply_layer(values, *weights):
            return forward_one(values, *weights, prefix_len)
        output, pull = jax.vjp(apply_layer, inputs.astype(jnp.float32), *params)
        gradients = pull(cotangent.astype(jnp.float32))
        totals = tuple((total_now + grad_now for total_now, grad_now in zip(totals, gradients[1:])))
        return (totals, (output.astype(jnp.bfloat16), gradients[0]))
    zero_sums = tuple((jnp.zeros(member.shape, jnp.float32) for member in params))
    totals, (output, grad_input) = lax.scan(per_seq, zero_sums, (block_input, prefix, grad_y))
    return (output, grad_input, totals[0], totals[1], totals[2], totals[3], totals[4], totals[5])
```

```python
import functools
import math

import jax
import jax.numpy as jnp
from jax import lax
from jax.experimental import pallas as pl
from jax.experimental.pallas import tpu as pltpu
from jax.sharding import PartitionSpec as P

H = 8
MICRO = 2


EPS = 1e-05
NEG = -1e30

MESH = pl.DeviceIdType.MESH
F32 = jnp.float32
BF16 = jnp.bfloat16
NN = (((1,), (0,)), ((), ()))
NT = (((1,), (1,)), ((), ()))
TN = (((0,), (0,)), ((), ()))
GELU_A = math.sqrt(2.0 / math.pi)
GELU_B = 0.044715

NZ, NW, ND = 4, 2 * 2, 2
NC = NZ * NW
WORDS = 128
BQ = 2 * WORDS
DH = 64


def dot(a, b, dims=NN):
    return lax.dot_general(a, b, dims, preferred_element_type=F32)


def sum_rows(v):
    return jnp.sum(v, axis=0, keepdims=True)


class Wires:
    def __init__(self, send, recv):
        self.send, self.recv, self.used, self.open = send, recv, 0, []

    def slots(self, count):
        first = self.used
        self.used += count
        return first

    def copy(self, src, dst, slot, device):
        return pltpu.make_async_remote_copy(
            src_ref=src,
            dst_ref=dst,
            send_sem=self.send.at[slot],
            recv_sem=self.recv.at[slot],
            device_id=device,
            device_id_type=MESH,
        )

    def start(self, src, dst, slot, device):
        c = self.copy(src, dst, slot, device)
        c.start()
        self.open.append(c)

    def landed(self, dst, slot, device):
        self.copy(dst, dst, slot, device).wait_recv()

    def drain(self):
        for c in self.open:
            c.wait_send()


class Place:
    def __init__(self):
        self.me = lax.axis_index("ctx")
        self.d = lax.axis_index("dp")
        self.z = self.me // NW
        self.w = lax.rem(self.me, NW)
        x, y = lax.rem(self.w, 2), self.w // 2
        self.w1 = y * 2 + (1 - x)
        self.w2 = (1 - y) * 2 + x
        self.w3 = (1 - y) * 2 + (1 - x)
        self.other = 1 - self.d
        self.partner = {"dp": self.other}
        self.across_x = {"ctx": self.z * NW + self.w1}
        self.across_y = {"ctx": self.z * NW + self.w2}

    def up(self, step):
        return lax.rem(self.z + step, NZ)

    def down(self, step):
        return lax.rem(self.z - step + NZ, NZ)

    def along_z(self, step):
        return {"ctx": self.up(step) * NW + self.w}


class Gather:
    def __init__(self, wires, place, buf):
        self.wires, self.at, self.buf = wires, place, buf
        self.half = buf.shape[3] // 2
        self.sz = wires.slots(NZ - 1)
        self.sx, self.sy = wires.slots(NZ), wires.slots(NZ)
        self.se, self.sf = wires.slots(NZ), wires.slots(NZ)
        self.sp = wires.slots(4 * NZ)

    def block(self, step, w):
        return self.buf.at[self.at.d, self.at.down(step), w]

    def top(self, ref):
        return ref.at[pl.ds(0, self.half)]

    def low(self, ref):
        return ref.at[pl.ds(self.half, self.half)]

    def send_z(self, src):
        p = self.at
        for step in range(1, NZ):
            self.wires.start(src, self.block(0, p.w), self.sz + step - 1, p.along_z(step))

    def wait_z(self, step):
        self.wires.landed(self.block(step, self.at.w), self.sz + step - 1, self.at.along_z(step))

    def send_plane(self, step):
        p, b = self.at, self.block(step, self.at.w)
        self.wires.start(b, b, self.sx + step, p.across_x)
        self.wires.start(b, b, self.sy + step, p.across_y)

    def send_core(self, group, step):
        p = self.at
        b = self.block(step, (p.w, p.w1, p.w2, p.w3)[group])
        self.wires.start(b, b, self.sp + group * NZ + step, p.partner)

    def relay_plane(self, step):
        p = self.at
        bx, by = self.block(step, p.w1), self.block(step, p.w2)
        self.wires.landed(bx, self.sx + step, p.across_x)
        self.wires.start(self.top(bx), self.top(bx), self.se + step, p.across_y)
        self.send_core(1, step)
        self.wires.landed(by, self.sy + step, p.across_y)
        self.wires.start(self.low(by), self.low(by), self.sf + step, p.across_x)
        self.send_core(2, step)

    def relay_corner(self, step):
        p, b = self.at, self.block(step, self.at.w3)
        self.wires.landed(self.top(b), self.se + step, p.across_y)
        self.wires.landed(self.low(b), self.sf + step, p.across_x)
        self.send_core(3, step)

    def wait_core(self):
        p = self.at
        for group, w in enumerate((p.w, p.w1, p.w2, p.w3)):
            for step in range(NZ):
                b = self.buf.at[p.other, p.down(step), w]
                self.wires.landed(b, self.sp + group * NZ + step, p.partner)


class Scatter:
    def __init__(self, wires, place, buf, from_core, from_x, from_y, relay, column, from_z):
        self.wires, self.at, self.buf = wires, place, buf
        self.from_core, self.from_x, self.from_y = from_core, from_x, from_y
        self.relay, self.column, self.from_z = relay, column, from_z
        self.rows = buf.shape[3]
        self.half = self.rows // 2
        self.sp = wires.slots(1)
        self.sx, self.sy = wires.slots(3), wires.slots(3)
        self.sz = wires.slots(NZ - 1)

    def part(self, w, low):
        return self.buf.at[self.at.d, :, w, pl.ds(self.half if low else 0, self.half)]

    def send_core(self):
        p = self.at
        self.wires.start(self.buf.at[p.other], self.from_core, self.sp, p.partner)

    def add_core(self):
        p = self.at
        self.wires.landed(self.from_core, self.sp, p.partner)

        def add(k, carry):
            z, w = k // NW, lax.rem(k, NW)
            mine = self.buf[p.d, z, w].astype(F32)
            self.buf[p.d, z, w] = (mine + self.from_core[z, w].astype(F32)).astype(BF16)
            return carry

        lax.fori_loop(0, NC, add, 0)

    def send_plane(self):
        p = self.at
        for k, w in enumerate((p.w3, p.w1)):
            self.wires.start(self.part(w, False), self.from_x.at[k], self.sx + k, p.across_x)
        for k, w in enumerate((p.w3, p.w2)):
            self.wires.start(self.part(w, True), self.from_y.at[k], self.sy + k, p.across_y)

    def relay_corner(self):
        p, h = self.at, self.half
        self.wires.landed(self.from_x.at[0], self.sx, p.across_x)

        def add_top(z, carry):
            mine = self.buf[p.d, z, p.w2, pl.ds(0, h)].astype(F32)
            self.relay[0, z] = (mine + self.from_x[0, z].astype(F32)).astype(BF16)
            return carry

        lax.fori_loop(0, NZ, add_top, 0)
        self.wires.start(self.relay.at[0], self.from_y.at[2], self.sy + 2, p.across_y)
        self.wires.landed(self.from_y.at[0], self.sy, p.across_y)

        def add_low(z, carry):
            mine = self.buf[p.d, z, p.w1, pl.ds(h, h)].astype(F32)
            self.relay[1, z] = (mine + self.from_y[0, z].astype(F32)).astype(BF16)
            return carry

        lax.fori_loop(0, NZ, add_low, 0)
        self.wires.start(self.relay.at[1], self.from_x.at[2], self.sx + 2, p.across_x)

    def send_z(self):
        p, h = self.at, self.half
        self.wires.landed(self.from_x.at[1], self.sx + 1, p.across_x)
        self.wires.landed(self.from_y.at[1], self.sy + 1, p.across_y)
        self.wires.landed(self.from_y.at[2], self.sy + 2, p.across_y)
        self.wires.landed(self.from_x.at[2], self.sx + 2, p.across_x)

        def add(z, carry):
            top = self.buf[p.d, z, p.w, pl.ds(0, h)].astype(F32)
            top = top + self.from_x[1, z].astype(F32) + self.from_y[2, z].astype(F32)
            self.column[z, pl.ds(0, h)] = top.astype(BF16)
            low = self.buf[p.d, z, p.w, pl.ds(h, h)].astype(F32)
            low = low + self.from_y[1, z].astype(F32) + self.from_x[2, z].astype(F32)
            self.column[z, pl.ds(h, h)] = low.astype(BF16)
            return carry

        lax.fori_loop(0, NZ, add, 0)
        for step in range(1, NZ):
            self.wires.start(
                self.column.at[p.up(step)], self.from_z.at[step - 1], self.sz + step - 1, p.along_z(step)
            )

    def total(self):
        p = self.at
        for step in range(1, NZ):
            self.wires.landed(self.from_z.at[step - 1], self.sz + step - 1, p.along_z(step))
        acc = self.column[p.z].astype(F32)
        for step in range(1, NZ):
            acc = acc + self.from_z[step - 1].astype(F32)
        return acc


class Exchange:
    def __init__(self, wires, place, src, dst, inner=None):
        self.wires, self.at, self.src, self.dst = wires, place, src, dst
        self.inner = inner
        self.first = wires.slots(NC - 1)

    def view(self, ref, k):
        return ref.at[k] if self.inner is None else ref.at[k, self.inner]

    def slot(self, offset):
        return self.first + offset - 1

    def send(self, offset):
        to = lax.rem(self.at.me + offset, NC)
        return self.wires.copy(
            self.view(self.src, to), self.view(self.dst, self.at.me), self.slot(offset), {"ctx": to}
        )

    def send_to(self, chip):
        offset = lax.rem(chip - self.at.me + NC, NC)

        @pl.when(offset > 0)
        def _():
            self.send(offset).start()

        @pl.when(offset == 0)
        def _():
            self.keep()

    def keep(self):
        me = self.at.me
        if self.inner is None:
            self.dst[me] = self.src[me]
        else:
            self.dst[me, self.inner] = self.src[me, self.inner]

    def send_all(self):
        for offset in range(1, NC):
            self.send(offset).start()
        self.keep()

    def wait(self):
        for offset in range(1, NC):
            frm = lax.rem(self.at.me - offset + NC, NC)
            dst = self.view(self.dst, frm)
            self.wires.copy(dst, dst, self.slot(offset), {"ctx": frm}).wait_recv()

    def drain(self):
        for offset in range(1, NC):
            self.send(offset).wait_send()


def norm_stats(v):
    centred = v - jnp.mean(v, axis=0, keepdims=True)
    rstd = lax.rsqrt(jnp.mean(centred * centred, axis=0, keepdims=True) + EPS)
    return centred * rstd, rstd


def norm_back(grad, hat, rstd, gain):
    g = grad * gain
    return rstd * (g - jnp.mean(g, axis=0, keepdims=True) - hat * jnp.mean(g * hat, axis=0, keepdims=True))


def gelu_both(p):
    t = jnp.tanh(GELU_A * (p + GELU_B * p * p * p))
    half = 0.5 * (1.0 + t)
    slope = half + 0.5 * p * (1.0 - t * t) * (GELU_A * (1.0 + 3.0 * GELU_B * p * p))
    return p * half, slope


def step_kernel(
    prefix_ref, x_ref, dy_ref, pack_ref,
    out_ref, gx_ref, gq_ref, gf_ref, gains_ref,
    send_sem, recv_sem, own_sem,
    QG, FG, HAT1, RST1, NRM, DYT,
    QS, QR, KN, VN, SC, PR, OT, LI, AS, AR, ATT,
    RES, HAT2, RST2, NRM2, ACT, SLOPE, DPRE, ACC, DRES, DAI,
    DS, DR, DAP, DEL, DQ, DQS, DPR, DPJ,
    GF, GFC, GFX, GFY, GFR, GFS, GFZ,
    GQ, GQC, GQX, GQY, GQR, GQS, GQZ,
    TS, TR,
):
    place = Place()
    wires = Wires(send_sem, recv_sem)
    me = place.me
    width = HAT1.shape[0]
    heads = width // DH
    half = width // 2
    qrows, frows = QG.shape[3], FG.shape[3]
    nq = PR.shape[0]
    pre_blocks = (nq * BQ // 2) // BQ

    gq = Gather(wires, place, QG)
    gf = Gather(wires, place, FG)
    qkv_x = Exchange(wires, place, QS, QR)
    att_x = Exchange(wires, place, AS, AR)
    datt_x = Exchange(wires, place, DS, DR)
    dkv_x = Exchange(wires, place, DQS, DPR, pl.ds(1, 2))
    dq_x = Exchange(wires, place, DQS, DPR, pl.ds(0, 1))
    sf = Scatter(wires, place, GF, GFC, GFX, GFY, GFR, GFS, GFZ)
    sq = Scatter(wires, place, GQ, GQC, GQX, GQY, GQR, GQS, GQZ)
    tot = wires.slots(6)

    barrier = pltpu.get_barrier_semaphore()
    for offset in range(1, NC):
        pl.semaphore_signal(barrier, inc=1, device_id={"ctx": lax.rem(me + offset, NC)}, device_id_type=MESH)
    pl.semaphore_signal(barrier, inc=1, device_id=place.partner, device_id_type=MESH)

    own_q = pltpu.make_async_copy(pack_ref.at[pl.ds(0, qrows)], gq.block(0, place.w), own_sem.at[0])
    own_f = pltpu.make_async_copy(pack_ref.at[pl.ds(qrows, frows)], gf.block(0, place.w), own_sem.at[1])
    own_q.start()
    own_f.start()
    own_q.wait()
    own_f.wait()
    pl.semaphore_wait(barrier, NC)

    gq.send_z(gq.block(0, place.w))
    gq.send_plane(0)
    gq.send_core(0, 0)

    hat, rstd = norm_stats(x_ref[...].astype(F32).T)
    HAT1[...] = hat
    RST1[...] = rstd
    DYT[...] = dy_ref[...].astype(F32).T.astype(BF16)

    for step in range(1, NZ):
        gq.wait_z(step)
        gq.send_plane(step)
        gq.send_core(0, step)
    gf.send_z(gf.block(0, place.w))
    for step in range(NZ):
        gq.relay_plane(step)
    for step in range(NZ):
        gq.relay_corner(step)
    gq.wait_core()

    gains = QG[0, :, :, pl.ds(0, 32), :].reshape(width, 256)
    gain_one = gains[:, 0:1].astype(F32)
    gain_two = gains[:, 128:129].astype(F32)
    NRM[...] = (HAT1[...] * gain_one).astype(BF16)
    wrows = qrows - 32
    for j in range(NZ):
        proj = sum(
            dot(QG[k, j, :, pl.ds(32, wrows), :].reshape(NW * wrows, 256), NRM[k * half:(k + 1) * half])
            for k in range(ND)
        )
        for t in range(NW * wrows // DH):
            kind, head = divmod(j * (NW * wrows // DH) + t, heads)
            unit = proj[t * DH:(t + 1) * DH].astype(BF16)
            if kind == 0:
                unit = (unit.astype(F32) * DH ** (-0.5)).astype(BF16)
            for b in range(2):
                QS[b * heads + head, kind] = unit[:, b * WORDS:(b + 1) * WORDS]
    qkv_x.send_all()

    gf.send_plane(0)
    gf.send_core(0, 0)
    for step in range(1, NZ):
        gf.wait_z(step)
        gf.send_plane(step)
        gf.send_core(0, step)

    qkv_x.wait()
    prefix = prefix_ref[me // heads]

    def to_rows(c, carry):
        rows = pl.ds(pl.multiple_of(c * WORDS, WORDS), WORDS)
        KN[rows, :] = QR[c, 1].astype(F32).T.astype(BF16)
        VN[rows, :] = QR[c, 2].astype(F32).T.astype(BF16)
        return carry

    lax.fori_loop(0, NC, to_rows, 0)

    def pair(ref, b, kind=None):
        if kind is None:
            return jnp.concatenate([ref[2 * b], ref[2 * b + 1]], axis=1)
        return jnp.concatenate([ref[2 * b, kind], ref[2 * b + 1, kind]], axis=1)

    def rows_of(b):
        return pl.ds(pl.multiple_of(b * BQ, BQ), BQ)

    def attend(qb, carry):
        queries = pair(QR, qb, 0)

        def scores(masked, kb, top):
            s = dot(KN[rows_of(kb), :], queries)
            if masked:
                key = kb * BQ + lax.broadcasted_iota(jnp.int32, (BQ, BQ), 0)
                word = qb * BQ + lax.broadcasted_iota(jnp.int32, (BQ, BQ), 1)
                s = jnp.where((key <= word) | (key < prefix), s, NEG)
            SC[rows_of(kb), :] = s
            return jnp.maximum(top, jnp.max(s.reshape(BQ // 8, 8, BQ), axis=0))

        last = jnp.maximum(qb + 1, pre_blocks)
        top = jnp.full((8, BQ), NEG, F32)
        top = lax.fori_loop(0, qb, functools.partial(scores, False), top)
        top = lax.fori_loop(qb, last, functools.partial(scores, True), top)
        top = jnp.max(top, axis=0, keepdims=True)

        def weigh(kb, state):
            total, acc = state
            p = jnp.exp(SC[rows_of(kb), :] - top)
            total = total + jnp.sum(p.reshape(BQ // 8, 8, BQ), axis=0)
            p = p.astype(BF16)
            PR[qb, rows_of(kb), :] = p
            return total, acc + dot(pair(QR, kb, 2), p)

        total, acc = lax.fori_loop(0, last, weigh, (jnp.zeros((8, BQ), F32), jnp.zeros((DH, BQ), F32)))
        inv = 1.0 / jnp.sum(total, axis=0, keepdims=True)
        out = acc * inv
        OT[qb] = out
        LI[qb] = inv
        out = out.astype(BF16)
        for k in range(2):
            AS[2 * qb + k] = out[:, k * WORDS:(k + 1) * WORDS]
            att_x.send_to(2 * qb + k)
        return carry

    lax.fori_loop(0, nq // 2, attend, 0)
    for step in range(NZ):
        gf.relay_plane(step)
    lax.fori_loop(nq // 2, nq, attend, 0)
    for step in range(NZ):
        gf.relay_corner(step)

    att_x.wait()
    gf.wait_core()
    for h in range(heads):
        ATT[h * DH:(h + 1) * DH] = jnp.concatenate([AR[h], AR[heads + h]], axis=1)

    orow = width // NC
    urow = ACT.shape[0] * BQ // NC
    nf = ACT.shape[0]

    def w_out(k):
        return FG[k, :, :, pl.ds(0, orow), :].reshape(width, 256)

    def w_up(k, c):
        return FG[k, c // 2, pl.ds(2 * (c % 2), 2), pl.ds(orow, urow), :].reshape(BQ, 256)

    def w_down(c):
        rows = orow + urow + (c % 4) * orow
        return FG[c // 4, :, :, pl.ds(rows, orow), :].reshape(width, 256)

    mixed = sum(dot(w_out(k), ATT[k * half:(k + 1) * half]) for k in range(ND))
    res = x_ref[...].astype(F32).T + mixed
    RES[...] = res
    hat2, rstd2 = norm_stats(res)
    HAT2[...] = hat2
    RST2[...] = rstd2
    NRM2[...] = (hat2 * gain_two).astype(BF16)

    for c in range(nf):
        pre = sum(dot(w_up(k, c), NRM2[k * half:(k + 1) * half]) for k in range(ND))
        act, slope = gelu_both(pre)
        ACT[c] = act.astype(BF16)
        SLOPE[c] = slope
    ACC[...] = jnp.zeros_like(ACC)
    for c in range(nf):
        dact = dot(w_down(c), DYT[...], TN)
        dpre = (dact * SLOPE[c]).astype(BF16)
        DPRE[c] = dpre
        for k in range(ND):
            ACC[k * half:(k + 1) * half] += dot(w_up(k, c), dpre, TN)
    dn2 = ACC[...]
    dres = DYT[...].astype(F32) + norm_back(dn2, HAT2[...], RST2[...], gain_two)
    DRES[...] = dres
    DAI[...] = dres.astype(BF16)
    ones = jnp.ones((8, 2 * WORDS), F32)
    row_two = lax.dot_general(
        ones, dn2 * HAT2[...], NT, precision=lax.Precision.HIGHEST, preferred_element_type=F32
    )
    for k in range(ND):
        datt = dot(w_out(k), DAI[...], TN).astype(BF16)
        for t in range(half // DH):
            h = k * (half // DH) + t
            for b in range(2):
                DS[b * heads + h] = datt[t * DH:(t + 1) * DH, b * WORDS:(b + 1) * WORDS]
    datt_x.send_all()

    for r in range(2):
        acc = RES[r * half:(r + 1) * half]
        for c in range(nf):
            rows = orow + urow + (c % 4) * orow
            w = FG[c // 4, pl.ds(2 * r, 2), :, pl.ds(rows, orow), :].reshape(half, 256)
            acc = acc + dot(w, ACT[c])
        out_ref[r * half:(r + 1) * half] = acc.astype(BF16)
    for c in range(nf):
        rows = orow + urow + (c % 4) * orow
        GF[c // 4, :, :, pl.ds(rows, orow), :] = dot(DYT[...], ACT[c], NT).astype(BF16).reshape(NZ, NW, orow, 256)
        for k in range(ND):
            up = dot(DPRE[c], NRM2[k * half:(k + 1) * half], NT).astype(BF16)
            GF[k, c // 2, pl.ds(2 * (c % 2), 2), pl.ds(orow, urow), :] = up.reshape(2, urow, 256)
    for k in range(ND):
        mix = dot(DAI[...], ATT[k * half:(k + 1) * half], NT).astype(BF16)
        GF[k, :, :, pl.ds(0, orow), :] = mix.reshape(NZ, NW, orow, 256)
    sf.send_core()

    datt_x.wait()

    def ready(qb, carry):
        datt = pair(DR, qb).astype(F32)
        inv = LI[qb]
        DEL[qb] = sum_rows(datt * OT[qb]) * inv
        DAP[qb] = (datt * inv).astype(BF16)
        DQ[qb] = jnp.zeros((DH, BQ), F32)
        return carry

    lax.fori_loop(0, nq, ready, 0)

    def put(ref, b, kind, val):
        val = val.astype(BF16)
        for k in range(2):
            ref[2 * b + k, kind] = val[:, k * WORDS:(k + 1) * WORDS]

    def send_dq(qb):
        put(DQS, qb, 0, DQ[qb] * DH ** (-0.5))
        for k in range(2):
            dq_x.send_to(2 * qb + k)

    def attend_back(kb, carry):
        keys, vals, keys_t = KN[rows_of(kb), :], VN[rows_of(kb), :], pair(QR, kb, 1)
        first = jnp.where(kb < pre_blocks, 0, kb)

        def one(qb, state):
            dk, dv = state
            dp = dot(vals, DAP[qb])
            p = PR[qb, rows_of(kb), :]
            ds = (p.astype(F32) * (dp - DEL[qb])).astype(BF16)
            DQ[qb] += dot(keys_t, ds)
            return dk + dot(pair(QR, qb, 0), ds, NT), dv + dot(DAP[qb], p, NT)

        zero = jnp.zeros((DH, BQ), F32)
        dk, dv = lax.fori_loop(first, nq, one, (zero, zero))
        put(DQS, kb, 1, dk)
        put(DQS, kb, 2, dv)
        for k in range(2):
            dkv_x.send_to(2 * kb + k)
        return carry

    def late(kb, carry):
        attend_back(kb, 0)
        send_dq(kb)
        return carry

    def early_dq(qb, carry):
        send_dq(qb)
        return carry

    lax.fori_loop(0, 1, attend_back, 0)
    sf.add_core()
    sf.send_plane()
    lax.fori_loop(1, pre_blocks, attend_back, 0)
    lax.fori_loop(0, pre_blocks, early_dq, 0)
    lax.fori_loop(pre_blocks, nq, late, 0)
    sf.relay_corner()
    dq_x.wait()
    dkv_x.wait()

    for kind in range(3):
        for h in range(heads):
            r = (kind * heads + h) * DH
            DPJ[r:r + DH] = jnp.concatenate([DPR[h, kind], DPR[heads + h, kind]], axis=1)
    blk = NW * wrows
    for j in range(NZ):
        for k in range(ND):
            g = dot(DPJ[j * blk:(j + 1) * blk], NRM[k * half:(k + 1) * half], NT)
            GQ[k, j] = g.astype(BF16).reshape(NW, wrows, 256)
    sq.send_core()
    sf.send_z()
    ACC[...] = jnp.zeros_like(ACC)
    for k in range(ND):
        for j in range(NZ):
            w = QG[k, j, :, pl.ds(32, wrows), :].reshape(blk, 256)
            ACC[k * half:(k + 1) * half] += dot(w, DPJ[j * blk:(j + 1) * blk], TN)
    dn1 = ACC[...]
    gx_ref[...] = DRES[...] + norm_back(dn1, HAT1[...], RST1[...], gain_one)
    row_one = lax.dot_general(
        ones, dn1 * HAT1[...], NT, precision=lax.Precision.HIGHEST, preferred_element_type=F32
    )

    TS[0] = jnp.where(lax.broadcasted_iota(jnp.int32, (8, width), 0) == 0, row_one, row_two)
    wires.start(TS.at[0], TR.at[0], tot, place.partner)
    sq.add_core()
    sq.send_plane()
    wires.landed(TR.at[0], tot, place.partner)
    TS[1] = TS[0] + TR[0]
    wires.start(TS.at[1], TR.at[1], tot + 1, place.across_x)
    sq.relay_corner()
    wires.landed(TR.at[1], tot + 1, place.across_x)
    TS[2] = TS[1] + TR[1]
    wires.start(TS.at[2], TR.at[2], tot + 2, place.across_y)
    gf_ref[...] = sf.total()
    sq.send_z()
    wires.landed(TR.at[2], tot + 2, place.across_y)
    TS[3] = TS[2] + TR[2]
    for step in range(1, NZ):
        wires.start(TS.at[3], TR.at[2 + step], tot + 2 + step, place.along_z(step))
    gq_ref[...] = sq.total()
    for step in range(1, NZ):
        wires.landed(TR.at[2 + step], tot + 2 + step, place.along_z(step))
    gains_ref[...] = TS[3] + TR[3] + TR[4] + TR[5]

    wires.drain()
    for x in (qkv_x, att_x, datt_x, dkv_x, dq_x):
        x.drain()


def fused(ctx_count, block_input, prefix, ln1_gain, w_qkv, w_out, ln2_gain, w_up, w_down, grad_y):
    width = block_input.shape[2]
    ff = w_down.shape[0] * ND
    words = 2 * WORDS
    nq = NC * WORDS // BQ
    nf = ff // BQ
    orow, qrow, urow = width // NC, 3 * width // NC, ff // NC
    qrows, frows = 32 + qrow, orow + urow + 4 * orow

    gains = jnp.concatenate(
        [jnp.broadcast_to(g[:, None], (orow, 128)) for g in (ln1_gain, ln2_gain)], axis=1
    )
    down = jnp.swapaxes(w_down.T.reshape(orow, 4, 256), 0, 1).reshape(4 * orow, 256)
    pack = jnp.concatenate([gains, w_qkv.T, w_out.T, w_up.T, down], axis=0)
    x = block_input.reshape(words, width)
    dy = grad_y.reshape(words, width)

    def vm(*shape, dtype=BF16):
        return pltpu.VMEM(shape, dtype)

    def scatter_bufs(rows):
        return [
            vm(ND, NZ, NW, rows, 256),
            vm(NZ, NW, rows, 256),
            vm(3, NZ, rows // 2, 256),
            vm(3, NZ, rows // 2, 256),
            vm(2, NZ, rows // 2, 256),
            vm(NZ, rows, 256),
            vm(NZ - 1, rows, 256),
        ]

    length = NC * WORDS
    msgs = 512
    vmem = pl.BlockSpec(memory_space=pltpu.VMEM)
    out, gx, gq, gf, tot = pl.pallas_call(
        step_kernel,
        out_shape=(
            jax.ShapeDtypeStruct((width, words), BF16),
            jax.ShapeDtypeStruct((width, words), F32),
            jax.ShapeDtypeStruct((qrow, 256), F32),
            jax.ShapeDtypeStruct((frows, 256), F32),
            jax.ShapeDtypeStruct((8, width), F32),
        ),
        in_specs=[pl.BlockSpec(memory_space=pltpu.SMEM), vmem, vmem, vmem],
        out_specs=(vmem,) * 5,
        scratch_shapes=[
            pltpu.SemaphoreType.DMA((N_SEMS,)),
            pltpu.SemaphoreType.DMA((N_SEMS,)),
            pltpu.SemaphoreType.DMA((2,)),
            vm(ND, NZ, NW, qrows, 256),
            vm(ND, NZ, NW, frows, 256),
            vm(width, words, dtype=F32),
            vm(1, words, dtype=F32),
            vm(width, words),
            vm(width, words),
            vm(NC, 3, DH, WORDS),
            vm(NC, 3, DH, WORDS),
            vm(length, DH),
            vm(length, DH),
            vm(length, BQ, dtype=F32),
            vm(nq, length, BQ),
            vm(nq, DH, BQ, dtype=F32),
            vm(nq, 1, BQ, dtype=F32),
            vm(NC, DH, WORDS),
            vm(NC, DH, WORDS),
            vm(width, words),
            vm(width, words, dtype=F32),
            vm(width, words, dtype=F32),
            vm(1, words, dtype=F32),
            vm(width, words),
            vm(nf, BQ, words),
            vm(nf, BQ, words, dtype=F32),
            vm(nf, BQ, words),
            vm(width, words, dtype=F32),
            vm(width, words, dtype=F32),
            vm(width, words),
            vm(NC, DH, WORDS),
            vm(NC, DH, WORDS),
            vm(nq, DH, BQ),
            vm(nq, 1, BQ, dtype=F32),
            vm(nq, DH, BQ, dtype=F32),
            vm(NC, 3, DH, WORDS),
            vm(NC, 3, DH, WORDS),
            vm(3 * width, words),
            *scatter_bufs(frows),
            *scatter_bufs(qrow),
            vm(4, 8, width, dtype=F32),
            vm(6, 8, width, dtype=F32),
        ],
        compiler_params=pltpu.CompilerParams(
            collective_id=0, has_side_effects=True, vmem_limit_bytes=66 * 1024 * 1024 - 2 ** 21
        ),
        name="block_step",
    )(prefix, x, dy, pack)

    own = lax.dynamic_slice_in_dim(tot, lax.axis_index("ctx") * orow, orow, 1)
    g_out = gf[:orow].T
    g_up = gf[orow:orow + urow].T
    g_down = jnp.swapaxes(gf[orow + urow:].reshape(4, orow, 256), 0, 1).reshape(orow, 4 * 256).T
    return (
        out.T.reshape(block_input.shape),
        gx.T.reshape(block_input.shape),
        own[0],
        gq.T,
        g_out,
        own[1],
        g_up,
        g_down,
    )


N_SEMS = 256


def fits(mesh, block_input, w_down):
    seqs, length, width = block_input.shape
    return (
        mesh.shape["ctx"] == NC
        and mesh.shape["dp"] == ND
        and seqs == 2 * ND
        and length == NC * WORDS
        and width == H * DH
        and 2 * H == NC
        and w_down.shape[0] == 4 * width
    )


def layer_norm(values, gain):
    centred = values - jnp.mean(values, axis=-1, keepdims=True)
    spread = jnp.mean(centred * centred, axis=-1, keepdims=True)
    return centred * lax.rsqrt(spread + EPS) * gain


def row_product(left, right):
    return jnp.dot(left, right, preferred_element_type=jnp.float32)


def cross_rows(left, right):
    return lax.dot_general(
        left, right, (((0,), (0,)), ((), ())), preferred_element_type=jnp.float32
    )


def back_product(left, right):
    return lax.dot_general(
        left, right, (((1,), (1,)), ((), ())), preferred_element_type=jnp.float32
    )


def visible_mask(query_first, query_count, key_first, key_count, prefixes):
    query_pos = query_first + jnp.arange(query_count, dtype=jnp.int32)
    key_pos = key_first + jnp.arange(key_count, dtype=jnp.int32)
    causal = key_pos[None, :] <= query_pos[:, None]
    before = key_pos[None, None, :] < prefixes[:, None, None]
    return (causal[None] | before)[:, None]


def attend_forward(queries, keys_own, values_own, prefixes, my_first, scale):
    batch, rows, heads, head_dim = queries.shape
    key_first = jnp.int32(0)
    key_rows = lax.all_gather(keys_own, "ctx", axis=1, tiled=True)
    value_rows = lax.all_gather(values_own, "ctx", axis=1, tiled=True)
    count = key_rows.shape[1]
    top = jnp.full((batch, heads, rows), NEG, jnp.float32)
    summed = jnp.zeros((batch, rows, heads, head_dim), jnp.float32)
    keys_h = key_rows.reshape(batch, count, heads, head_dim)
    values_h = value_rows.reshape(batch, count, heads, head_dim)
    scores = (
        jnp.einsum("bqhd,bkhd->bhqk", queries, keys_h, preferred_element_type=jnp.float32) * scale
    )
    scores = jnp.where(visible_mask(my_first, rows, key_first, count, prefixes), scores, NEG)
    new_top = jnp.maximum(top, jnp.max(scores, axis=-1))
    factor = jnp.exp(top - new_top)
    probs = jnp.exp(scores - new_top[..., None])
    total = jnp.sum(probs, axis=-1)
    summed = summed * jnp.swapaxes(factor, 1, 2)[..., None] + jnp.einsum(
        "bhqk,bkhd->bqhd", probs.astype(jnp.bfloat16), values_h, preferred_element_type=jnp.float32
    )
    top, total, summed = (new_top, total, summed)
    attended = summed / jnp.swapaxes(total, 1, 2)[..., None]
    log_sum = top + jnp.log(total)
    return (attended.reshape(batch, rows, heads * head_dim), log_sum)


def attend_backward(
    queries, keys_own, values_own, attended, grad_att, log_sum, prefixes, my_first, scale
):
    batch, rows, heads, head_dim = queries.shape
    width = heads * head_dim
    keys_full, values_full = (
        lax.all_gather(keys_own, "ctx", axis=1, tiled=True),
        lax.all_gather(values_own, "ctx", axis=1, tiled=True),
    )
    length = keys_full.shape[1]
    key_block = math.gcd(length, 512)
    grad_h = grad_att.reshape(batch, rows, heads, head_dim)
    delta = jnp.swapaxes(
        jnp.sum(
            grad_h.astype(jnp.float32) * attended.reshape(batch, rows, heads, head_dim), axis=-1
        ),
        1,
        2,
    )

    def one_block(counter, carried):
        key_first = counter * key_block
        q_sum, k_sum, v_sum = carried
        keys_h = lax.dynamic_slice_in_dim(keys_full, key_first, key_block, 1).reshape(
            batch, key_block, heads, head_dim
        )
        values_h = lax.dynamic_slice_in_dim(values_full, key_first, key_block, 1).reshape(
            batch, key_block, heads, head_dim
        )
        scores = (
            jnp.einsum("bqhd,bkhd->bhqk", queries, keys_h, preferred_element_type=jnp.float32)
            * scale
        )
        scores = jnp.where(
            visible_mask(my_first, rows, key_first, key_block, prefixes), scores, NEG
        )
        probs = jnp.exp(scores - log_sum[..., None])
        grad_probs = jnp.einsum(
            "bqhd,bkhd->bhqk", grad_h, values_h, preferred_element_type=jnp.float32
        )
        grad_scores = (probs * (grad_probs - delta[..., None])).astype(jnp.bfloat16)
        q_sum = (
            q_sum
            + jnp.einsum("bhqk,bkhd->bqhd", grad_scores, keys_h, preferred_element_type=jnp.float32)
            * scale
        )
        v_part = jnp.einsum(
            "bhqk,bqhd->bkhd",
            probs.astype(jnp.bfloat16),
            grad_h,
            preferred_element_type=jnp.float32,
        )
        k_part = (
            jnp.einsum("bhqk,bqhd->bkhd", grad_scores, queries, preferred_element_type=jnp.float32)
            * scale
        )
        k_sum = lax.dynamic_update_slice_in_dim(
            k_sum, k_part.reshape(batch, key_block, width), key_first, 1
        )
        v_sum = lax.dynamic_update_slice_in_dim(
            v_sum, v_part.reshape(batch, key_block, width), key_first, 1
        )
        return (q_sum, k_sum, v_sum)

    initial = (
        jnp.zeros((batch, rows, heads, head_dim), jnp.float32),
        jnp.zeros((batch, length, width), jnp.float32),
        jnp.zeros((batch, length, width), jnp.float32),
    )
    q_sum, k_sum, v_sum = lax.fori_loop(0, length // key_block, one_block, initial)
    k_own, v_own = (
        lax.psum_scatter(k_sum.astype(jnp.bfloat16), "ctx", scatter_dimension=1, tiled=True).astype(
            jnp.float32
        ),
        lax.psum_scatter(v_sum.astype(jnp.bfloat16), "ctx", scatter_dimension=1, tiled=True).astype(
            jnp.float32
        ),
    )
    return (q_sum.reshape(batch, rows, width), k_own, v_own)


def local(block_input, prefix, ln1_gain, w_qkv, w_out, ln2_gain, w_up, w_down, grad_y):
    ctx_count = lax.axis_size("ctx")
    blk_rows = block_input.shape[1]
    width = block_input.shape[2]
    head_dim = width // H
    scale = head_dim ** (-0.5)
    my_first = lax.axis_index("ctx") * blk_rows
    per_micro = block_input.shape[0] // MICRO
    by_ctx = (
        lax.all_gather(w_qkv, "ctx", axis=1, tiled=True),
        lax.all_gather(w_out, "ctx", axis=1, tiled=True),
        lax.all_gather(w_up, "ctx", axis=1, tiled=True),
        lax.all_gather(w_down, "ctx", axis=1, tiled=True),
        lax.all_gather(ln1_gain, "ctx", axis=0, tiled=True),
        lax.all_gather(ln2_gain, "ctx", axis=0, tiled=True),
    )
    full_fwd = (
        lax.all_gather(by_ctx[0], "dp", axis=0, tiled=True),
        lax.all_gather(by_ctx[1], "dp", axis=0, tiled=True),
        lax.all_gather(by_ctx[2], "dp", axis=0, tiled=True),
        lax.all_gather(by_ctx[3], "dp", axis=0, tiled=True),
    )
    gain_one = by_ctx[4].astype(jnp.float32)
    gain_two = by_ctx[5].astype(jnp.float32)
    saved = []
    outputs = []
    for micro_idx in range(MICRO):
        lower_row = micro_idx * per_micro
        inputs = block_input[lower_row : lower_row + per_micro].astype(jnp.float32)
        prefixes = prefix[lower_row : lower_row + per_micro]
        flat = inputs.reshape(-1, width)
        normed = layer_norm(flat, gain_one).astype(jnp.bfloat16)
        projected = (
            row_product(normed, full_fwd[0])
            .astype(jnp.bfloat16)
            .reshape(per_micro, blk_rows, 3 * width)
        )
        queries = projected[..., :width].reshape(per_micro, blk_rows, H, head_dim)
        keys_own = projected[..., width : 2 * width]
        values_own = projected[..., 2 * width :]
        attended, log_sum = attend_forward(queries, keys_own, values_own, prefixes, my_first, scale)
        mixed_in = attended.reshape(-1, width).astype(jnp.bfloat16)
        resid = flat + row_product(mixed_in, full_fwd[1])
        normed_two = layer_norm(resid, gain_two).astype(jnp.bfloat16)
        hidden_pre = row_product(normed_two, full_fwd[2])
        activated = jax.nn.gelu(hidden_pre).astype(jnp.bfloat16)
        result = resid + row_product(activated, full_fwd[3])
        outputs.append(result.astype(jnp.bfloat16).reshape(per_micro, blk_rows, width))
        saved.append(
            (
                flat,
                normed,
                queries,
                keys_own,
                values_own,
                attended,
                log_sum,
                mixed_in,
                resid,
                normed_two,
                hidden_pre,
                activated,
                prefixes,
            )
        )
    back_ctx = (
        lax.all_gather(w_qkv, "ctx", axis=1, tiled=True),
        lax.all_gather(w_out, "ctx", axis=1, tiled=True),
        lax.all_gather(w_up, "ctx", axis=1, tiled=True),
        lax.all_gather(w_down, "ctx", axis=1, tiled=True),
    )
    w_back = (
        lax.all_gather(back_ctx[0], "dp", axis=0, tiled=True),
        lax.all_gather(back_ctx[1], "dp", axis=0, tiled=True),
        lax.all_gather(back_ctx[2], "dp", axis=0, tiled=True),
        lax.all_gather(back_ctx[3], "dp", axis=0, tiled=True),
    )
    sum_proj = jnp.zeros(w_back[0].shape, jnp.float32)
    sum_mix = jnp.zeros(w_back[1].shape, jnp.float32)
    sum_expand = jnp.zeros(w_back[2].shape, jnp.float32)
    sum_reduce = jnp.zeros(w_back[3].shape, jnp.float32)
    gain_acc_one = jnp.zeros((width,), jnp.float32)
    gain_acc_two = jnp.zeros((width,), jnp.float32)
    grad_parts = [None] * MICRO
    for micro_idx in reversed(range(MICRO)):
        (
            flat,
            normed,
            queries,
            keys_own,
            values_own,
            attended,
            log_sum,
            mixed_in,
            resid,
            normed_two,
            hidden_pre,
            activated,
            prefixes,
        ) = saved[micro_idx]
        lower_row = micro_idx * per_micro
        cot_b = grad_y[lower_row : lower_row + per_micro].reshape(-1, width)
        cotangent = cot_b.astype(jnp.float32)
        sum_reduce = sum_reduce + cross_rows(activated, cot_b)
        grad_act = back_product(cot_b, w_back[3])
        gelu_pull = jax.vjp(jax.nn.gelu, hidden_pre)[1]
        grad_hidden = gelu_pull(grad_act)[0].astype(jnp.bfloat16)
        sum_expand = sum_expand + cross_rows(normed_two, grad_hidden)
        grad_normed_two = back_product(grad_hidden, w_back[2])
        norm_pull_two = jax.vjp(layer_norm, resid, gain_two)[1]
        grad_resid_part, grad_gain_two = norm_pull_two(grad_normed_two)
        grad_resid = cotangent + grad_resid_part
        grad_mix_b = grad_resid.astype(jnp.bfloat16)
        sum_mix = sum_mix + cross_rows(mixed_in, grad_mix_b)
        grad_attended = back_product(grad_mix_b, w_back[1]).astype(jnp.bfloat16)
        q_grad, k_grad, v_grad = attend_backward(
            queries,
            keys_own,
            values_own,
            attended,
            grad_attended.reshape(per_micro, blk_rows, width),
            log_sum,
            prefixes,
            my_first,
            scale,
        )
        grad_proj = (
            jnp.concatenate([q_grad, k_grad, v_grad], axis=-1)
            .reshape(-1, 3 * width)
            .astype(jnp.bfloat16)
        )
        sum_proj = sum_proj + cross_rows(normed, grad_proj)
        grad_normed = back_product(grad_proj, w_back[0])
        norm_pull_one = jax.vjp(layer_norm, flat, gain_one)[1]
        grad_in_part, grad_gain_one = norm_pull_one(grad_normed)
        grad_parts[micro_idx] = (grad_resid + grad_in_part).reshape(per_micro, blk_rows, width)
        gain_acc_one = gain_acc_one + grad_gain_one
        gain_acc_two = gain_acc_two + grad_gain_two
    red_ctx = (
        lax.psum_scatter(
            sum_proj.astype(jnp.bfloat16), "ctx", scatter_dimension=1, tiled=True
        ).astype(jnp.float32),
        lax.psum_scatter(
            sum_mix.astype(jnp.bfloat16), "ctx", scatter_dimension=1, tiled=True
        ).astype(jnp.float32),
        lax.psum_scatter(
            sum_expand.astype(jnp.bfloat16), "ctx", scatter_dimension=1, tiled=True
        ).astype(jnp.float32),
        lax.psum_scatter(
            sum_reduce.astype(jnp.bfloat16), "ctx", scatter_dimension=1, tiled=True
        ).astype(jnp.float32),
    )
    red_dp = (
        lax.psum_scatter(
            red_ctx[0].astype(jnp.bfloat16), "dp", scatter_dimension=0, tiled=True
        ).astype(jnp.float32),
        lax.psum_scatter(
            red_ctx[1].astype(jnp.bfloat16), "dp", scatter_dimension=0, tiled=True
        ).astype(jnp.float32),
        lax.psum_scatter(
            red_ctx[2].astype(jnp.bfloat16), "dp", scatter_dimension=0, tiled=True
        ).astype(jnp.float32),
        lax.psum_scatter(
            red_ctx[3].astype(jnp.bfloat16), "dp", scatter_dimension=0, tiled=True
        ).astype(jnp.float32),
    )
    gain_total = lax.psum(jnp.stack([gain_acc_one, gain_acc_two]), ("dp", "ctx"))
    shard_width = width // ctx_count
    own_gains = lax.dynamic_slice_in_dim(
        gain_total, lax.axis_index("ctx") * shard_width, shard_width, 1
    )
    output = jnp.concatenate(outputs, axis=0)
    grad_input = jnp.concatenate(grad_parts, axis=0)
    return (
        output,
        grad_input,
        own_gains[0],
        red_dp[0],
        red_dp[1],
        own_gains[1],
        red_dp[2],
        red_dp[3],
    )


def solution(mesh):
    row, split = P("dp", "ctx"), P("dp", "ctx", None)
    in_specs = (split, P("dp"), P("ctx"), row, row, P("ctx"), row, row, split)
    out_specs = (split, split, P("ctx"), row, row, P("ctx"), row, row)

    def run(block_input, prefix, ln1_gain, w_qkv, w_out, ln2_gain, w_up, w_down, grad_y):
        body = functools.partial(fused, NC) if fits(mesh, block_input, w_down) else local
        return jax.shard_map(body, mesh=mesh, in_specs=in_specs, out_specs=out_specs, check_vma=False)(
            block_input, prefix, ln1_gain, w_qkv, w_out, ln2_gain, w_up, w_down, grad_y
        )

    return run
```

```python
import functools
import math

import jax
import jax.numpy as jnp
from jax import lax
from jax.experimental import pallas as pl
from jax.experimental.pallas import tpu as pltpu
from jax.sharding import PartitionSpec as P

H = 8
MICRO = 2


EPS = 1e-05
NEG = -1e30

MESH = pl.DeviceIdType.MESH
F32 = jnp.float32
BF16 = jnp.bfloat16
NN = (((1,), (0,)), ((), ()))
NT = (((1,), (1,)), ((), ()))
TN = (((0,), (0,)), ((), ()))
GELU_A = math.sqrt(2.0 / math.pi)
GELU_B = 0.044715

NZ, NW, ND = 4, 2 * 2, 2
NC = NZ * NW
WORDS = 128
BQ = 2 * WORDS
GROWS = 16
DH = 64


def dot(a, b, dims=NN):
    return lax.dot_general(a, b, dims, preferred_element_type=F32)


def sum_rows(v):
    return jnp.sum(v, axis=0, keepdims=True)


class Wires:
    def __init__(self, send, recv):
        self.send, self.recv, self.used, self.out, self.open = send, recv, 0, 0, []

    def slots(self, count):
        first = self.used
        self.used += count
        return first

    def group(self, ref):
        self.out += 1
        self.open.append((ref, self.out - 1))
        return self.out - 1

    def copy(self, src, dst, slot, device, out=0):
        return pltpu.make_async_remote_copy(
            src_ref=src,
            dst_ref=dst,
            send_sem=self.send.at[out],
            recv_sem=self.recv.at[slot],
            device_id=device,
            device_id_type=MESH,
        )

    def start(self, src, dst, slot, device, out=None):
        out = self.group(src) if out is None else out
        self.copy(src, dst, slot, device, out).start()

    def landed(self, dst, slot, device):
        self.copy(dst, dst, slot, device).wait_recv()

    def drain(self, device):
        for ref, out in self.open:
            self.copy(ref, ref, 0, device, out).wait_send()


class Place:
    def __init__(self):
        self.me = lax.axis_index("ctx")
        self.d = lax.axis_index("dp")
        self.z = self.me // NW
        self.w = lax.rem(self.me, NW)
        x, y = lax.rem(self.w, 2), self.w // 2
        self.w1 = y * 2 + (1 - x)
        self.w2 = (1 - y) * 2 + x
        self.w3 = (1 - y) * 2 + (1 - x)
        self.other = 1 - self.d
        self.partner = {"dp": self.other}
        self.across_x = {"ctx": self.z * NW + self.w1}
        self.across_y = {"ctx": self.z * NW + self.w2}

    def up(self, step):
        return lax.rem(self.z + step, NZ)

    def down(self, step):
        return lax.rem(self.z - step + NZ, NZ)

    def along_z(self, step):
        return {"ctx": self.up(step) * NW + self.w}


class Gather:
    def __init__(self, wires, place, buf):
        self.wires, self.at, self.buf = wires, place, buf
        self.half = buf.shape[3] // 2
        self.sz = wires.slots(NZ - 1)
        self.sx, self.sy = wires.slots(NZ), wires.slots(NZ)
        self.se, self.sf = wires.slots(NZ), wires.slots(NZ)
        self.sp = wires.slots(1)
        row = buf.at[0, 0]
        self.oz = wires.group(buf.at[0, 0, pl.ds(0, NZ - 1)])
        self.ox, self.oy = wires.group(row), wires.group(row)
        self.oe = wires.group(buf.at[0, 0, :, pl.ds(0, self.half)])
        self.of = wires.group(buf.at[0, 0, :, pl.ds(0, self.half)])
        self.op = wires.group(buf.at[0])

    def block(self, step, w):
        return self.buf.at[self.at.d, self.at.down(step), w]

    def top(self, ref):
        return ref.at[pl.ds(0, self.half)]

    def low(self, ref):
        return ref.at[pl.ds(self.half, self.half)]

    def send_z(self, src):
        p = self.at
        for step in range(1, NZ):
            self.wires.start(src, self.block(0, p.w), self.sz + step - 1, p.along_z(step), self.oz)

    def wait_z(self, step):
        self.wires.landed(self.block(step, self.at.w), self.sz + step - 1, self.at.along_z(step))

    def send_plane(self, step):
        p, b = self.at, self.block(step, self.at.w)
        self.wires.start(b, b, self.sx + step, p.across_x, self.ox)
        self.wires.start(b, b, self.sy + step, p.across_y, self.oy)

    def send_core(self, group, step):
        p = self.at
        b = self.block(step, (p.w, p.w1, p.w2, p.w3)[group])
        self.wires.start(b, b, self.sp, p.partner, self.op)

    def relay_plane(self, step):
        p = self.at
        bx, by = self.block(step, p.w1), self.block(step, p.w2)
        self.wires.landed(bx, self.sx + step, p.across_x)
        self.wires.start(self.top(bx), self.top(bx), self.se + step, p.across_y, self.oe)
        self.send_core(1, step)
        self.wires.landed(by, self.sy + step, p.across_y)
        self.wires.start(self.low(by), self.low(by), self.sf + step, p.across_x, self.of)
        self.send_core(2, step)

    def relay_corner(self, step):
        p, b = self.at, self.block(step, self.at.w3)
        self.wires.landed(self.top(b), self.se + step, p.across_y)
        self.wires.landed(self.low(b), self.sf + step, p.across_x)
        self.send_core(3, step)

    def wait_core(self):
        self.wires.landed(self.buf.at[self.at.other], self.sp, self.at.partner)


class Scatter:
    def __init__(self, wires, place, buf, from_core, from_x, from_y, relay, column, from_z):
        self.wires, self.at, self.buf = wires, place, buf
        self.from_core, self.from_x, self.from_y = from_core, from_x, from_y
        self.relay, self.column, self.from_z = relay, column, from_z
        self.rows = buf.shape[3]
        self.half = self.rows // 2
        self.sp = wires.slots(1)
        self.sx, self.sy = wires.slots(3), wires.slots(3)
        self.sz = wires.slots(NZ - 1)

    def part(self, w, low):
        return self.buf.at[self.at.d, :, w, pl.ds(self.half if low else 0, self.half)]

    def send_core(self):
        p = self.at
        self.wires.start(self.buf.at[p.other], self.from_core, self.sp, p.partner)

    def add_core(self):
        p = self.at
        self.wires.landed(self.from_core, self.sp, p.partner)

        def add(k, carry):
            z, w = k // NW, lax.rem(k, NW)
            mine = self.buf[p.d, z, w].astype(F32)
            self.buf[p.d, z, w] = (mine + self.from_core[z, w].astype(F32)).astype(BF16)
            return carry

        lax.fori_loop(0, NC, add, 0)

    def send_plane(self):
        p = self.at
        for k, w in enumerate((p.w3, p.w1)):
            self.wires.start(self.part(w, False), self.from_x.at[k], self.sx + k, p.across_x)
        for k, w in enumerate((p.w3, p.w2)):
            self.wires.start(self.part(w, True), self.from_y.at[k], self.sy + k, p.across_y)

    def relay_corner(self):
        p, h = self.at, self.half
        self.wires.landed(self.from_x.at[0], self.sx, p.across_x)

        def add_top(z, carry):
            mine = self.buf[p.d, z, p.w2, pl.ds(0, h)].astype(F32)
            self.relay[0, z] = (mine + self.from_x[0, z].astype(F32)).astype(BF16)
            return carry

        lax.fori_loop(0, NZ, add_top, 0)
        self.wires.start(self.relay.at[0], self.from_y.at[2], self.sy + 2, p.across_y)
        self.wires.landed(self.from_y.at[0], self.sy, p.across_y)

        def add_low(z, carry):
            mine = self.buf[p.d, z, p.w1, pl.ds(h, h)].astype(F32)
            self.relay[1, z] = (mine + self.from_y[0, z].astype(F32)).astype(BF16)
            return carry

        lax.fori_loop(0, NZ, add_low, 0)
        self.wires.start(self.relay.at[1], self.from_x.at[2], self.sx + 2, p.across_x)

    def send_z(self):
        p, h = self.at, self.half
        self.wires.landed(self.from_x.at[1], self.sx + 1, p.across_x)
        self.wires.landed(self.from_y.at[1], self.sy + 1, p.across_y)
        self.wires.landed(self.from_y.at[2], self.sy + 2, p.across_y)
        self.wires.landed(self.from_x.at[2], self.sx + 2, p.across_x)

        def add(z, carry):
            top = self.buf[p.d, z, p.w, pl.ds(0, h)].astype(F32)
            top = top + self.from_x[1, z].astype(F32) + self.from_y[2, z].astype(F32)
            self.column[z, pl.ds(0, h)] = top.astype(BF16)
            low = self.buf[p.d, z, p.w, pl.ds(h, h)].astype(F32)
            low = low + self.from_y[1, z].astype(F32) + self.from_x[2, z].astype(F32)
            self.column[z, pl.ds(h, h)] = low.astype(BF16)
            return carry

        lax.fori_loop(0, NZ, add, 0)
        for step in range(1, NZ):
            self.wires.start(
                self.column.at[p.up(step)], self.from_z.at[step - 1], self.sz + step - 1, p.along_z(step)
            )

    def total(self):
        p = self.at
        for step in range(1, NZ):
            self.wires.landed(self.from_z.at[step - 1], self.sz + step - 1, p.along_z(step))
        acc = self.column[p.z].astype(F32)
        for step in range(1, NZ):
            acc = acc + self.from_z[step - 1].astype(F32)
        return acc


class Exchange:
    def __init__(self, wires, place, src, dst, inner=None):
        self.wires, self.at, self.src, self.dst = wires, place, src, dst
        self.inner = inner
        self.slot = wires.slots(1)
        self.rest = dst.at[pl.ds(0, NC - 1)] if inner is None else dst.at[pl.ds(0, NC - 1), inner]
        self.out = wires.group(self.rest)

    def view(self, ref, k):
        return ref.at[k] if self.inner is None else ref.at[k, self.inner]

    def send(self, offset):
        to = lax.rem(self.at.me + offset, NC)
        return self.wires.copy(
            self.view(self.src, to), self.view(self.dst, self.at.me), self.slot, {"ctx": to}, self.out
        )

    def send_to(self, chip):
        offset = lax.rem(chip - self.at.me + NC, NC)

        @pl.when(offset > 0)
        def _():
            self.send(offset).start()

        @pl.when(offset == 0)
        def _():
            self.keep()

    def keep(self):
        me = self.at.me
        if self.inner is None:
            self.dst[me] = self.src[me]
        else:
            self.dst[me, self.inner] = self.src[me, self.inner]

    def send_all(self):
        for offset in range(1, NC):
            self.send(offset).start()
        self.keep()

    def wait(self):
        self.wires.landed(self.rest, self.slot, self.at.partner)


def norm_stats(v):
    centred = v - jnp.mean(v, axis=0, keepdims=True)
    rstd = lax.rsqrt(jnp.mean(centred * centred, axis=0, keepdims=True) + EPS)
    return centred * rstd, rstd


def norm_back(grad, hat, rstd, gain):
    g = grad * gain
    return rstd * (g - jnp.mean(g, axis=0, keepdims=True) - hat * jnp.mean(g * hat, axis=0, keepdims=True))


def gelu_both(p):
    t = jnp.tanh(GELU_A * (p + GELU_B * p * p * p))
    half = 0.5 * (1.0 + t)
    slope = half + 0.5 * p * (1.0 - t * t) * (GELU_A * (1.0 + 3.0 * GELU_B * p * p))
    return p * half, slope


def step_kernel(
    prefix_ref, x_hbm, dy_hbm, gains_hbm, wq_hbm, wo_hbm, wu_hbm, wd_hbm,
    out_hbm, gx_hbm, gq_hbm, go_hbm, gu_hbm, gd_hbm, g1_hbm, g2_hbm,
    send_sem, recv_sem, own_sem,
    x_ref, dy_ref, WU, out_ref, gx_ref, gq_ref, gf_ref, GU, G1, G2,
    QG, FG, HAT1, RST1, NRM, DYT,
    QS, QR, KN, VN, SC, PR, OT, LI, AS, AR, ATT,
    RES, HAT2, RST2, NRM2, ACT, SLOPE, DPRE, ACC, DRES, DAI,
    DS, DR, DAP, DEL, DQ, DQS, DPR, DPJ,
    GF, GFC, GFX, GFY, GFR, GFS, GFZ,
    GQ, GQC, GQX, GQY, GQR, GQS, GQZ,
    TS, TR,
):
    place = Place()
    wires = Wires(send_sem, recv_sem)
    me = place.me
    width = HAT1.shape[0]
    heads = width // DH
    half = width // 2
    qrows, frows = QG.shape[3], FG.shape[3]
    nq = PR.shape[0]
    pre_blocks = (nq * BQ // 2) // BQ
    orow = width // NC
    urow = ACT.shape[0] * BQ // NC
    nf = ACT.shape[0]

    gq = Gather(wires, place, QG)
    gf = Gather(wires, place, FG)
    qkv_x = Exchange(wires, place, QS, QR)
    att_x = Exchange(wires, place, AS, AR)
    datt_x = Exchange(wires, place, DS, DR)
    dkv_x = Exchange(wires, place, DQS, DPR, pl.ds(1, 2))
    dq_x = Exchange(wires, place, DQS, DPR, pl.ds(0, 1))
    sf = Scatter(wires, place, GF, GFC, GFX, GFY, GFR, GFS, GFZ)
    sq = Scatter(wires, place, GQ, GQC, GQX, GQY, GQR, GQS, GQZ)
    tot = wires.slots(6)

    barrier = pltpu.get_barrier_semaphore()
    for offset in range(1, NC):
        pl.semaphore_signal(barrier, inc=1, device_id={"ctx": lax.rem(me + offset, NC)}, device_id_type=MESH)
    pl.semaphore_signal(barrier, inc=1, device_id=place.partner, device_id_type=MESH)

    mine_q, mine_f = gq.block(0, place.w), gf.block(0, place.w)
    local = [0]

    def local_copy(src, dst):
        c = pltpu.make_async_copy(src, dst, own_sem.at[local[0]])
        local[0] += 1
        c.start()
        return c

    first = [
        local_copy(gains_hbm, mine_q.at[pl.ds(0, GROWS)]),
        local_copy(wq_hbm, mine_q.at[pl.ds(GROWS, qrows - GROWS)]),
    ]
    words_in = local_copy(x_hbm, x_ref)
    up_in = local_copy(wu_hbm, WU)
    rest = [local_copy(wo_hbm, mine_f.at[pl.ds(0, orow)])]
    for c in range(4):
        rest.append(
            local_copy(wd_hbm.at[:, pl.ds(c * 256, 256)], mine_f.at[pl.ds(orow + urow + c * orow, orow)])
        )
    dy_in = local_copy(dy_hbm, dy_ref)
    for c in first:
        c.wait()
    pl.semaphore_wait(barrier, NC)

    gq.send_z(gq.block(0, place.w))
    gq.send_plane(0)
    gq.send_core(0, 0)

    up_in.wait()
    FG[place.d, place.z, place.w, pl.ds(orow, urow), :] = WU[...].astype(F32).T.astype(BF16)
    words_in.wait()
    hat, rstd = norm_stats(x_ref[...].astype(F32).T)
    HAT1[...] = hat
    RST1[...] = rstd
    for c in rest:
        c.wait()

    for step in range(1, NZ):
        gq.wait_z(step)
        gq.send_plane(step)
        gq.send_core(0, step)
    gf.send_z(gf.block(0, place.w))
    dy_in.wait()
    DYT[...] = dy_ref[...].astype(F32).T.astype(BF16)
    for step in range(NZ):
        gq.relay_plane(step)
    for step in range(NZ):
        gq.relay_corner(step)
    gq.wait_core()

    gains = QG[0, :, :, pl.ds(0, GROWS), :].reshape(NC * GROWS, 256).astype(F32).T
    gain_one, gain_two = (
        jnp.concatenate([gains[r:r + orow, k * GROWS:k * GROWS + 1] for k in range(NC)], axis=0) for r in (0, 128)
    )
    NRM[...] = (HAT1[...] * gain_one).astype(BF16)
    wrows = qrows - GROWS
    for j in range(NZ):
        proj = sum(
            dot(QG[k, j, :, pl.ds(GROWS, wrows), :].reshape(NW * wrows, 256), NRM[k * half:(k + 1) * half])
            for k in range(ND)
        )
        for t in range(NW * wrows // DH):
            kind, head = divmod(j * (NW * wrows // DH) + t, heads)
            unit = proj[t * DH:(t + 1) * DH].astype(BF16)
            if kind == 0:
                unit = (unit.astype(F32) * DH ** (-0.5)).astype(BF16)
            for b in range(2):
                QS[b * heads + head, kind] = unit[:, b * WORDS:(b + 1) * WORDS]
    qkv_x.send_all()

    gf.send_plane(0)
    gf.send_core(0, 0)
    for step in range(1, NZ):
        gf.wait_z(step)
        gf.send_plane(step)
        gf.send_core(0, step)

    qkv_x.wait()
    prefix = prefix_ref[me // heads]

    def to_rows(c, carry):
        rows = pl.ds(pl.multiple_of(c * WORDS, WORDS), WORDS)
        KN[rows, :] = QR[c, 1].astype(F32).T.astype(BF16)
        VN[rows, :] = QR[c, 2].astype(F32).T.astype(BF16)
        return carry

    lax.fori_loop(0, NC, to_rows, 0)

    def pair(ref, b, kind=None):
        if kind is None:
            return jnp.concatenate([ref[2 * b], ref[2 * b + 1]], axis=1)
        return jnp.concatenate([ref[2 * b, kind], ref[2 * b + 1, kind]], axis=1)

    def rows_of(b):
        return pl.ds(pl.multiple_of(b * BQ, BQ), BQ)

    def attend(qb, carry):
        queries = pair(QR, qb, 0)

        def scores(masked, kb, top):
            s = dot(KN[rows_of(kb), :], queries)
            if masked:
                key = kb * BQ + lax.broadcasted_iota(jnp.int32, (BQ, BQ), 0)
                word = qb * BQ + lax.broadcasted_iota(jnp.int32, (BQ, BQ), 1)
                s = jnp.where((key <= word) | (key < prefix), s, NEG)
            SC[rows_of(kb), :] = s
            return jnp.maximum(top, jnp.max(s.reshape(BQ // 8, 8, BQ), axis=0))

        last = jnp.maximum(qb + 1, pre_blocks)
        top = jnp.full((8, BQ), NEG, F32)
        top = lax.fori_loop(0, qb, functools.partial(scores, False), top)
        top = lax.fori_loop(qb, last, functools.partial(scores, True), top)
        top = jnp.max(top, axis=0, keepdims=True)

        def weigh(kb, state):
            total, acc = state
            p = jnp.exp(SC[rows_of(kb), :] - top)
            total = total + jnp.sum(p.reshape(BQ // 8, 8, BQ), axis=0)
            p = p.astype(BF16)
            PR[qb, rows_of(kb), :] = p
            return total, acc + dot(pair(QR, kb, 2), p)

        total, acc = lax.fori_loop(0, last, weigh, (jnp.zeros((8, BQ), F32), jnp.zeros((DH, BQ), F32)))
        inv = 1.0 / jnp.sum(total, axis=0, keepdims=True)
        out = acc * inv
        OT[qb] = out
        LI[qb] = inv
        out = out.astype(BF16)
        for k in range(2):
            AS[2 * qb + k] = out[:, k * WORDS:(k + 1) * WORDS]
            att_x.send_to(2 * qb + k)
        return carry

    lax.fori_loop(0, nq // 2, attend, 0)
    for step in range(NZ):
        gf.relay_plane(step)
    lax.fori_loop(nq // 2, nq, attend, 0)
    for step in range(NZ):
        gf.relay_corner(step)

    att_x.wait()
    gf.wait_core()
    for h in range(heads):
        ATT[h * DH:(h + 1) * DH] = jnp.concatenate([AR[h], AR[heads + h]], axis=1)

    def w_out(k):
        return FG[k, :, :, pl.ds(0, orow), :].reshape(width, 256)

    def w_up(k, c):
        return FG[k, c // 2, pl.ds(2 * (c % 2), 2), pl.ds(orow, urow), :].reshape(BQ, 256)

    def w_down(c):
        rows = orow + urow + (c % 4) * orow
        return FG[c // 4, :, :, pl.ds(rows, orow), :].reshape(width, 256)

    mixed = sum(dot(w_out(k), ATT[k * half:(k + 1) * half]) for k in range(ND))
    res = x_ref[...].astype(F32).T + mixed
    RES[...] = res
    hat2, rstd2 = norm_stats(res)
    HAT2[...] = hat2
    RST2[...] = rstd2
    NRM2[...] = (hat2 * gain_two).astype(BF16)

    for c in range(nf):
        pre = sum(dot(w_up(k, c), NRM2[k * half:(k + 1) * half]) for k in range(ND))
        act, slope = gelu_both(pre)
        ACT[c] = act.astype(BF16)
        SLOPE[c] = slope
    ACC[...] = jnp.zeros_like(ACC)
    for c in range(nf):
        dact = dot(w_down(c), DYT[...], TN)
        dpre = (dact * SLOPE[c]).astype(BF16)
        DPRE[c] = dpre
        for k in range(ND):
            ACC[k * half:(k + 1) * half] += dot(w_up(k, c), dpre, TN)
    dn2 = ACC[...]
    dres = DYT[...].astype(F32) + norm_back(dn2, HAT2[...], RST2[...], gain_two)
    DRES[...] = dres
    DAI[...] = dres.astype(BF16)
    ones = jnp.ones((8, 2 * WORDS), F32)
    row_two = lax.dot_general(
        ones, dn2 * HAT2[...], NT, precision=lax.Precision.HIGHEST, preferred_element_type=F32
    )
    for k in range(ND):
        datt = dot(w_out(k), DAI[...], TN).astype(BF16)
        for t in range(half // DH):
            h = k * (half // DH) + t
            for b in range(2):
                DS[b * heads + h] = datt[t * DH:(t + 1) * DH, b * WORDS:(b + 1) * WORDS]
    datt_x.send_all()

    for r in range(2):
        acc = RES[r * half:(r + 1) * half]
        for c in range(nf):
            rows = orow + urow + (c % 4) * orow
            w = FG[c // 4, pl.ds(2 * r, 2), :, pl.ds(rows, orow), :].reshape(half, 256)
            acc = acc + dot(w, ACT[c])
        out_ref[:, r * half:(r + 1) * half] = acc.T.astype(BF16)
    outs = [local_copy(out_ref, out_hbm)]
    for c in range(nf):
        rows = orow + urow + (c % 4) * orow
        GF[c // 4, :, :, pl.ds(rows, orow), :] = dot(DYT[...], ACT[c], NT).astype(BF16).reshape(NZ, NW, orow, 256)
        for k in range(ND):
            up = dot(DPRE[c], NRM2[k * half:(k + 1) * half], NT).astype(BF16)
            GF[k, c // 2, pl.ds(2 * (c % 2), 2), pl.ds(orow, urow), :] = up.reshape(2, urow, 256)
    for k in range(ND):
        mix = dot(DAI[...], ATT[k * half:(k + 1) * half], NT).astype(BF16)
        GF[k, :, :, pl.ds(0, orow), :] = mix.reshape(NZ, NW, orow, 256)
    sf.send_core()

    datt_x.wait()

    def ready(qb, carry):
        datt = pair(DR, qb).astype(F32)
        inv = LI[qb]
        DEL[qb] = sum_rows(datt * OT[qb]) * inv
        DAP[qb] = (datt * inv).astype(BF16)
        DQ[qb] = jnp.zeros((DH, BQ), F32)
        return carry

    lax.fori_loop(0, nq, ready, 0)

    def put(ref, b, kind, val):
        val = val.astype(BF16)
        for k in range(2):
            ref[2 * b + k, kind] = val[:, k * WORDS:(k + 1) * WORDS]

    def send_dq(qb):
        put(DQS, qb, 0, DQ[qb] * DH ** (-0.5))
        for k in range(2):
            dq_x.send_to(2 * qb + k)

    def attend_back(kb, carry, finish=False):
        keys, vals, keys_t = KN[rows_of(kb), :], VN[rows_of(kb), :], pair(QR, kb, 1)
        first = jnp.where(kb < pre_blocks, 0, kb)

        def one(qb, state):
            dk, dv = state
            dp = dot(vals, DAP[qb])
            p = PR[qb, rows_of(kb), :]
            ds = (p.astype(F32) * (dp - DEL[qb])).astype(BF16)
            DQ[qb] += dot(keys_t, ds)
            if finish:
                send_dq(qb)
            return dk + dot(pair(QR, qb, 0), ds, NT), dv + dot(DAP[qb], p, NT)

        zero = jnp.zeros((DH, BQ), F32)
        dk, dv = lax.fori_loop(first, nq, one, (zero, zero))
        put(DQS, kb, 1, dk)
        put(DQS, kb, 2, dv)
        for k in range(2):
            dkv_x.send_to(2 * kb + k)
        return carry

    def back_from_last(i, carry):
        return attend_back(nq - 1 - i, carry)

    lax.fori_loop(0, 1, back_from_last, 0)
    sf.add_core()
    sf.send_plane()
    lax.fori_loop(1, nq - 1, back_from_last, 0)
    attend_back(0, 0, True)
    sf.relay_corner()
    dq_x.wait()
    dkv_x.wait()

    for kind in range(3):
        for h in range(heads):
            r = (kind * heads + h) * DH
            DPJ[r:r + DH] = jnp.concatenate([DPR[h, kind], DPR[heads + h, kind]], axis=1)
    blk = NW * wrows
    for j in range(NZ):
        for k in range(ND):
            g = dot(DPJ[j * blk:(j + 1) * blk], NRM[k * half:(k + 1) * half], NT)
            GQ[k, j] = g.astype(BF16).reshape(NW, wrows, 256)
    sq.send_core()
    sf.send_z()
    ACC[...] = jnp.zeros_like(ACC)
    for k in range(ND):
        for j in range(NZ):
            w = QG[k, j, :, pl.ds(GROWS, wrows), :].reshape(blk, 256)
            ACC[k * half:(k + 1) * half] += dot(w, DPJ[j * blk:(j + 1) * blk], TN)
    dn1 = ACC[...]
    gx_ref[...] = (DRES[...] + norm_back(dn1, HAT1[...], RST1[...], gain_one)).T
    outs.append(local_copy(gx_ref, gx_hbm))
    row_one = lax.dot_general(
        ones, dn1 * HAT1[...], NT, precision=lax.Precision.HIGHEST, preferred_element_type=F32
    )

    TS[0] = jnp.where(lax.broadcasted_iota(jnp.int32, (8, width), 0) == 0, row_one, row_two)
    wires.start(TS.at[0], TR.at[0], tot, place.partner)
    sq.add_core()
    sq.send_plane()
    wires.landed(TR.at[0], tot, place.partner)
    TS[1] = TS[0] + TR[0]
    wires.start(TS.at[1], TR.at[1], tot + 1, place.across_x)
    sq.relay_corner()
    wires.landed(TR.at[1], tot + 1, place.across_x)
    TS[2] = TS[1] + TR[1]
    wires.start(TS.at[2], TR.at[2], tot + 2, place.across_y)
    gf_ref[...] = sf.total()
    GU[...] = gf_ref[pl.ds(orow, urow), :].T
    outs.append(local_copy(gf_ref.at[pl.ds(0, orow)], go_hbm))
    outs.append(local_copy(GU, gu_hbm))
    for c in range(4):
        outs.append(local_copy(gf_ref.at[pl.ds(orow + urow + c * orow, orow)], gd_hbm.at[:, pl.ds(c * 256, 256)]))
    sq.send_z()
    wires.landed(TR.at[2], tot + 2, place.across_y)
    TS[3] = TS[2] + TR[2]
    for step in range(1, NZ):
        wires.start(TS.at[3], TR.at[2 + step], tot + 2 + step, place.along_z(step))
    gq_ref[...] = sq.total()
    outs.append(local_copy(gq_ref, gq_hbm))
    for step in range(1, NZ):
        wires.landed(TR.at[2 + step], tot + 2 + step, place.along_z(step))
    picked = lax.broadcasted_iota(jnp.int32, (width, 128), 0) == me * orow + lax.broadcasted_iota(
        jnp.int32, (width, 128), 1
    )
    own = lax.dot_general(
        TS[3] + TR[3] + TR[4] + TR[5], picked.astype(F32), NN,
        precision=lax.Precision.HIGHEST, preferred_element_type=F32,
    )
    G1[...] = own[0:1, 0:orow]
    G2[...] = own[1:2, 0:orow]
    outs.append(local_copy(G1, g1_hbm))
    outs.append(local_copy(G2, g2_hbm))

    assert (wires.out, wires.used, local[0]) == (N_SEND, N_RECV, N_OWN), (wires.out, wires.used, local[0])
    wires.drain(place.partner)
    for c in outs:
        c.wait()


def fused(ctx_count, block_input, prefix, ln1_gain, w_qkv, w_out, ln2_gain, w_up, w_down, grad_y):
    width = block_input.shape[2]
    ff = w_down.shape[0] * ND
    words = 2 * WORDS
    nq = NC * WORDS // BQ
    nf = ff // BQ
    orow, qrow, urow = width // NC, 3 * width // NC, ff // NC
    qrows, frows = GROWS + qrow, orow + urow + 4 * orow

    gains = jnp.concatenate([jnp.pad(g, (0, 128 - orow)) for g in (ln1_gain, ln2_gain)])
    gains = jnp.broadcast_to(gains[None], (GROWS, 256))
    x = block_input.reshape(words, width)
    dy = grad_y.reshape(words, width)

    def vm(*shape, dtype=BF16):
        return pltpu.VMEM(shape, dtype)

    def scatter_bufs(rows):
        return [
            vm(ND, NZ, NW, rows, 256),
            vm(NZ, NW, rows, 256),
            vm(3, NZ, rows // 2, 256),
            vm(3, NZ, rows // 2, 256),
            vm(2, NZ, rows // 2, 256),
            vm(NZ, rows, 256),
            vm(NZ - 1, rows, 256),
        ]

    length = NC * WORDS
    msgs = 512
    vmem = pl.BlockSpec(memory_space=pltpu.VMEM)
    hbm = pl.BlockSpec(memory_space=pl.ANY)
    out, gx, gq, g_out, g_up, g_down, g_one, g_two = pl.pallas_call(
        step_kernel,
        out_shape=(
            jax.ShapeDtypeStruct((words, width), BF16),
            jax.ShapeDtypeStruct((words, width), F32),
            jax.ShapeDtypeStruct((qrow, 256), F32),
            jax.ShapeDtypeStruct((orow, 256), F32),
            jax.ShapeDtypeStruct((256, urow), F32),
            jax.ShapeDtypeStruct((orow, 4 * 256), F32),
            jax.ShapeDtypeStruct((1, orow), F32),
            jax.ShapeDtypeStruct((1, orow), F32),
        ),
        in_specs=[pl.BlockSpec(memory_space=pltpu.SMEM)] + [hbm] * 7,
        out_specs=(hbm,) * 8,
        scratch_shapes=[
            pltpu.SemaphoreType.DMA((N_SEND,)),
            pltpu.SemaphoreType.DMA((N_RECV,)),
            pltpu.SemaphoreType.DMA((N_OWN,)),
            vm(words, width),
            vm(words, width),
            vm(256, urow),
            vm(words, width),
            vm(words, width, dtype=F32),
            vm(qrow, 256, dtype=F32),
            vm(frows, 256, dtype=F32),
            vm(256, urow, dtype=F32),
            vm(1, orow, dtype=F32),
            vm(1, orow, dtype=F32),
            vm(ND, NZ, NW, qrows, 256),
            vm(ND, NZ, NW, frows, 256),
            vm(width, words, dtype=F32),
            vm(1, words, dtype=F32),
            vm(width, words),
            vm(width, words),
            vm(NC, 3, DH, WORDS),
            vm(NC, 3, DH, WORDS),
            vm(length, DH),
            vm(length, DH),
            vm(length, BQ, dtype=F32),
            vm(nq, length, BQ),
            vm(nq, DH, BQ, dtype=F32),
            vm(nq, 1, BQ, dtype=F32),
            vm(NC, DH, WORDS),
            vm(NC, DH, WORDS),
            vm(width, words),
            vm(width, words, dtype=F32),
            vm(width, words, dtype=F32),
            vm(1, words, dtype=F32),
            vm(width, words),
            vm(nf, BQ, words),
            vm(nf, BQ, words, dtype=F32),
            vm(nf, BQ, words),
            vm(width, words, dtype=F32),
            vm(width, words, dtype=F32),
            vm(width, words),
            vm(NC, DH, WORDS),
            vm(NC, DH, WORDS),
            vm(nq, DH, BQ),
            vm(nq, 1, BQ, dtype=F32),
            vm(nq, DH, BQ, dtype=F32),
            vm(NC, 3, DH, WORDS),
            vm(NC, 3, DH, WORDS),
            vm(3 * width, words),
            *scatter_bufs(frows),
            *scatter_bufs(qrow),
            vm(4, 8, width, dtype=F32),
            vm(6, 8, width, dtype=F32),
        ],
        compiler_params=pltpu.CompilerParams(
            collective_id=0, has_side_effects=True, vmem_limit_bytes=66 * 1024 * 1024 - 2 ** 21
        ),
        name="block_step",
    )(prefix, x, dy, gains, w_qkv.T, w_out.T, w_up, w_down.T)

    return (
        out.reshape(block_input.shape),
        gx.reshape(block_input.shape),
        g_one.reshape(ln1_gain.shape),
        gq.T,
        g_out.T,
        g_two.reshape(ln2_gain.shape),
        g_up,
        g_down.T,
    )


N_SEND, N_RECV, N_OWN = 43, 71, 21


def fits(mesh, block_input, w_down):
    seqs, length, width = block_input.shape
    return (
        mesh.shape["ctx"] == NC
        and mesh.shape["dp"] == ND
        and seqs == 2 * ND
        and length == NC * WORDS
        and width == H * DH
        and 2 * H == NC
        and w_down.shape[0] == 4 * width
    )


def layer_norm(values, gain):
    centred = values - jnp.mean(values, axis=-1, keepdims=True)
    spread = jnp.mean(centred * centred, axis=-1, keepdims=True)
    return centred * lax.rsqrt(spread + EPS) * gain


def row_product(left, right):
    return jnp.dot(left, right, preferred_element_type=jnp.float32)


def cross_rows(left, right):
    return lax.dot_general(
        left, right, (((0,), (0,)), ((), ())), preferred_element_type=jnp.float32
    )


def back_product(left, right):
    return lax.dot_general(
        left, right, (((1,), (1,)), ((), ())), preferred_element_type=jnp.float32
    )


def visible_mask(query_first, query_count, key_first, key_count, prefixes):
    query_pos = query_first + jnp.arange(query_count, dtype=jnp.int32)
    key_pos = key_first + jnp.arange(key_count, dtype=jnp.int32)
    causal = key_pos[None, :] <= query_pos[:, None]
    before = key_pos[None, None, :] < prefixes[:, None, None]
    return (causal[None] | before)[:, None]


def attend_forward(queries, keys_own, values_own, prefixes, my_first, scale):
    batch, rows, heads, head_dim = queries.shape
    key_first = jnp.int32(0)
    key_rows = lax.all_gather(keys_own, "ctx", axis=1, tiled=True)
    value_rows = lax.all_gather(values_own, "ctx", axis=1, tiled=True)
    count = key_rows.shape[1]
    top = jnp.full((batch, heads, rows), NEG, jnp.float32)
    summed = jnp.zeros((batch, rows, heads, head_dim), jnp.float32)
    keys_h = key_rows.reshape(batch, count, heads, head_dim)
    values_h = value_rows.reshape(batch, count, heads, head_dim)
    scores = (
        jnp.einsum("bqhd,bkhd->bhqk", queries, keys_h, preferred_element_type=jnp.float32) * scale
    )
    scores = jnp.where(visible_mask(my_first, rows, key_first, count, prefixes), scores, NEG)
    new_top = jnp.maximum(top, jnp.max(scores, axis=-1))
    factor = jnp.exp(top - new_top)
    probs = jnp.exp(scores - new_top[..., None])
    total = jnp.sum(probs, axis=-1)
    summed = summed * jnp.swapaxes(factor, 1, 2)[..., None] + jnp.einsum(
        "bhqk,bkhd->bqhd", probs.astype(jnp.bfloat16), values_h, preferred_element_type=jnp.float32
    )
    top, total, summed = (new_top, total, summed)
    attended = summed / jnp.swapaxes(total, 1, 2)[..., None]
    log_sum = top + jnp.log(total)
    return (attended.reshape(batch, rows, heads * head_dim), log_sum)


def attend_backward(
    queries, keys_own, values_own, attended, grad_att, log_sum, prefixes, my_first, scale
):
    batch, rows, heads, head_dim = queries.shape
    width = heads * head_dim
    keys_full, values_full = (
        lax.all_gather(keys_own, "ctx", axis=1, tiled=True),
        lax.all_gather(values_own, "ctx", axis=1, tiled=True),
    )
    length = keys_full.shape[1]
    key_block = math.gcd(length, 512)
    grad_h = grad_att.reshape(batch, rows, heads, head_dim)
    delta = jnp.swapaxes(
        jnp.sum(
            grad_h.astype(jnp.float32) * attended.reshape(batch, rows, heads, head_dim), axis=-1
        ),
        1,
        2,
    )

    def one_block(counter, carried):
        key_first = counter * key_block
        q_sum, k_sum, v_sum = carried
        keys_h = lax.dynamic_slice_in_dim(keys_full, key_first, key_block, 1).reshape(
            batch, key_block, heads, head_dim
        )
        values_h = lax.dynamic_slice_in_dim(values_full, key_first, key_block, 1).reshape(
            batch, key_block, heads, head_dim
        )
        scores = (
            jnp.einsum("bqhd,bkhd->bhqk", queries, keys_h, preferred_element_type=jnp.float32)
            * scale
        )
        scores = jnp.where(
            visible_mask(my_first, rows, key_first, key_block, prefixes), scores, NEG
        )
        probs = jnp.exp(scores - log_sum[..., None])
        grad_probs = jnp.einsum(
            "bqhd,bkhd->bhqk", grad_h, values_h, preferred_element_type=jnp.float32
        )
        grad_scores = (probs * (grad_probs - delta[..., None])).astype(jnp.bfloat16)
        q_sum = (
            q_sum
            + jnp.einsum("bhqk,bkhd->bqhd", grad_scores, keys_h, preferred_element_type=jnp.float32)
            * scale
        )
        v_part = jnp.einsum(
            "bhqk,bqhd->bkhd",
            probs.astype(jnp.bfloat16),
            grad_h,
            preferred_element_type=jnp.float32,
        )
        k_part = (
            jnp.einsum("bhqk,bqhd->bkhd", grad_scores, queries, preferred_element_type=jnp.float32)
            * scale
        )
        k_sum = lax.dynamic_update_slice_in_dim(
            k_sum, k_part.reshape(batch, key_block, width), key_first, 1
        )
        v_sum = lax.dynamic_update_slice_in_dim(
            v_sum, v_part.reshape(batch, key_block, width), key_first, 1
        )
        return (q_sum, k_sum, v_sum)

    initial = (
        jnp.zeros((batch, rows, heads, head_dim), jnp.float32),
        jnp.zeros((batch, length, width), jnp.float32),
        jnp.zeros((batch, length, width), jnp.float32),
    )
    q_sum, k_sum, v_sum = lax.fori_loop(0, length // key_block, one_block, initial)
    k_own, v_own = (
        lax.psum_scatter(k_sum.astype(jnp.bfloat16), "ctx", scatter_dimension=1, tiled=True).astype(
            jnp.float32
        ),
        lax.psum_scatter(v_sum.astype(jnp.bfloat16), "ctx", scatter_dimension=1, tiled=True).astype(
            jnp.float32
        ),
    )
    return (q_sum.reshape(batch, rows, width), k_own, v_own)


def local(block_input, prefix, ln1_gain, w_qkv, w_out, ln2_gain, w_up, w_down, grad_y):
    ctx_count = lax.axis_size("ctx")
    blk_rows = block_input.shape[1]
    width = block_input.shape[2]
    head_dim = width // H
    scale = head_dim ** (-0.5)
    my_first = lax.axis_index("ctx") * blk_rows
    per_micro = block_input.shape[0] // MICRO
    by_ctx = (
        lax.all_gather(w_qkv, "ctx", axis=1, tiled=True),
        lax.all_gather(w_out, "ctx", axis=1, tiled=True),
        lax.all_gather(w_up, "ctx", axis=1, tiled=True),
        lax.all_gather(w_down, "ctx", axis=1, tiled=True),
        lax.all_gather(ln1_gain, "ctx", axis=0, tiled=True),
        lax.all_gather(ln2_gain, "ctx", axis=0, tiled=True),
    )
    full_fwd = (
        lax.all_gather(by_ctx[0], "dp", axis=0, tiled=True),
        lax.all_gather(by_ctx[1], "dp", axis=0, tiled=True),
        lax.all_gather(by_ctx[2], "dp", axis=0, tiled=True),
        lax.all_gather(by_ctx[3], "dp", axis=0, tiled=True),
    )
    gain_one = by_ctx[4].astype(jnp.float32)
    gain_two = by_ctx[5].astype(jnp.float32)
    saved = []
    outputs = []
    for micro_idx in range(MICRO):
        lower_row = micro_idx * per_micro
        inputs = block_input[lower_row : lower_row + per_micro].astype(jnp.float32)
        prefixes = prefix[lower_row : lower_row + per_micro]
        flat = inputs.reshape(-1, width)
        normed = layer_norm(flat, gain_one).astype(jnp.bfloat16)
        projected = (
            row_product(normed, full_fwd[0])
            .astype(jnp.bfloat16)
            .reshape(per_micro, blk_rows, 3 * width)
        )
        queries = projected[..., :width].reshape(per_micro, blk_rows, H, head_dim)
        keys_own = projected[..., width : 2 * width]
        values_own = projected[..., 2 * width :]
        attended, log_sum = attend_forward(queries, keys_own, values_own, prefixes, my_first, scale)
        mixed_in = attended.reshape(-1, width).astype(jnp.bfloat16)
        resid = flat + row_product(mixed_in, full_fwd[1])
        normed_two = layer_norm(resid, gain_two).astype(jnp.bfloat16)
        hidden_pre = row_product(normed_two, full_fwd[2])
        activated = jax.nn.gelu(hidden_pre).astype(jnp.bfloat16)
        result = resid + row_product(activated, full_fwd[3])
        outputs.append(result.astype(jnp.bfloat16).reshape(per_micro, blk_rows, width))
        saved.append(
            (
                flat,
                normed,
                queries,
                keys_own,
                values_own,
                attended,
                log_sum,
                mixed_in,
                resid,
                normed_two,
                hidden_pre,
                activated,
                prefixes,
            )
        )
    back_ctx = (
        lax.all_gather(w_qkv, "ctx", axis=1, tiled=True),
        lax.all_gather(w_out, "ctx", axis=1, tiled=True),
        lax.all_gather(w_up, "ctx", axis=1, tiled=True),
        lax.all_gather(w_down, "ctx", axis=1, tiled=True),
    )
    w_back = (
        lax.all_gather(back_ctx[0], "dp", axis=0, tiled=True),
        lax.all_gather(back_ctx[1], "dp", axis=0, tiled=True),
        lax.all_gather(back_ctx[2], "dp", axis=0, tiled=True),
        lax.all_gather(back_ctx[3], "dp", axis=0, tiled=True),
    )
    sum_proj = jnp.zeros(w_back[0].shape, jnp.float32)
    sum_mix = jnp.zeros(w_back[1].shape, jnp.float32)
    sum_expand = jnp.zeros(w_back[2].shape, jnp.float32)
    sum_reduce = jnp.zeros(w_back[3].shape, jnp.float32)
    gain_acc_one = jnp.zeros((width,), jnp.float32)
    gain_acc_two = jnp.zeros((width,), jnp.float32)
    grad_parts = [None] * MICRO
    for micro_idx in reversed(range(MICRO)):
        (
            flat,
            normed,
            queries,
            keys_own,
            values_own,
            attended,
            log_sum,
            mixed_in,
            resid,
            normed_two,
            hidden_pre,
            activated,
            prefixes,
        ) = saved[micro_idx]
        lower_row = micro_idx * per_micro
        cot_b = grad_y[lower_row : lower_row + per_micro].reshape(-1, width)
        cotangent = cot_b.astype(jnp.float32)
        sum_reduce = sum_reduce + cross_rows(activated, cot_b)
        grad_act = back_product(cot_b, w_back[3])
        gelu_pull = jax.vjp(jax.nn.gelu, hidden_pre)[1]
        grad_hidden = gelu_pull(grad_act)[0].astype(jnp.bfloat16)
        sum_expand = sum_expand + cross_rows(normed_two, grad_hidden)
        grad_normed_two = back_product(grad_hidden, w_back[2])
        norm_pull_two = jax.vjp(layer_norm, resid, gain_two)[1]
        grad_resid_part, grad_gain_two = norm_pull_two(grad_normed_two)
        grad_resid = cotangent + grad_resid_part
        grad_mix_b = grad_resid.astype(jnp.bfloat16)
        sum_mix = sum_mix + cross_rows(mixed_in, grad_mix_b)
        grad_attended = back_product(grad_mix_b, w_back[1]).astype(jnp.bfloat16)
        q_grad, k_grad, v_grad = attend_backward(
            queries,
            keys_own,
            values_own,
            attended,
            grad_attended.reshape(per_micro, blk_rows, width),
            log_sum,
            prefixes,
            my_first,
            scale,
        )
        grad_proj = (
            jnp.concatenate([q_grad, k_grad, v_grad], axis=-1)
            .reshape(-1, 3 * width)
            .astype(jnp.bfloat16)
        )
        sum_proj = sum_proj + cross_rows(normed, grad_proj)
        grad_normed = back_product(grad_proj, w_back[0])
        norm_pull_one = jax.vjp(layer_norm, flat, gain_one)[1]
        grad_in_part, grad_gain_one = norm_pull_one(grad_normed)
        grad_parts[micro_idx] = (grad_resid + grad_in_part).reshape(per_micro, blk_rows, width)
        gain_acc_one = gain_acc_one + grad_gain_one
        gain_acc_two = gain_acc_two + grad_gain_two
    red_ctx = (
        lax.psum_scatter(
            sum_proj.astype(jnp.bfloat16), "ctx", scatter_dimension=1, tiled=True
        ).astype(jnp.float32),
        lax.psum_scatter(
            sum_mix.astype(jnp.bfloat16), "ctx", scatter_dimension=1, tiled=True
        ).astype(jnp.float32),
        lax.psum_scatter(
            sum_expand.astype(jnp.bfloat16), "ctx", scatter_dimension=1, tiled=True
        ).astype(jnp.float32),
        lax.psum_scatter(
            sum_reduce.astype(jnp.bfloat16), "ctx", scatter_dimension=1, tiled=True
        ).astype(jnp.float32),
    )
    red_dp = (
        lax.psum_scatter(
            red_ctx[0].astype(jnp.bfloat16), "dp", scatter_dimension=0, tiled=True
        ).astype(jnp.float32),
        lax.psum_scatter(
            red_ctx[1].astype(jnp.bfloat16), "dp", scatter_dimension=0, tiled=True
        ).astype(jnp.float32),
        lax.psum_scatter(
            red_ctx[2].astype(jnp.bfloat16), "dp", scatter_dimension=0, tiled=True
        ).astype(jnp.float32),
        lax.psum_scatter(
            red_ctx[3].astype(jnp.bfloat16), "dp", scatter_dimension=0, tiled=True
        ).astype(jnp.float32),
    )
    gain_total = lax.psum(jnp.stack([gain_acc_one, gain_acc_two]), ("dp", "ctx"))
    shard_width = width // ctx_count
    own_gains = lax.dynamic_slice_in_dim(
        gain_total, lax.axis_index("ctx") * shard_width, shard_width, 1
    )
    output = jnp.concatenate(outputs, axis=0)
    grad_input = jnp.concatenate(grad_parts, axis=0)
    return (
        output,
        grad_input,
        own_gains[0],
        red_dp[0],
        red_dp[1],
        own_gains[1],
        red_dp[2],
        red_dp[3],
    )


def solution(mesh):
    row, split = P("dp", "ctx"), P("dp", "ctx", None)
    in_specs = (split, P("dp"), P("ctx"), row, row, P("ctx"), row, row, split)
    out_specs = (split, split, P("ctx"), row, row, P("ctx"), row, row)

    def run(block_input, prefix, ln1_gain, w_qkv, w_out, ln2_gain, w_up, w_down, grad_y):
        body = functools.partial(fused, NC) if fits(mesh, block_input, w_down) else local
        return jax.shard_map(body, mesh=mesh, in_specs=in_specs, out_specs=out_specs, check_vma=False)(
            block_input, prefix, ln1_gain, w_qkv, w_out, ln2_gain, w_up, w_down, grad_y
        )

    return run
```

```python
import functools
import math

import jax
import jax.numpy as jnp
from jax import lax
from jax.experimental import pallas as pl
from jax.experimental.pallas import tpu as pltpu
from jax.sharding import PartitionSpec as P

H = 8
MICRO = 2


EPS = 1e-05
NEG = -1e30

MESH = pl.DeviceIdType.MESH
F32 = jnp.float32
BF16 = jnp.bfloat16
NN = (((1,), (0,)), ((), ()))
NT = (((1,), (1,)), ((), ()))
TN = (((0,), (0,)), ((), ()))
GELU_A = math.sqrt(2.0 / math.pi)
GELU_B = 0.044715

NZ, NW, ND = 4, 2 * 2, 2
NC = NZ * NW
WORDS = 128
BQ = 2 * WORDS
GROWS = 16
PACK = 4
BA = PACK * WORDS
DH = 64


def dot(a, b, dims=NN):
    return lax.dot_general(a, b, dims, preferred_element_type=F32)


def sum_rows(v):
    return jnp.sum(v, axis=0, keepdims=True)


class Wires:
    def __init__(self, send, recv):
        self.send, self.recv, self.used, self.out, self.open = send, recv, 0, 0, []

    def slots(self, count):
        first = self.used
        self.used += count
        return first

    def group(self, ref, when=None):
        self.out += 1
        self.open.append((ref, self.out - 1, when))
        return self.out - 1

    def copy(self, src, dst, slot, device, out=0):
        return pltpu.make_async_remote_copy(
            src_ref=src,
            dst_ref=dst,
            send_sem=self.send.at[out],
            recv_sem=self.recv.at[slot],
            device_id=device,
            device_id_type=MESH,
        )

    def start(self, src, dst, slot, device, out=None):
        out = self.group(src) if out is None else out
        self.copy(src, dst, slot, device, out).start()

    def landed(self, dst, slot, device):
        self.copy(dst, dst, slot, device).wait_recv()

    def drain(self, device):
        for ref, out, when in self.open:
            sent = self.copy(ref, ref, 0, device, out)
            if when is None:
                sent.wait_send()
            else:
                pl.when(when)(sent.wait_send)


class Place:
    def __init__(self):
        self.me = lax.axis_index("ctx")
        self.d = lax.axis_index("dp")
        self.z = self.me // NW
        self.w = lax.rem(self.me, NW)
        x, y = lax.rem(self.w, 2), self.w // 2
        self.w1 = y * 2 + (1 - x)
        self.w2 = (1 - y) * 2 + x
        self.w3 = (1 - y) * 2 + (1 - x)
        self.other = 1 - self.d
        self.partner = {"dp": self.other}
        self.across_x = {"ctx": self.z * NW + self.w1}
        self.across_y = {"ctx": self.z * NW + self.w2}

    def up(self, step):
        return lax.rem(self.z + step, NZ)

    def down(self, step):
        return lax.rem(self.z - step + NZ, NZ)

    def along_z(self, step):
        return {"ctx": self.up(step) * NW + self.w}


class Gather:
    def __init__(self, wires, place, buf):
        self.wires, self.at, self.buf = wires, place, buf
        self.half = buf.shape[3] // 2
        self.sz = wires.slots(NZ - 1)
        self.sx, self.sy = wires.slots(NZ), wires.slots(NZ)
        self.se, self.sf = wires.slots(NZ), wires.slots(NZ)
        self.sp = wires.slots(1)
        row = buf.at[0, 0]
        z = place.z
        self.has_up, self.has_down = z < NZ - 1, z > 0
        self.o_up = wires.group(buf.at[0, 0, 0], self.has_up)
        self.o_down = wires.group(buf.at[0, 0, 0], self.has_down)
        self.oz = wires.group(buf.at[0, 0, pl.ds(0, NZ - 1)], self.has_up & self.has_down)
        first = jnp.where(z == 0, 3, 1)
        last = jnp.where(z == 0, 1, jnp.where(z == NZ - 1, 3, 2))
        self.order = (first, 6 - first - last, last)
        self.ox, self.oy = wires.group(row), wires.group(row)
        self.oe = wires.group(buf.at[0, 0, :, pl.ds(0, self.half)])
        self.of = wires.group(buf.at[0, 0, :, pl.ds(0, self.half)])
        self.op = wires.group(buf.at[0])

    def block(self, step, w):
        return self.buf.at[self.at.d, self.at.down(step), w]

    def top(self, ref):
        return ref.at[pl.ds(0, self.half)]

    def low(self, ref):
        return ref.at[pl.ds(self.half, self.half)]

    def send_z(self, src):
        p = self.at
        dst = self.block(0, p.w)

        @pl.when(self.has_up)
        def _():
            self.wires.start(src, dst, self.sz, p.along_z(1), self.o_up)

        @pl.when(self.has_down)
        def _():
            self.wires.start(src, dst, self.sz + NZ - 2, p.along_z(NZ - 1), self.o_down)

    def wait_z(self, step):
        self.wires.landed(self.block(step, self.at.w), self.sz + step - 1, self.at.along_z(step))

    def pass_z(self, step):
        p = self.at
        self.wait_z(step)
        b = self.block(step, p.w)

        @pl.when((p.z >= step) & self.has_up)
        def _():
            self.wires.start(b, b, self.sz + step, p.along_z(1), self.oz)

        @pl.when((p.z < step) & self.has_down)
        def _():
            self.wires.start(b, b, self.sz + step - 2, p.along_z(NZ - 1), self.oz)

    def send_plane(self, step):
        p, b = self.at, self.block(step, self.at.w)
        self.wires.start(b, b, self.sx + step, p.across_x, self.ox)
        self.wires.start(b, b, self.sy + step, p.across_y, self.oy)

    def send_core(self, group, step):
        p = self.at
        b = self.block(step, (p.w, p.w1, p.w2, p.w3)[group])
        self.wires.start(b, b, self.sp, p.partner, self.op)

    def relay_plane(self, step):
        p = self.at
        bx, by = self.block(step, p.w1), self.block(step, p.w2)
        self.wires.landed(bx, self.sx + step, p.across_x)
        self.wires.start(self.top(bx), self.top(bx), self.se + step, p.across_y, self.oe)
        self.send_core(1, step)
        self.wires.landed(by, self.sy + step, p.across_y)
        self.wires.start(self.low(by), self.low(by), self.sf + step, p.across_x, self.of)
        self.send_core(2, step)

    def relay_corner(self, step):
        p, b = self.at, self.block(step, self.at.w3)
        self.wires.landed(self.top(b), self.se + step, p.across_y)
        self.wires.landed(self.low(b), self.sf + step, p.across_x)
        self.send_core(3, step)

    def wait_core(self):
        self.wires.landed(self.buf.at[self.at.other], self.sp, self.at.partner)


class Scatter:
    def __init__(self, wires, place, buf, from_core, from_x, from_y, relay, column, from_z):
        self.wires, self.at, self.buf = wires, place, buf
        self.from_core, self.from_x, self.from_y = from_core, from_x, from_y
        self.relay, self.column, self.from_z = relay, column, from_z
        self.rows = buf.shape[3]
        self.half = self.rows // 2
        self.sp = wires.slots(1)
        self.sx, self.sy = wires.slots(3), wires.slots(3)
        self.sz = wires.slots(NZ - 1)

    def part(self, w, low):
        return self.buf.at[self.at.d, :, w, pl.ds(self.half if low else 0, self.half)]

    def send_core(self):
        p = self.at
        self.wires.start(self.buf.at[p.other], self.from_core, self.sp, p.partner)

    def add_core(self):
        p = self.at
        self.wires.landed(self.from_core, self.sp, p.partner)

        def add(k, carry):
            z, w = k // NW, lax.rem(k, NW)
            mine = self.buf[p.d, z, w].astype(F32)
            self.buf[p.d, z, w] = (mine + self.from_core[z, w].astype(F32)).astype(BF16)
            return carry

        lax.fori_loop(0, NC, add, 0)

    def send_plane(self):
        p = self.at
        for k, w in enumerate((p.w3, p.w1)):
            self.wires.start(self.part(w, False), self.from_x.at[k], self.sx + k, p.across_x)
        for k, w in enumerate((p.w3, p.w2)):
            self.wires.start(self.part(w, True), self.from_y.at[k], self.sy + k, p.across_y)

    def relay_corner(self):
        p, h = self.at, self.half
        self.wires.landed(self.from_x.at[0], self.sx, p.across_x)

        def add_top(z, carry):
            mine = self.buf[p.d, z, p.w2, pl.ds(0, h)].astype(F32)
            self.relay[0, z] = (mine + self.from_x[0, z].astype(F32)).astype(BF16)
            return carry

        lax.fori_loop(0, NZ, add_top, 0)
        self.wires.start(self.relay.at[0], self.from_y.at[2], self.sy + 2, p.across_y)
        self.wires.landed(self.from_y.at[0], self.sy, p.across_y)

        def add_low(z, carry):
            mine = self.buf[p.d, z, p.w1, pl.ds(h, h)].astype(F32)
            self.relay[1, z] = (mine + self.from_y[0, z].astype(F32)).astype(BF16)
            return carry

        lax.fori_loop(0, NZ, add_low, 0)
        self.wires.start(self.relay.at[1], self.from_x.at[2], self.sx + 2, p.across_x)

    def send_z(self):
        p, h = self.at, self.half
        self.wires.landed(self.from_x.at[1], self.sx + 1, p.across_x)
        self.wires.landed(self.from_y.at[1], self.sy + 1, p.across_y)
        self.wires.landed(self.from_y.at[2], self.sy + 2, p.across_y)
        self.wires.landed(self.from_x.at[2], self.sx + 2, p.across_x)

        def add(z, carry):
            top = self.buf[p.d, z, p.w, pl.ds(0, h)].astype(F32)
            top = top + self.from_x[1, z].astype(F32) + self.from_y[2, z].astype(F32)
            self.column[z, pl.ds(0, h)] = top.astype(BF16)
            low = self.buf[p.d, z, p.w, pl.ds(h, h)].astype(F32)
            low = low + self.from_y[1, z].astype(F32) + self.from_x[2, z].astype(F32)
            self.column[z, pl.ds(h, h)] = low.astype(BF16)
            return carry

        lax.fori_loop(0, NZ, add, 0)
        for step in range(1, NZ):
            self.wires.start(
                self.column.at[p.up(step)], self.from_z.at[step - 1], self.sz + step - 1, p.along_z(step)
            )

    def total(self):
        p = self.at
        for step in range(1, NZ):
            self.wires.landed(self.from_z.at[step - 1], self.sz + step - 1, p.along_z(step))
        acc = self.column[p.z].astype(F32)
        for step in range(1, NZ):
            acc = acc + self.from_z[step - 1].astype(F32)
        return acc


class Exchange:
    def __init__(self, wires, place, src, dst, inner=None):
        self.wires, self.at, self.src, self.dst = wires, place, src, dst
        self.inner = inner
        self.slot = wires.slots(1)
        self.rest = dst.at[pl.ds(0, NC - 1)] if inner is None else dst.at[pl.ds(0, NC - 1), inner]
        self.out = wires.group(self.rest)

    def view(self, ref, k):
        return ref.at[k] if self.inner is None else ref.at[k, self.inner]

    def send(self, offset):
        to = lax.rem(self.at.me + offset, NC)
        return self.wires.copy(
            self.view(self.src, to), self.view(self.dst, self.at.me), self.slot, {"ctx": to}, self.out
        )

    def send_to(self, chip):
        offset = lax.rem(chip - self.at.me + NC, NC)

        @pl.when(offset > 0)
        def _():
            self.send(offset).start()

        @pl.when(offset == 0)
        def _():
            self.keep()

    def keep(self):
        me = self.at.me
        if self.inner is None:
            self.dst[me] = self.src[me]
        else:
            self.dst[me, self.inner] = self.src[me, self.inner]

    def send_all(self):
        for offset in range(1, NC):
            self.send(offset).start()
        self.keep()

    def wait(self):
        self.wires.landed(self.rest, self.slot, self.at.partner)


def norm_stats(v):
    centred = v - jnp.mean(v, axis=0, keepdims=True)
    rstd = lax.rsqrt(jnp.mean(centred * centred, axis=0, keepdims=True) + EPS)
    return centred * rstd, rstd


def norm_back(grad, hat, rstd, gain):
    g = grad * gain
    return rstd * (g - jnp.mean(g, axis=0, keepdims=True) - hat * jnp.mean(g * hat, axis=0, keepdims=True))


def gelu_both(p):
    t = jnp.tanh(GELU_A * (p + GELU_B * p * p * p))
    half = 0.5 * (1.0 + t)
    slope = half + 0.5 * p * (1.0 - t * t) * (GELU_A * (1.0 + 3.0 * GELU_B * p * p))
    return p * half, slope


def step_kernel(
    prefix_ref, x_hbm, dy_hbm, gains_hbm, wq_hbm, wo_hbm, wu_hbm, wd_hbm,
    out_hbm, gx_hbm, gq_hbm, go_hbm, gu_hbm, gd_hbm, g1_hbm, g2_hbm,
    send_sem, recv_sem, own_sem,
    x_ref, dy_ref, WU, out_ref, gx_ref, gq_ref, gf_ref, GU, G1, G2,
    QG, FG, HAT1, RST1, NRM, DYT,
    QS, QR, KN, VN, PR, OT, LI, TOP, LAST, AS, AR, ATT,
    RES, HAT2, RST2, NRM2, ACT, SLOPE, DPRE, ACC, DRES, DAI,
    DS, DR, DEL, DQ, DQS, DPR, DPJ,
    GF, GFC, GFX, GFY, GFR, GFS, GFZ,
    GQ, GQC, GQX, GQY, GQR, GQS, GQZ,
    TS, TR,
):
    place = Place()
    wires = Wires(send_sem, recv_sem)
    me = place.me
    width = HAT1.shape[0]
    heads = width // DH
    half = width // 2
    qrows, frows = QG.shape[3], FG.shape[3]
    nq = PR.shape[0]
    pre_blocks = nq // 2
    orow = width // NC
    urow = ACT.shape[0] * BQ // NC
    nf = ACT.shape[0]

    gq = Gather(wires, place, QG)
    gf = Gather(wires, place, FG)
    qkv_x = Exchange(wires, place, QS, QR)
    att_x = Exchange(wires, place, AS, AR)
    datt_x = Exchange(wires, place, DS, DR)
    dkv_x = Exchange(wires, place, DQS, DPR, pl.ds(1, 2))
    dq_x = Exchange(wires, place, DQS, DPR, pl.ds(0, 1))
    sf = Scatter(wires, place, GF, GFC, GFX, GFY, GFR, GFS, GFZ)
    sq = Scatter(wires, place, GQ, GQC, GQX, GQY, GQR, GQS, GQZ)
    tot = wires.slots(6)

    barrier = pltpu.get_barrier_semaphore()
    for offset in range(1, NC):
        pl.semaphore_signal(barrier, inc=1, device_id={"ctx": lax.rem(me + offset, NC)}, device_id_type=MESH)
    pl.semaphore_signal(barrier, inc=1, device_id=place.partner, device_id_type=MESH)

    mine_q, mine_f = gq.block(0, place.w), gf.block(0, place.w)
    local = [0]

    def local_copy(src, dst):
        c = pltpu.make_async_copy(src, dst, own_sem.at[local[0]])
        local[0] += 1
        c.start()
        return c

    first = [
        local_copy(gains_hbm, mine_q.at[pl.ds(0, GROWS)]),
        local_copy(wq_hbm, mine_q.at[pl.ds(GROWS, qrows - GROWS)]),
    ]
    words_in = local_copy(x_hbm, x_ref)
    up_in = local_copy(wu_hbm, WU)
    rest = [local_copy(wo_hbm, mine_f.at[pl.ds(0, orow)])]
    for c in range(4):
        rest.append(
            local_copy(wd_hbm.at[:, pl.ds(c * 256, 256)], mine_f.at[pl.ds(orow + urow + c * orow, orow)])
        )
    dy_in = local_copy(dy_hbm, dy_ref)
    for c in first:
        c.wait()
    pl.semaphore_wait(barrier, NC)

    gq.send_z(gq.block(0, place.w))
    gq.send_plane(0)
    gq.send_core(0, 0)

    up_in.wait()
    FG[place.d, place.z, place.w, pl.ds(orow, urow), :] = WU[...].astype(F32).T.astype(BF16)
    words_in.wait()
    hat, rstd = norm_stats(x_ref[...].astype(F32).T)
    HAT1[...] = hat
    RST1[...] = rstd
    for c in rest:
        c.wait()
    gf.send_plane(0)
    gf.send_core(0, 0)

    for step in gq.order:
        gq.pass_z(step)
        gq.send_plane(step)
        gq.send_core(0, step)
    gf.send_z(gf.block(0, place.w))
    dy_in.wait()
    DYT[...] = dy_ref[...].astype(F32).T.astype(BF16)
    for step in (0, *gq.order):
        gq.relay_plane(step)
    gf.pass_z(gf.order[0])
    for step in (0, *gq.order):
        gq.relay_corner(step)
    gf.pass_z(gf.order[1])
    gq.wait_core()
    gf.pass_z(gf.order[2])

    gains = QG[0, :, :, pl.ds(0, GROWS), :].reshape(NC * GROWS, 256).astype(F32).T
    gain_one, gain_two = (
        jnp.concatenate([gains[r:r + orow, k * GROWS:k * GROWS + 1] for k in range(NC)], axis=0) for r in (0, 128)
    )
    NRM[...] = (HAT1[...] * gain_one).astype(BF16)
    wrows = qrows - GROWS
    for j in range(NZ):
        proj = sum(
            dot(QG[k, j, :, pl.ds(GROWS, wrows), :].reshape(NW * wrows, 256), NRM[k * half:(k + 1) * half])
            for k in range(ND)
        )
        for t in range(NW * wrows // DH):
            kind, head = divmod(j * (NW * wrows // DH) + t, heads)
            unit = proj[t * DH:(t + 1) * DH].astype(BF16)
            if kind == 0:
                unit = (unit.astype(F32) * DH ** (-0.5)).astype(BF16)
            for b in range(2):
                QS[b * heads + head, kind] = unit[:, b * WORDS:(b + 1) * WORDS]
    qkv_x.send_all()

    for step in gf.order:
        gf.send_plane(step)
        gf.send_core(0, step)

    qkv_x.wait()
    prefix = prefix_ref[me // heads]

    def to_rows(c, carry):
        rows = pl.ds(pl.multiple_of(c * WORDS, WORDS), WORDS)
        KN[rows, :] = QR[c, 1].astype(F32).T.astype(BF16)
        VN[rows, :] = QR[c, 2].astype(F32).T.astype(BF16)
        return carry

    lax.fori_loop(0, NC, to_rows, 0)

    def pair(ref, b, kind=None):
        parts = [ref[PACK * b + k] if kind is None else ref[PACK * b + k, kind] for k in range(PACK)]
        return jnp.concatenate(parts, axis=1)

    def rows_of(b):
        return pl.ds(pl.multiple_of(b * BA, BA), BA)

    def attend(qb, carry):
        queries = pair(QR, qb, 0)

        def step(masked, kb, state):
            top, total, acc = state
            s = dot(KN[rows_of(kb), :], queries)
            if masked:
                key = kb * BA + lax.broadcasted_iota(jnp.int32, (BA, BA), 0)
                word = qb * BA + lax.broadcasted_iota(jnp.int32, (BA, BA), 1)
                s = jnp.where((key <= word) | (key < prefix), s, NEG)
            high = jnp.max(jnp.max(s.reshape(BA // 8, 8, BA), axis=0), axis=0, keepdims=True)
            new = jnp.maximum(top, high)
            TOP[qb, kb] = new
            scale = jnp.exp(top - new)
            p = jnp.exp(s - new)
            total = total * scale + jnp.sum(p.reshape(BA // 8, 8, BA), axis=0)
            p = p.astype(BF16)
            PR[qb, rows_of(kb), :] = p
            return new, total, acc * scale + dot(pair(QR, kb, 2), p)

        state = (jnp.full((1, BA), NEG, F32), jnp.zeros((8, BA), F32), jnp.zeros((DH, BA), F32))
        state = lax.fori_loop(0, qb, functools.partial(step, False), state)
        last = jnp.maximum(qb + 1, pre_blocks)
        top, total, acc = lax.fori_loop(qb, last, functools.partial(step, True), state)
        inv = 1.0 / jnp.sum(total, axis=0, keepdims=True)
        out = acc * inv
        OT[qb] = out
        LI[qb] = inv
        LAST[qb] = top
        out = out.astype(BF16)
        for k in range(PACK):
            AS[PACK * qb + k] = out[:, k * WORDS:(k + 1) * WORDS]
            att_x.send_to(PACK * qb + k)
        return carry

    lax.fori_loop(0, nq // 2, attend, 0)
    for step in (0, *gf.order):
        gf.relay_plane(step)
    lax.fori_loop(nq // 2, nq, attend, 0)
    for step in (0, *gf.order):
        gf.relay_corner(step)

    att_x.wait()
    gf.wait_core()
    for h in range(heads):
        ATT[h * DH:(h + 1) * DH] = jnp.concatenate([AR[h], AR[heads + h]], axis=1)

    def w_out(k):
        return FG[k, :, :, pl.ds(0, orow), :].reshape(width, 256)

    def w_up(k, c):
        return FG[k, c // 2, pl.ds(2 * (c % 2), 2), pl.ds(orow, urow), :].reshape(BQ, 256)

    def w_down(c):
        rows = orow + urow + (c % 4) * orow
        return FG[c // 4, :, :, pl.ds(rows, orow), :].reshape(width, 256)

    mixed = sum(dot(w_out(k), ATT[k * half:(k + 1) * half]) for k in range(ND))
    res = x_ref[...].astype(F32).T + mixed
    RES[...] = res
    hat2, rstd2 = norm_stats(res)
    HAT2[...] = hat2
    RST2[...] = rstd2
    NRM2[...] = (hat2 * gain_two).astype(BF16)

    for c in range(nf):
        pre = sum(dot(w_up(k, c), NRM2[k * half:(k + 1) * half]) for k in range(ND))
        act, slope = gelu_both(pre)
        ACT[c] = act.astype(BF16)
        SLOPE[c] = slope
    ACC[...] = jnp.zeros_like(ACC)
    for c in range(nf):
        dact = dot(w_down(c), DYT[...], TN)
        dpre = (dact * SLOPE[c]).astype(BF16)
        DPRE[c] = dpre
        for k in range(ND):
            ACC[k * half:(k + 1) * half] += dot(w_up(k, c), dpre, TN)
    dn2 = ACC[...]
    dres = DYT[...].astype(F32) + norm_back(dn2, HAT2[...], RST2[...], gain_two)
    DRES[...] = dres
    DAI[...] = dres.astype(BF16)
    ones = jnp.ones((8, 2 * WORDS), F32)
    row_two = lax.dot_general(
        ones, dn2 * HAT2[...], NT, precision=lax.Precision.HIGHEST, preferred_element_type=F32
    )
    for k in range(ND):
        datt = dot(w_out(k), DAI[...], TN).astype(BF16)
        for t in range(half // DH):
            h = k * (half // DH) + t
            for b in range(2):
                DS[b * heads + h] = datt[t * DH:(t + 1) * DH, b * WORDS:(b + 1) * WORDS]
    datt_x.send_all()

    for r in range(2):
        acc = RES[r * half:(r + 1) * half]
        for c in range(nf):
            rows = orow + urow + (c % 4) * orow
            w = FG[c // 4, pl.ds(2 * r, 2), :, pl.ds(rows, orow), :].reshape(half, 256)
            acc = acc + dot(w, ACT[c])
        out_ref[:, r * half:(r + 1) * half] = acc.T.astype(BF16)
    outs = [local_copy(out_ref, out_hbm)]
    for c in range(nf):
        rows = orow + urow + (c % 4) * orow
        GF[c // 4, :, :, pl.ds(rows, orow), :] = dot(DYT[...], ACT[c], NT).astype(BF16).reshape(NZ, NW, orow, 256)
        for k in range(ND):
            up = dot(DPRE[c], NRM2[k * half:(k + 1) * half], NT).astype(BF16)
            GF[k, c // 2, pl.ds(2 * (c % 2), 2), pl.ds(orow, urow), :] = up.reshape(2, urow, 256)
    for k in range(ND):
        mix = dot(DAI[...], ATT[k * half:(k + 1) * half], NT).astype(BF16)
        GF[k, :, :, pl.ds(0, orow), :] = mix.reshape(NZ, NW, orow, 256)
    sf.send_core()

    datt_x.wait()

    def ready(qb, carry):
        DEL[qb] = sum_rows(pair(DR, qb).astype(F32) * OT[qb])
        DQ[qb] = jnp.zeros((DH, BA), F32)
        return carry

    lax.fori_loop(0, nq, ready, 0)

    def put(ref, b, kind, val):
        val = val.astype(BF16)
        for k in range(PACK):
            ref[PACK * b + k, kind] = val[:, k * WORDS:(k + 1) * WORDS]

    def send_dq(qb):
        put(DQS, qb, 0, DQ[qb] * DH ** (-0.5))
        for k in range(PACK):
            dq_x.send_to(PACK * qb + k)

    def attend_back(kb, carry, finish=False):
        keys, vals, keys_t = KN[rows_of(kb), :], VN[rows_of(kb), :], pair(QR, kb, 1)
        first = jnp.where(kb < pre_blocks, 0, kb)

        def one(qb, state):
            dk, dv = state
            norm = jnp.exp(TOP[qb, kb] - LAST[qb]) * LI[qb]
            datt = (pair(DR, qb).astype(F32) * norm).astype(BF16)
            dp = dot(vals, datt)
            p = PR[qb, rows_of(kb), :]
            ds = (p.astype(F32) * (dp - DEL[qb] * norm)).astype(BF16)
            DQ[qb] += dot(keys_t, ds)
            if finish:
                send_dq(qb)
            return dk + dot(pair(QR, qb, 0), ds, NT), dv + dot(datt, p, NT)

        zero = jnp.zeros((DH, BA), F32)
        dk, dv = lax.fori_loop(first, nq, one, (zero, zero))
        put(DQS, kb, 1, dk)
        put(DQS, kb, 2, dv)
        for k in range(PACK):
            dkv_x.send_to(PACK * kb + k)
        return carry

    def back_from_last(i, carry):
        return attend_back(nq - 1 - i, carry)

    lax.fori_loop(0, 1, back_from_last, 0)
    sf.add_core()
    sf.send_plane()
    lax.fori_loop(1, nq - 1, back_from_last, 0)
    attend_back(0, 0, True)
    sf.relay_corner()
    dq_x.wait()
    dkv_x.wait()

    for kind in range(3):
        for h in range(heads):
            r = (kind * heads + h) * DH
            DPJ[r:r + DH] = jnp.concatenate([DPR[h, kind], DPR[heads + h, kind]], axis=1)
    blk = NW * wrows
    for j in range(NZ):
        for k in range(ND):
            g = dot(DPJ[j * blk:(j + 1) * blk], NRM[k * half:(k + 1) * half], NT)
            GQ[k, j] = g.astype(BF16).reshape(NW, wrows, 256)
    sq.send_core()
    sf.send_z()
    ACC[...] = jnp.zeros_like(ACC)
    for k in range(ND):
        for j in range(NZ):
            w = QG[k, j, :, pl.ds(GROWS, wrows), :].reshape(blk, 256)
            ACC[k * half:(k + 1) * half] += dot(w, DPJ[j * blk:(j + 1) * blk], TN)
    dn1 = ACC[...]
    gx_ref[...] = (DRES[...] + norm_back(dn1, HAT1[...], RST1[...], gain_one)).T
    outs.append(local_copy(gx_ref, gx_hbm))
    row_one = lax.dot_general(
        ones, dn1 * HAT1[...], NT, precision=lax.Precision.HIGHEST, preferred_element_type=F32
    )

    TS[0] = jnp.where(lax.broadcasted_iota(jnp.int32, (8, width), 0) == 0, row_one, row_two)
    wires.start(TS.at[0], TR.at[0], tot, place.partner)
    sq.add_core()
    sq.send_plane()
    wires.landed(TR.at[0], tot, place.partner)
    TS[1] = TS[0] + TR[0]
    wires.start(TS.at[1], TR.at[1], tot + 1, place.across_x)
    sq.relay_corner()
    wires.landed(TR.at[1], tot + 1, place.across_x)
    TS[2] = TS[1] + TR[1]
    wires.start(TS.at[2], TR.at[2], tot + 2, place.across_y)
    gf_ref[...] = sf.total()
    GU[...] = gf_ref[pl.ds(orow, urow), :].T
    outs.append(local_copy(gf_ref.at[pl.ds(0, orow)], go_hbm))
    outs.append(local_copy(GU, gu_hbm))
    for c in range(4):
        outs.append(local_copy(gf_ref.at[pl.ds(orow + urow + c * orow, orow)], gd_hbm.at[:, pl.ds(c * 256, 256)]))
    sq.send_z()
    wires.landed(TR.at[2], tot + 2, place.across_y)
    TS[3] = TS[2] + TR[2]
    for step in range(1, NZ):
        wires.start(TS.at[3], TR.at[2 + step], tot + 2 + step, place.along_z(step))
    gq_ref[...] = sq.total()
    outs.append(local_copy(gq_ref, gq_hbm))
    for step in range(1, NZ):
        wires.landed(TR.at[2 + step], tot + 2 + step, place.along_z(step))
    picked = lax.broadcasted_iota(jnp.int32, (width, 128), 0) == me * orow + lax.broadcasted_iota(
        jnp.int32, (width, 128), 1
    )
    own = lax.dot_general(
        TS[3] + TR[3] + TR[4] + TR[5], picked.astype(F32), NN,
        precision=lax.Precision.HIGHEST, preferred_element_type=F32,
    )
    G1[...] = own[0:1, 0:orow]
    G2[...] = own[1:2, 0:orow]
    outs.append(local_copy(G1, g1_hbm))
    outs.append(local_copy(G2, g2_hbm))

    assert (wires.out, wires.used, local[0]) == (N_SEND, N_RECV, N_OWN), (wires.out, wires.used, local[0])
    wires.drain(place.partner)
    for c in outs:
        c.wait()


def fused(ctx_count, block_input, prefix, ln1_gain, w_qkv, w_out, ln2_gain, w_up, w_down, grad_y):
    width = block_input.shape[2]
    ff = w_down.shape[0] * ND
    words = 2 * WORDS
    nq = NC * WORDS // BA
    nf = ff // BQ
    orow, qrow, urow = width // NC, 3 * width // NC, ff // NC
    qrows, frows = GROWS + qrow, orow + urow + 4 * orow

    gains = jnp.concatenate([jnp.pad(g, (0, 128 - orow)) for g in (ln1_gain, ln2_gain)])
    gains = jnp.broadcast_to(gains[None], (GROWS, 256))
    x = block_input.reshape(words, width)
    dy = grad_y.reshape(words, width)

    def vm(*shape, dtype=BF16):
        return pltpu.VMEM(shape, dtype)

    def scatter_bufs(rows):
        return [
            vm(ND, NZ, NW, rows, 256),
            vm(NZ, NW, rows, 256),
            vm(3, NZ, rows // 2, 256),
            vm(3, NZ, rows // 2, 256),
            vm(2, NZ, rows // 2, 256),
            vm(NZ, rows, 256),
            vm(NZ - 1, rows, 256),
        ]

    length = NC * WORDS
    msgs = 512
    vmem = pl.BlockSpec(memory_space=pltpu.VMEM)
    hbm = pl.BlockSpec(memory_space=pl.ANY)
    out, gx, gq, g_out, g_up, g_down, g_one, g_two = pl.pallas_call(
        step_kernel,
        out_shape=(
            jax.ShapeDtypeStruct((words, width), BF16),
            jax.ShapeDtypeStruct((words, width), F32),
            jax.ShapeDtypeStruct((qrow, 256), F32),
            jax.ShapeDtypeStruct((orow, 256), F32),
            jax.ShapeDtypeStruct((256, urow), F32),
            jax.ShapeDtypeStruct((orow, 4 * 256), F32),
            jax.ShapeDtypeStruct((1, orow), F32),
            jax.ShapeDtypeStruct((1, orow), F32),
        ),
        in_specs=[pl.BlockSpec(memory_space=pltpu.SMEM)] + [hbm] * 7,
        out_specs=(hbm,) * 8,
        scratch_shapes=[
            pltpu.SemaphoreType.DMA((N_SEND,)),
            pltpu.SemaphoreType.DMA((N_RECV,)),
            pltpu.SemaphoreType.DMA((N_OWN,)),
            vm(words, width),
            vm(words, width),
            vm(256, urow),
            vm(words, width),
            vm(words, width, dtype=F32),
            vm(qrow, 256, dtype=F32),
            vm(frows, 256, dtype=F32),
            vm(256, urow, dtype=F32),
            vm(1, orow, dtype=F32),
            vm(1, orow, dtype=F32),
            vm(ND, NZ, NW, qrows, 256),
            vm(ND, NZ, NW, frows, 256),
            vm(width, words, dtype=F32),
            vm(1, words, dtype=F32),
            vm(width, words),
            vm(width, words),
            vm(NC, 3, DH, WORDS),
            vm(NC, 3, DH, WORDS),
            vm(length, DH),
            vm(length, DH),
            vm(nq, length, BA),
            vm(nq, DH, BA, dtype=F32),
            vm(nq, 1, BA, dtype=F32),
            vm(nq, nq, 1, BA, dtype=F32),
            vm(nq, 1, BA, dtype=F32),
            vm(NC, DH, WORDS),
            vm(NC, DH, WORDS),
            vm(width, words),
            vm(width, words, dtype=F32),
            vm(width, words, dtype=F32),
            vm(1, words, dtype=F32),
            vm(width, words),
            vm(nf, BQ, words),
            vm(nf, BQ, words, dtype=F32),
            vm(nf, BQ, words),
            vm(width, words, dtype=F32),
            vm(width, words, dtype=F32),
            vm(width, words),
            vm(NC, DH, WORDS),
            vm(NC, DH, WORDS),
            vm(nq, 1, BA, dtype=F32),
            vm(nq, DH, BA, dtype=F32),
            vm(NC, 3, DH, WORDS),
            vm(NC, 3, DH, WORDS),
            vm(3 * width, words),
            *scatter_bufs(frows),
            *scatter_bufs(qrow),
            vm(4, 8, width, dtype=F32),
            vm(6, 8, width, dtype=F32),
        ],
        compiler_params=pltpu.CompilerParams(
            collective_id=0, has_side_effects=True, vmem_limit_bytes=66 * 1024 * 1024 - 2 ** 21
        ),
        name="block_step",
    )(prefix, x, dy, gains, w_qkv.T, w_out.T, w_up, w_down.T)

    return (
        out.reshape(block_input.shape),
        gx.reshape(block_input.shape),
        g_one.reshape(ln1_gain.shape),
        gq.T,
        g_out.T,
        g_two.reshape(ln2_gain.shape),
        g_up,
        g_down.T,
    )


N_SEND, N_RECV, N_OWN = 47, 71, 21


def fits(mesh, block_input, w_down):
    seqs, length, width = block_input.shape
    return (
        mesh.shape["ctx"] == NC
        and mesh.shape["dp"] == ND
        and seqs == 2 * ND
        and length == NC * WORDS
        and width == H * DH
        and 2 * H == NC
        and w_down.shape[0] == 4 * width
    )


def layer_norm(values, gain):
    centred = values - jnp.mean(values, axis=-1, keepdims=True)
    spread = jnp.mean(centred * centred, axis=-1, keepdims=True)
    return centred * lax.rsqrt(spread + EPS) * gain


def row_product(left, right):
    return jnp.dot(left, right, preferred_element_type=jnp.float32)


def cross_rows(left, right):
    return lax.dot_general(
        left, right, (((0,), (0,)), ((), ())), preferred_element_type=jnp.float32
    )


def back_product(left, right):
    return lax.dot_general(
        left, right, (((1,), (1,)), ((), ())), preferred_element_type=jnp.float32
    )


def visible_mask(query_first, query_count, key_first, key_count, prefixes):
    query_pos = query_first + jnp.arange(query_count, dtype=jnp.int32)
    key_pos = key_first + jnp.arange(key_count, dtype=jnp.int32)
    causal = key_pos[None, :] <= query_pos[:, None]
    before = key_pos[None, None, :] < prefixes[:, None, None]
    return (causal[None] | before)[:, None]


def attend_forward(queries, keys_own, values_own, prefixes, my_first, scale):
    batch, rows, heads, head_dim = queries.shape
    key_first = jnp.int32(0)
    key_rows = lax.all_gather(keys_own, "ctx", axis=1, tiled=True)
    value_rows = lax.all_gather(values_own, "ctx", axis=1, tiled=True)
    count = key_rows.shape[1]
    top = jnp.full((batch, heads, rows), NEG, jnp.float32)
    summed = jnp.zeros((batch, rows, heads, head_dim), jnp.float32)
    keys_h = key_rows.reshape(batch, count, heads, head_dim)
    values_h = value_rows.reshape(batch, count, heads, head_dim)
    scores = (
        jnp.einsum("bqhd,bkhd->bhqk", queries, keys_h, preferred_element_type=jnp.float32) * scale
    )
    scores = jnp.where(visible_mask(my_first, rows, key_first, count, prefixes), scores, NEG)
    new_top = jnp.maximum(top, jnp.max(scores, axis=-1))
    factor = jnp.exp(top - new_top)
    probs = jnp.exp(scores - new_top[..., None])
    total = jnp.sum(probs, axis=-1)
    summed = summed * jnp.swapaxes(factor, 1, 2)[..., None] + jnp.einsum(
        "bhqk,bkhd->bqhd", probs.astype(jnp.bfloat16), values_h, preferred_element_type=jnp.float32
    )
    top, total, summed = (new_top, total, summed)
    attended = summed / jnp.swapaxes(total, 1, 2)[..., None]
    log_sum = top + jnp.log(total)
    return (attended.reshape(batch, rows, heads * head_dim), log_sum)


def attend_backward(
    queries, keys_own, values_own, attended, grad_att, log_sum, prefixes, my_first, scale
):
    batch, rows, heads, head_dim = queries.shape
    width = heads * head_dim
    keys_full, values_full = (
        lax.all_gather(keys_own, "ctx", axis=1, tiled=True),
        lax.all_gather(values_own, "ctx", axis=1, tiled=True),
    )
    length = keys_full.shape[1]
    key_block = math.gcd(length, 512)
    grad_h = grad_att.reshape(batch, rows, heads, head_dim)
    delta = jnp.swapaxes(
        jnp.sum(
            grad_h.astype(jnp.float32) * attended.reshape(batch, rows, heads, head_dim), axis=-1
        ),
        1,
        2,
    )

    def one_block(counter, carried):
        key_first = counter * key_block
        q_sum, k_sum, v_sum = carried
        keys_h = lax.dynamic_slice_in_dim(keys_full, key_first, key_block, 1).reshape(
            batch, key_block, heads, head_dim
        )
        values_h = lax.dynamic_slice_in_dim(values_full, key_first, key_block, 1).reshape(
            batch, key_block, heads, head_dim
        )
        scores = (
            jnp.einsum("bqhd,bkhd->bhqk", queries, keys_h, preferred_element_type=jnp.float32)
            * scale
        )
        scores = jnp.where(
            visible_mask(my_first, rows, key_first, key_block, prefixes), scores, NEG
        )
        probs = jnp.exp(scores - log_sum[..., None])
        grad_probs = jnp.einsum(
            "bqhd,bkhd->bhqk", grad_h, values_h, preferred_element_type=jnp.float32
        )
        grad_scores = (probs * (grad_probs - delta[..., None])).astype(jnp.bfloat16)
        q_sum = (
            q_sum
            + jnp.einsum("bhqk,bkhd->bqhd", grad_scores, keys_h, preferred_element_type=jnp.float32)
            * scale
        )
        v_part = jnp.einsum(
            "bhqk,bqhd->bkhd",
            probs.astype(jnp.bfloat16),
            grad_h,
            preferred_element_type=jnp.float32,
        )
        k_part = (
            jnp.einsum("bhqk,bqhd->bkhd", grad_scores, queries, preferred_element_type=jnp.float32)
            * scale
        )
        k_sum = lax.dynamic_update_slice_in_dim(
            k_sum, k_part.reshape(batch, key_block, width), key_first, 1
        )
        v_sum = lax.dynamic_update_slice_in_dim(
            v_sum, v_part.reshape(batch, key_block, width), key_first, 1
        )
        return (q_sum, k_sum, v_sum)

    initial = (
        jnp.zeros((batch, rows, heads, head_dim), jnp.float32),
        jnp.zeros((batch, length, width), jnp.float32),
        jnp.zeros((batch, length, width), jnp.float32),
    )
    q_sum, k_sum, v_sum = lax.fori_loop(0, length // key_block, one_block, initial)
    k_own, v_own = (
        lax.psum_scatter(k_sum.astype(jnp.bfloat16), "ctx", scatter_dimension=1, tiled=True).astype(
            jnp.float32
        ),
        lax.psum_scatter(v_sum.astype(jnp.bfloat16), "ctx", scatter_dimension=1, tiled=True).astype(
            jnp.float32
        ),
    )
    return (q_sum.reshape(batch, rows, width), k_own, v_own)


def local(block_input, prefix, ln1_gain, w_qkv, w_out, ln2_gain, w_up, w_down, grad_y):
    ctx_count = lax.axis_size("ctx")
    blk_rows = block_input.shape[1]
    width = block_input.shape[2]
    head_dim = width // H
    scale = head_dim ** (-0.5)
    my_first = lax.axis_index("ctx") * blk_rows
    per_micro = block_input.shape[0] // MICRO
    by_ctx = (
        lax.all_gather(w_qkv, "ctx", axis=1, tiled=True),
        lax.all_gather(w_out, "ctx", axis=1, tiled=True),
        lax.all_gather(w_up, "ctx", axis=1, tiled=True),
        lax.all_gather(w_down, "ctx", axis=1, tiled=True),
        lax.all_gather(ln1_gain, "ctx", axis=0, tiled=True),
        lax.all_gather(ln2_gain, "ctx", axis=0, tiled=True),
    )
    full_fwd = (
        lax.all_gather(by_ctx[0], "dp", axis=0, tiled=True),
        lax.all_gather(by_ctx[1], "dp", axis=0, tiled=True),
        lax.all_gather(by_ctx[2], "dp", axis=0, tiled=True),
        lax.all_gather(by_ctx[3], "dp", axis=0, tiled=True),
    )
    gain_one = by_ctx[4].astype(jnp.float32)
    gain_two = by_ctx[5].astype(jnp.float32)
    saved = []
    outputs = []
    for micro_idx in range(MICRO):
        lower_row = micro_idx * per_micro
        inputs = block_input[lower_row : lower_row + per_micro].astype(jnp.float32)
        prefixes = prefix[lower_row : lower_row + per_micro]
        flat = inputs.reshape(-1, width)
        normed = layer_norm(flat, gain_one).astype(jnp.bfloat16)
        projected = (
            row_product(normed, full_fwd[0])
            .astype(jnp.bfloat16)
            .reshape(per_micro, blk_rows, 3 * width)
        )
        queries = projected[..., :width].reshape(per_micro, blk_rows, H, head_dim)
        keys_own = projected[..., width : 2 * width]
        values_own = projected[..., 2 * width :]
        attended, log_sum = attend_forward(queries, keys_own, values_own, prefixes, my_first, scale)
        mixed_in = attended.reshape(-1, width).astype(jnp.bfloat16)
        resid = flat + row_product(mixed_in, full_fwd[1])
        normed_two = layer_norm(resid, gain_two).astype(jnp.bfloat16)
        hidden_pre = row_product(normed_two, full_fwd[2])
        activated = jax.nn.gelu(hidden_pre).astype(jnp.bfloat16)
        result = resid + row_product(activated, full_fwd[3])
        outputs.append(result.astype(jnp.bfloat16).reshape(per_micro, blk_rows, width))
        saved.append(
            (
                flat,
                normed,
                queries,
                keys_own,
                values_own,
                attended,
                log_sum,
                mixed_in,
                resid,
                normed_two,
                hidden_pre,
                activated,
                prefixes,
            )
        )
    back_ctx = (
        lax.all_gather(w_qkv, "ctx", axis=1, tiled=True),
        lax.all_gather(w_out, "ctx", axis=1, tiled=True),
        lax.all_gather(w_up, "ctx", axis=1, tiled=True),
        lax.all_gather(w_down, "ctx", axis=1, tiled=True),
    )
    w_back = (
        lax.all_gather(back_ctx[0], "dp", axis=0, tiled=True),
        lax.all_gather(back_ctx[1], "dp", axis=0, tiled=True),
        lax.all_gather(back_ctx[2], "dp", axis=0, tiled=True),
        lax.all_gather(back_ctx[3], "dp", axis=0, tiled=True),
    )
    sum_proj = jnp.zeros(w_back[0].shape, jnp.float32)
    sum_mix = jnp.zeros(w_back[1].shape, jnp.float32)
    sum_expand = jnp.zeros(w_back[2].shape, jnp.float32)
    sum_reduce = jnp.zeros(w_back[3].shape, jnp.float32)
    gain_acc_one = jnp.zeros((width,), jnp.float32)
    gain_acc_two = jnp.zeros((width,), jnp.float32)
    grad_parts = [None] * MICRO
    for micro_idx in reversed(range(MICRO)):
        (
            flat,
            normed,
            queries,
            keys_own,
            values_own,
            attended,
            log_sum,
            mixed_in,
            resid,
            normed_two,
            hidden_pre,
            activated,
            prefixes,
        ) = saved[micro_idx]
        lower_row = micro_idx * per_micro
        cot_b = grad_y[lower_row : lower_row + per_micro].reshape(-1, width)
        cotangent = cot_b.astype(jnp.float32)
        sum_reduce = sum_reduce + cross_rows(activated, cot_b)
        grad_act = back_product(cot_b, w_back[3])
        gelu_pull = jax.vjp(jax.nn.gelu, hidden_pre)[1]
        grad_hidden = gelu_pull(grad_act)[0].astype(jnp.bfloat16)
        sum_expand = sum_expand + cross_rows(normed_two, grad_hidden)
        grad_normed_two = back_product(grad_hidden, w_back[2])
        norm_pull_two = jax.vjp(layer_norm, resid, gain_two)[1]
        grad_resid_part, grad_gain_two = norm_pull_two(grad_normed_two)
        grad_resid = cotangent + grad_resid_part
        grad_mix_b = grad_resid.astype(jnp.bfloat16)
        sum_mix = sum_mix + cross_rows(mixed_in, grad_mix_b)
        grad_attended = back_product(grad_mix_b, w_back[1]).astype(jnp.bfloat16)
        q_grad, k_grad, v_grad = attend_backward(
            queries,
            keys_own,
            values_own,
            attended,
            grad_attended.reshape(per_micro, blk_rows, width),
            log_sum,
            prefixes,
            my_first,
            scale,
        )
        grad_proj = (
            jnp.concatenate([q_grad, k_grad, v_grad], axis=-1)
            .reshape(-1, 3 * width)
            .astype(jnp.bfloat16)
        )
        sum_proj = sum_proj + cross_rows(normed, grad_proj)
        grad_normed = back_product(grad_proj, w_back[0])
        norm_pull_one = jax.vjp(layer_norm, flat, gain_one)[1]
        grad_in_part, grad_gain_one = norm_pull_one(grad_normed)
        grad_parts[micro_idx] = (grad_resid + grad_in_part).reshape(per_micro, blk_rows, width)
        gain_acc_one = gain_acc_one + grad_gain_one
        gain_acc_two = gain_acc_two + grad_gain_two
    red_ctx = (
        lax.psum_scatter(
            sum_proj.astype(jnp.bfloat16), "ctx", scatter_dimension=1, tiled=True
        ).astype(jnp.float32),
        lax.psum_scatter(
            sum_mix.astype(jnp.bfloat16), "ctx", scatter_dimension=1, tiled=True
        ).astype(jnp.float32),
        lax.psum_scatter(
            sum_expand.astype(jnp.bfloat16), "ctx", scatter_dimension=1, tiled=True
        ).astype(jnp.float32),
        lax.psum_scatter(
            sum_reduce.astype(jnp.bfloat16), "ctx", scatter_dimension=1, tiled=True
        ).astype(jnp.float32),
    )
    red_dp = (
        lax.psum_scatter(
            red_ctx[0].astype(jnp.bfloat16), "dp", scatter_dimension=0, tiled=True
        ).astype(jnp.float32),
        lax.psum_scatter(
            red_ctx[1].astype(jnp.bfloat16), "dp", scatter_dimension=0, tiled=True
        ).astype(jnp.float32),
        lax.psum_scatter(
            red_ctx[2].astype(jnp.bfloat16), "dp", scatter_dimension=0, tiled=True
        ).astype(jnp.float32),
        lax.psum_scatter(
            red_ctx[3].astype(jnp.bfloat16), "dp", scatter_dimension=0, tiled=True
        ).astype(jnp.float32),
    )
    gain_total = lax.psum(jnp.stack([gain_acc_one, gain_acc_two]), ("dp", "ctx"))
    shard_width = width // ctx_count
    own_gains = lax.dynamic_slice_in_dim(
        gain_total, lax.axis_index("ctx") * shard_width, shard_width, 1
    )
    output = jnp.concatenate(outputs, axis=0)
    grad_input = jnp.concatenate(grad_parts, axis=0)
    return (
        output,
        grad_input,
        own_gains[0],
        red_dp[0],
        red_dp[1],
        own_gains[1],
        red_dp[2],
        red_dp[3],
    )


def solution(mesh):
    row, split = P("dp", "ctx"), P("dp", "ctx", None)
    in_specs = (split, P("dp"), P("ctx"), row, row, P("ctx"), row, row, split)
    out_specs = (split, split, P("ctx"), row, row, P("ctx"), row, row)

    def run(block_input, prefix, ln1_gain, w_qkv, w_out, ln2_gain, w_up, w_down, grad_y):
        body = functools.partial(fused, NC) if fits(mesh, block_input, w_down) else local
        return jax.shard_map(body, mesh=mesh, in_specs=in_specs, out_specs=out_specs, check_vma=False)(
            block_input, prefix, ln1_gain, w_qkv, w_out, ln2_gain, w_up, w_down, grad_y
        )

    return run
```

```python
import functools
import math

import jax
import jax.numpy as jnp
from jax import lax
from jax.experimental import pallas as pl
from jax.experimental.pallas import tpu as pltpu
from jax.sharding import PartitionSpec as P

H = 8
MICRO = 2


EPS = 1e-05
NEG = -1e30

MESH = pl.DeviceIdType.MESH
F32 = jnp.float32
BF16 = jnp.bfloat16
NN = (((1,), (0,)), ((), ()))
NT = (((1,), (1,)), ((), ()))
TN = (((0,), (0,)), ((), ()))
GELU_A = math.sqrt(2.0 / math.pi)
GELU_B = 0.044715

NZ, NW, ND = 4, 2 * 2, 2
NC = NZ * NW
WORDS = 128
BQ = 2 * WORDS
GROWS = 16
PACK = 4
BA = PACK * WORDS
DH = 64


def dot(a, b, dims=NN):
    return lax.dot_general(a, b, dims, preferred_element_type=F32)


def sum_rows(v):
    return jnp.sum(v, axis=0, keepdims=True)


class Wires:
    def __init__(self, send, recv):
        self.send, self.recv, self.used, self.out, self.open = send, recv, 0, 0, []

    def slots(self, count):
        first = self.used
        self.used += count
        return first

    def group(self, ref, when=None):
        self.out += 1
        self.open.append((ref, self.out - 1, when))
        return self.out - 1

    def copy(self, src, dst, slot, device, out=0):
        return pltpu.make_async_remote_copy(
            src_ref=src,
            dst_ref=dst,
            send_sem=self.send.at[out],
            recv_sem=self.recv.at[slot],
            device_id=device,
            device_id_type=MESH,
        )

    def start(self, src, dst, slot, device, out=None):
        out = self.group(src) if out is None else out
        self.copy(src, dst, slot, device, out).start()

    def landed(self, dst, slot, device):
        self.copy(dst, dst, slot, device).wait_recv()

    def drain(self, device):
        for ref, out, when in self.open:
            sent = self.copy(ref, ref, 0, device, out)
            if when is None:
                sent.wait_send()
            else:
                pl.when(when)(sent.wait_send)


class Place:
    def __init__(self):
        self.me = lax.axis_index("ctx")
        self.d = lax.axis_index("dp")
        self.z = self.me // NW
        self.w = lax.rem(self.me, NW)
        x, y = lax.rem(self.w, 2), self.w // 2
        self.w1 = y * 2 + (1 - x)
        self.w2 = (1 - y) * 2 + x
        self.w3 = (1 - y) * 2 + (1 - x)
        self.other = 1 - self.d
        self.partner = {"dp": self.other}
        self.across_x = {"ctx": self.z * NW + self.w1}
        self.across_y = {"ctx": self.z * NW + self.w2}

    def up(self, step):
        return lax.rem(self.z + step, NZ)

    def down(self, step):
        return lax.rem(self.z - step + NZ, NZ)

    def along_z(self, step):
        return {"ctx": self.up(step) * NW + self.w}


class Gather:
    def __init__(self, wires, place, buf):
        self.wires, self.at, self.buf = wires, place, buf
        self.half = buf.shape[3] // 2
        self.sz = wires.slots(NZ - 1)
        self.sx, self.sy = wires.slots(NZ), wires.slots(NZ)
        self.se, self.sf = wires.slots(NZ), wires.slots(NZ)
        self.sp = wires.slots(1)
        row = buf.at[0, 0]
        z = place.z
        self.has_up, self.has_down = z < NZ - 1, z > 0
        self.o_up = wires.group(buf.at[0, 0, 0], self.has_up)
        self.o_down = wires.group(buf.at[0, 0, 0], self.has_down)
        self.oz = wires.group(buf.at[0, 0, pl.ds(0, NZ - 1)], self.has_up & self.has_down)
        first = jnp.where(z == 0, 3, 1)
        last = jnp.where(z == 0, 1, jnp.where(z == NZ - 1, 3, 2))
        self.order = (first, 6 - first - last, last)
        self.ox, self.oy = wires.group(row), wires.group(row)
        self.oe = wires.group(buf.at[0, 0, :, pl.ds(0, self.half)])
        self.of = wires.group(buf.at[0, 0, :, pl.ds(0, self.half)])
        self.op = wires.group(buf.at[0])

    def block(self, step, w):
        return self.buf.at[self.at.d, self.at.down(step), w]

    def top(self, ref):
        return ref.at[pl.ds(0, self.half)]

    def low(self, ref):
        return ref.at[pl.ds(self.half, self.half)]

    def send_z(self, src):
        p = self.at
        dst = self.block(0, p.w)

        @pl.when(self.has_up)
        def _():
            self.wires.start(src, dst, self.sz, p.along_z(1), self.o_up)

        @pl.when(self.has_down)
        def _():
            self.wires.start(src, dst, self.sz + NZ - 2, p.along_z(NZ - 1), self.o_down)

    def wait_z(self, step):
        self.wires.landed(self.block(step, self.at.w), self.sz + step - 1, self.at.along_z(step))

    def pass_z(self, step):
        p = self.at
        self.wait_z(step)
        b = self.block(step, p.w)

        @pl.when((p.z >= step) & self.has_up)
        def _():
            self.wires.start(b, b, self.sz + step, p.along_z(1), self.oz)

        @pl.when((p.z < step) & self.has_down)
        def _():
            self.wires.start(b, b, self.sz + step - 2, p.along_z(NZ - 1), self.oz)

    def send_plane(self, step):
        p, b = self.at, self.block(step, self.at.w)
        self.wires.start(b, b, self.sx + step, p.across_x, self.ox)
        self.wires.start(b, b, self.sy + step, p.across_y, self.oy)

    def send_core(self, group, step):
        p = self.at
        b = self.block(step, (p.w, p.w1, p.w2, p.w3)[group])
        self.wires.start(b, b, self.sp, p.partner, self.op)

    def relay_plane(self, step):
        p = self.at
        bx, by = self.block(step, p.w1), self.block(step, p.w2)
        self.wires.landed(bx, self.sx + step, p.across_x)
        self.wires.start(self.top(bx), self.top(bx), self.se + step, p.across_y, self.oe)
        self.send_core(1, step)
        self.wires.landed(by, self.sy + step, p.across_y)
        self.wires.start(self.low(by), self.low(by), self.sf + step, p.across_x, self.of)
        self.send_core(2, step)

    def relay_corner(self, step):
        p, b = self.at, self.block(step, self.at.w3)
        self.wires.landed(self.top(b), self.se + step, p.across_y)
        self.wires.landed(self.low(b), self.sf + step, p.across_x)
        self.send_core(3, step)

    def wait_core(self):
        self.wires.landed(self.buf.at[self.at.other], self.sp, self.at.partner)


class Scatter:
    def __init__(self, wires, place, buf, from_core, from_x, from_y, relay, column, from_z):
        self.wires, self.at, self.buf = wires, place, buf
        self.from_core, self.from_x, self.from_y = from_core, from_x, from_y
        self.relay, self.column, self.from_z = relay, column, from_z
        self.rows = buf.shape[3]
        self.half = self.rows // 2
        self.sp = wires.slots(1)
        self.sx, self.sy = wires.slots(3), wires.slots(3)
        self.sz = wires.slots(NZ - 1)

    def part(self, w, low):
        return self.buf.at[self.at.d, :, w, pl.ds(self.half if low else 0, self.half)]

    def send_core(self):
        p = self.at
        self.wires.start(self.buf.at[p.other], self.from_core, self.sp, p.partner)

    def add_core(self):
        p = self.at
        self.wires.landed(self.from_core, self.sp, p.partner)

        def add(k, carry):
            z, w = k // NW, lax.rem(k, NW)
            mine = self.buf[p.d, z, w].astype(F32)
            self.buf[p.d, z, w] = (mine + self.from_core[z, w].astype(F32)).astype(BF16)
            return carry

        lax.fori_loop(0, NC, add, 0)

    def send_plane(self):
        p = self.at
        for k, w in enumerate((p.w3, p.w1)):
            self.wires.start(self.part(w, False), self.from_x.at[k], self.sx + k, p.across_x)
        for k, w in enumerate((p.w3, p.w2)):
            self.wires.start(self.part(w, True), self.from_y.at[k], self.sy + k, p.across_y)

    def relay_corner(self):
        p, h = self.at, self.half
        self.wires.landed(self.from_x.at[0], self.sx, p.across_x)

        def add_top(z, carry):
            mine = self.buf[p.d, z, p.w2, pl.ds(0, h)].astype(F32)
            self.relay[0, z] = (mine + self.from_x[0, z].astype(F32)).astype(BF16)
            return carry

        lax.fori_loop(0, NZ, add_top, 0)
        self.wires.start(self.relay.at[0], self.from_y.at[2], self.sy + 2, p.across_y)
        self.wires.landed(self.from_y.at[0], self.sy, p.across_y)

        def add_low(z, carry):
            mine = self.buf[p.d, z, p.w1, pl.ds(h, h)].astype(F32)
            self.relay[1, z] = (mine + self.from_y[0, z].astype(F32)).astype(BF16)
            return carry

        lax.fori_loop(0, NZ, add_low, 0)
        self.wires.start(self.relay.at[1], self.from_x.at[2], self.sx + 2, p.across_x)

    def send_z(self):
        p, h = self.at, self.half
        self.wires.landed(self.from_x.at[1], self.sx + 1, p.across_x)
        self.wires.landed(self.from_y.at[1], self.sy + 1, p.across_y)
        self.wires.landed(self.from_y.at[2], self.sy + 2, p.across_y)
        self.wires.landed(self.from_x.at[2], self.sx + 2, p.across_x)

        def add(z, carry):
            top = self.buf[p.d, z, p.w, pl.ds(0, h)].astype(F32)
            top = top + self.from_x[1, z].astype(F32) + self.from_y[2, z].astype(F32)
            self.column[z, pl.ds(0, h)] = top.astype(BF16)
            low = self.buf[p.d, z, p.w, pl.ds(h, h)].astype(F32)
            low = low + self.from_y[1, z].astype(F32) + self.from_x[2, z].astype(F32)
            self.column[z, pl.ds(h, h)] = low.astype(BF16)
            return carry

        lax.fori_loop(0, NZ, add, 0)
        for step in range(1, NZ):
            self.wires.start(
                self.column.at[p.up(step)], self.from_z.at[step - 1], self.sz + step - 1, p.along_z(step)
            )

    def total(self):
        p = self.at
        for step in range(1, NZ):
            self.wires.landed(self.from_z.at[step - 1], self.sz + step - 1, p.along_z(step))
        acc = self.column[p.z].astype(F32)
        for step in range(1, NZ):
            acc = acc + self.from_z[step - 1].astype(F32)
        return acc


class Exchange:
    def __init__(self, wires, place, src, dst, inner=None):
        self.wires, self.at, self.src, self.dst = wires, place, src, dst
        self.inner = inner
        self.slot = wires.slots(1)
        self.rest = dst.at[pl.ds(0, NC - 1)] if inner is None else dst.at[pl.ds(0, NC - 1), inner]
        self.out = wires.group(self.rest)

    def view(self, ref, k):
        return ref.at[k] if self.inner is None else ref.at[k, self.inner]

    def send(self, offset):
        to = lax.rem(self.at.me + offset, NC)
        return self.wires.copy(
            self.view(self.src, to), self.view(self.dst, self.at.me), self.slot, {"ctx": to}, self.out
        )

    def send_to(self, chip):
        offset = lax.rem(chip - self.at.me + NC, NC)

        @pl.when(offset > 0)
        def _():
            self.send(offset).start()

        @pl.when(offset == 0)
        def _():
            self.keep()

    def keep(self):
        me = self.at.me
        if self.inner is None:
            self.dst[me] = self.src[me]
        else:
            self.dst[me, self.inner] = self.src[me, self.inner]

    def send_all(self):
        for offset in range(1, NC):
            self.send(offset).start()
        self.keep()

    def wait(self):
        self.wires.landed(self.rest, self.slot, self.at.partner)


def norm_stats(v):
    centred = v - jnp.mean(v, axis=0, keepdims=True)
    rstd = lax.rsqrt(jnp.mean(centred * centred, axis=0, keepdims=True) + EPS)
    return centred * rstd, rstd


def norm_back(grad, hat, rstd, gain):
    g = grad * gain
    return rstd * (g - jnp.mean(g, axis=0, keepdims=True) - hat * jnp.mean(g * hat, axis=0, keepdims=True))


def gelu_both(p):
    t = jnp.tanh(GELU_A * (p + GELU_B * p * p * p))
    half = 0.5 * (1.0 + t)
    slope = half + 0.5 * p * (1.0 - t * t) * (GELU_A * (1.0 + 3.0 * GELU_B * p * p))
    return p * half, slope


def step_kernel(
    prefix_ref, x_hbm, dy_hbm, gains_hbm, wq_hbm, wo_hbm, wu_hbm, wd_hbm,
    out_hbm, gx_hbm, gq_hbm, go_hbm, gu_hbm, gd_hbm, g1_hbm, g2_hbm,
    send_sem, recv_sem, own_sem,
    x_ref, dy_ref, WU, out_ref, gx_ref, gq_ref, gf_ref, GU, G1, G2,
    QG, FG, HAT1, RST1, NRM, DYT,
    QS, QR, KN, VN, PR, OT, LI, TOP, LAST, AS, AR, ATT,
    RES, HAT2, RST2, NRM2, ACT, SLOPE, DPRE, ACC, DRES, DAI,
    DS, DR, DEL, DQ, DQS, DPR, DPJ,
    GF, GFC, GFX, GFY, GFR, GFS, GFZ,
    GQ, GQC, GQX, GQY, GQR, GQS, GQZ,
    TS, TR,
):
    place = Place()
    wires = Wires(send_sem, recv_sem)
    me = place.me
    width = HAT1.shape[0]
    heads = width // DH
    half = width // 2
    qrows, frows = QG.shape[3], FG.shape[3]
    nq = PR.shape[0]
    pre_blocks = nq // 2
    orow = width // NC
    urow = ACT.shape[0] * BQ // NC
    nf = ACT.shape[0]

    gq = Gather(wires, place, QG)
    gf = Gather(wires, place, FG)
    qkv_x = Exchange(wires, place, QS, QR)
    att_x = Exchange(wires, place, AS, AR)
    datt_x = Exchange(wires, place, DS, DR)
    dkv_x = Exchange(wires, place, DQS, DPR, pl.ds(1, 2))
    dq_x = Exchange(wires, place, DQS, DPR, pl.ds(0, 1))
    sf = Scatter(wires, place, GF, GFC, GFX, GFY, GFR, GFS, GFZ)
    sq = Scatter(wires, place, GQ, GQC, GQX, GQY, GQR, GQS, GQZ)
    tot = wires.slots(6)

    barrier = pltpu.get_barrier_semaphore()
    for offset in range(1, NC):
        pl.semaphore_signal(barrier, inc=1, device_id={"ctx": lax.rem(me + offset, NC)}, device_id_type=MESH)
    pl.semaphore_signal(barrier, inc=1, device_id=place.partner, device_id_type=MESH)

    mine_q, mine_f = gq.block(0, place.w), gf.block(0, place.w)
    local = [0]

    def local_copy(src, dst):
        c = pltpu.make_async_copy(src, dst, own_sem.at[local[0]])
        local[0] += 1
        c.start()
        return c

    first = [
        local_copy(gains_hbm, mine_q.at[pl.ds(0, GROWS)]),
        local_copy(wq_hbm, mine_q.at[pl.ds(GROWS, qrows - GROWS)]),
    ]
    words_in = local_copy(x_hbm, x_ref)
    up_in = local_copy(wu_hbm, WU)
    rest = [local_copy(wo_hbm, mine_f.at[pl.ds(0, orow)])]
    for c in range(4):
        rest.append(
            local_copy(wd_hbm.at[:, pl.ds(c * 256, 256)], mine_f.at[pl.ds(orow + urow + c * orow, orow)])
        )
    dy_in = local_copy(dy_hbm, dy_ref)
    for c in first:
        c.wait()
    pl.semaphore_wait(barrier, NC)

    gq.send_z(gq.block(0, place.w))
    gq.send_plane(0)
    gq.send_core(0, 0)

    up_in.wait()
    FG[place.d, place.z, place.w, pl.ds(orow, urow), :] = WU[...].astype(F32).T.astype(BF16)
    words_in.wait()
    hat, rstd = norm_stats(x_ref[...].astype(F32).T)
    HAT1[...] = hat
    RST1[...] = rstd
    for c in rest:
        c.wait()
    gf.send_plane(0)
    gf.send_core(0, 0)

    for step in gq.order:
        gq.pass_z(step)
        gq.send_plane(step)
        gq.send_core(0, step)
    gf.send_z(gf.block(0, place.w))
    dy_in.wait()
    DYT[...] = dy_ref[...].astype(F32).T.astype(BF16)
    for step in (0, *gq.order):
        gq.relay_plane(step)
    gf.pass_z(gf.order[0])
    for step in (0, *gq.order):
        gq.relay_corner(step)
    gf.pass_z(gf.order[1])
    gq.wait_core()
    gf.pass_z(gf.order[2])

    gains = QG[0, :, :, pl.ds(0, GROWS), :].reshape(NC * GROWS, 256).astype(F32).T
    gain_one, gain_two = (
        jnp.concatenate([gains[r:r + orow, k * GROWS:k * GROWS + 1] for k in range(NC)], axis=0) for r in (0, 128)
    )
    NRM[...] = (HAT1[...] * gain_one).astype(BF16)
    wrows = qrows - GROWS
    for j in range(NZ):
        proj = sum(
            dot(QG[k, j, :, pl.ds(GROWS, wrows), :].reshape(NW * wrows, 256), NRM[k * half:(k + 1) * half])
            for k in range(ND)
        )
        for t in range(NW * wrows // DH):
            kind, head = divmod(j * (NW * wrows // DH) + t, heads)
            unit = proj[t * DH:(t + 1) * DH].astype(BF16)
            if kind == 0:
                unit = (unit.astype(F32) * DH ** (-0.5)).astype(BF16)
            for b in range(2):
                QS[b * heads + head, kind] = unit[:, b * WORDS:(b + 1) * WORDS]
    qkv_x.send_all()

    for step in gf.order:
        gf.send_plane(step)
        gf.send_core(0, step)

    gf.relay_plane(0)
    qkv_x.wait()
    prefix = prefix_ref[me // heads]

    def to_rows(c, carry):
        rows = pl.ds(pl.multiple_of(c * WORDS, WORDS), WORDS)
        KN[rows, :] = QR[c, 1].astype(F32).T.astype(BF16)
        VN[rows, :] = QR[c, 2].astype(F32).T.astype(BF16)
        return carry

    lax.fori_loop(0, NC, to_rows, 0)

    def pair(ref, b, kind=None):
        parts = [ref[PACK * b + k] if kind is None else ref[PACK * b + k, kind] for k in range(PACK)]
        return jnp.concatenate(parts, axis=1)

    def rows_of(b):
        return pl.ds(pl.multiple_of(b * BA, BA), BA)

    def attend(qb, carry):
        queries = pair(QR, qb, 0)

        def step(masked, kb, state):
            top, total, acc = state
            s = dot(KN[rows_of(kb), :], queries)
            if masked:
                key = kb * BA + lax.broadcasted_iota(jnp.int32, (BA, BA), 0)
                word = qb * BA + lax.broadcasted_iota(jnp.int32, (BA, BA), 1)
                s = jnp.where((key <= word) | (key < prefix), s, NEG)
            high = jnp.max(jnp.max(s.reshape(BA // 8, 8, BA), axis=0), axis=0, keepdims=True)
            new = jnp.maximum(top, high)
            TOP[qb, kb] = new
            scale = jnp.exp(top - new)
            p = jnp.exp(s - new)
            total = total * scale + jnp.sum(p.reshape(BA // 8, 8, BA), axis=0)
            p = p.astype(BF16)
            PR[qb, rows_of(kb), :] = p
            return new, total, acc * scale + dot(pair(QR, kb, 2), p)

        state = (jnp.full((1, BA), NEG, F32), jnp.zeros((8, BA), F32), jnp.zeros((DH, BA), F32))
        state = lax.fori_loop(0, qb, functools.partial(step, False), state)
        last = jnp.maximum(qb + 1, pre_blocks)
        top, total, acc = lax.fori_loop(qb, last, functools.partial(step, True), state)
        inv = 1.0 / jnp.sum(total, axis=0, keepdims=True)
        out = acc * inv
        OT[qb] = out
        LI[qb] = inv
        LAST[qb] = top
        out = out.astype(BF16)
        for k in range(PACK):
            AS[PACK * qb + k] = out[:, k * WORDS:(k + 1) * WORDS]
            att_x.send_to(PACK * qb + k)
        return carry

    lax.fori_loop(0, 2, attend, 0)
    gf.relay_plane(gf.order[0])
    gf.relay_plane(gf.order[1])
    gf.relay_plane(gf.order[2])
    lax.fori_loop(2, 4, attend, 0)
    gf.relay_corner(0)
    gf.relay_corner(gf.order[0])
    gf.relay_corner(gf.order[1])
    gf.relay_corner(gf.order[2])

    att_x.wait()
    gf.wait_core()
    for h in range(heads):
        ATT[h * DH:(h + 1) * DH] = jnp.concatenate([AR[h], AR[heads + h]], axis=1)

    def w_out(k):
        return FG[k, :, :, pl.ds(0, orow), :].reshape(width, 256)

    def w_up(k, c):
        return FG[k, c // 2, pl.ds(2 * (c % 2), 2), pl.ds(orow, urow), :].reshape(BQ, 256)

    def w_down(c):
        rows = orow + urow + (c % 4) * orow
        return FG[c // 4, :, :, pl.ds(rows, orow), :].reshape(width, 256)

    mixed = sum(dot(w_out(k), ATT[k * half:(k + 1) * half]) for k in range(ND))
    res = x_ref[...].astype(F32).T + mixed
    RES[...] = res
    hat2, rstd2 = norm_stats(res)
    HAT2[...] = hat2
    RST2[...] = rstd2
    NRM2[...] = (hat2 * gain_two).astype(BF16)

    for c in range(nf):
        pre = sum(dot(w_up(k, c), NRM2[k * half:(k + 1) * half]) for k in range(ND))
        act, slope = gelu_both(pre)
        ACT[c] = act.astype(BF16)
        SLOPE[c] = slope
    ACC[...] = jnp.zeros_like(ACC)
    for c in range(nf):
        dact = dot(w_down(c), DYT[...], TN)
        dpre = (dact * SLOPE[c]).astype(BF16)
        DPRE[c] = dpre
        for k in range(ND):
            ACC[k * half:(k + 1) * half] += dot(w_up(k, c), dpre, TN)
    dn2 = ACC[...]
    dres = DYT[...].astype(F32) + norm_back(dn2, HAT2[...], RST2[...], gain_two)
    DRES[...] = dres
    DAI[...] = dres.astype(BF16)
    ones = jnp.ones((8, 2 * WORDS), F32)
    row_two = lax.dot_general(
        ones, dn2 * HAT2[...], NT, precision=lax.Precision.HIGHEST, preferred_element_type=F32
    )
    for k in range(ND):
        datt = dot(w_out(k), DAI[...], TN).astype(BF16)
        for t in range(half // DH):
            h = k * (half // DH) + t
            for b in range(2):
                DS[b * heads + h] = datt[t * DH:(t + 1) * DH, b * WORDS:(b + 1) * WORDS]
    datt_x.send_all()

    for c in range(nf):
        rows = orow + urow + (c % 4) * orow
        GF[c // 4, :, :, pl.ds(rows, orow), :] = dot(DYT[...], ACT[c], NT).astype(BF16).reshape(NZ, NW, orow, 256)
        for k in range(ND):
            up = dot(DPRE[c], NRM2[k * half:(k + 1) * half], NT).astype(BF16)
            GF[k, c // 2, pl.ds(2 * (c % 2), 2), pl.ds(orow, urow), :] = up.reshape(2, urow, 256)
    for k in range(ND):
        mix = dot(DAI[...], ATT[k * half:(k + 1) * half], NT).astype(BF16)
        GF[k, :, :, pl.ds(0, orow), :] = mix.reshape(NZ, NW, orow, 256)
    sf.send_core()
    for r in range(2):
        acc = RES[r * half:(r + 1) * half]
        for c in range(nf):
            rows = orow + urow + (c % 4) * orow
            w = FG[c // 4, pl.ds(2 * r, 2), :, pl.ds(rows, orow), :].reshape(half, 256)
            acc = acc + dot(w, ACT[c])
        out_ref[:, r * half:(r + 1) * half] = acc.T.astype(BF16)
    outs = [local_copy(out_ref, out_hbm)]

    datt_x.wait()

    def ready(qb, carry):
        DEL[qb] = sum_rows(pair(DR, qb).astype(F32) * OT[qb])
        DQ[qb] = jnp.zeros((DH, BA), F32)
        return carry

    lax.fori_loop(0, nq, ready, 0)

    def put(ref, b, kind, val):
        val = val.astype(BF16)
        for k in range(PACK):
            ref[PACK * b + k, kind] = val[:, k * WORDS:(k + 1) * WORDS]

    def send_dq(qb):
        put(DQS, qb, 0, DQ[qb] * DH ** (-0.5))
        for k in range(PACK):
            dq_x.send_to(PACK * qb + k)

    def attend_back(kb, carry, finish=False):
        keys, vals, keys_t = KN[rows_of(kb), :], VN[rows_of(kb), :], pair(QR, kb, 1)
        first = jnp.where(kb < pre_blocks, 0, kb)

        def one(qb, state):
            dk, dv = state
            norm = jnp.exp(TOP[qb, kb] - LAST[qb]) * LI[qb]
            datt = (pair(DR, qb).astype(F32) * norm).astype(BF16)
            dp = dot(vals, datt)
            p = PR[qb, rows_of(kb), :]
            ds = (p.astype(F32) * (dp - DEL[qb] * norm)).astype(BF16)
            DQ[qb] += dot(keys_t, ds)
            if finish:
                send_dq(qb)
            return dk + dot(pair(QR, qb, 0), ds, NT), dv + dot(datt, p, NT)

        zero = jnp.zeros((DH, BA), F32)
        dk, dv = lax.fori_loop(first, nq, one, (zero, zero))
        put(DQS, kb, 1, dk)
        put(DQS, kb, 2, dv)
        for k in range(PACK):
            dkv_x.send_to(PACK * kb + k)
        return carry

    def back_from_last(i, carry):
        return attend_back(nq - 1 - i, carry)

    lax.fori_loop(0, 1, back_from_last, 0)
    sf.add_core()
    sf.send_plane()
    lax.fori_loop(1, nq - 1, back_from_last, 0)
    attend_back(0, 0, True)
    sf.relay_corner()
    dq_x.wait()
    dkv_x.wait()

    for kind in range(3):
        for h in range(heads):
            r = (kind * heads + h) * DH
            DPJ[r:r + DH] = jnp.concatenate([DPR[h, kind], DPR[heads + h, kind]], axis=1)
    blk = NW * wrows
    for j in range(NZ):
        for k in range(ND):
            g = dot(DPJ[j * blk:(j + 1) * blk], NRM[k * half:(k + 1) * half], NT)
            GQ[k, j] = g.astype(BF16).reshape(NW, wrows, 256)
    sq.send_core()
    sf.send_z()
    ACC[...] = jnp.zeros_like(ACC)
    for k in range(ND):
        for j in range(NZ):
            w = QG[k, j, :, pl.ds(GROWS, wrows), :].reshape(blk, 256)
            ACC[k * half:(k + 1) * half] += dot(w, DPJ[j * blk:(j + 1) * blk], TN)
    dn1 = ACC[...]
    gx_ref[...] = (DRES[...] + norm_back(dn1, HAT1[...], RST1[...], gain_one)).T
    outs.append(local_copy(gx_ref, gx_hbm))
    row_one = lax.dot_general(
        ones, dn1 * HAT1[...], NT, precision=lax.Precision.HIGHEST, preferred_element_type=F32
    )

    TS[0] = jnp.where(lax.broadcasted_iota(jnp.int32, (8, width), 0) == 0, row_one, row_two)
    wires.start(TS.at[0], TR.at[0], tot, place.partner)
    sq.add_core()
    sq.send_plane()
    wires.landed(TR.at[0], tot, place.partner)
    TS[1] = TS[0] + TR[0]
    wires.start(TS.at[1], TR.at[1], tot + 1, place.across_x)
    sq.relay_corner()
    wires.landed(TR.at[1], tot + 1, place.across_x)
    TS[2] = TS[1] + TR[1]
    wires.start(TS.at[2], TR.at[2], tot + 2, place.across_y)
    gf_ref[...] = sf.total()
    GU[...] = gf_ref[pl.ds(orow, urow), :].T
    outs.append(local_copy(gf_ref.at[pl.ds(0, orow)], go_hbm))
    outs.append(local_copy(GU, gu_hbm))
    for c in range(4):
        outs.append(local_copy(gf_ref.at[pl.ds(orow + urow + c * orow, orow)], gd_hbm.at[:, pl.ds(c * 256, 256)]))
    sq.send_z()
    wires.landed(TR.at[2], tot + 2, place.across_y)
    TS[3] = TS[2] + TR[2]
    for step in range(1, NZ):
        wires.start(TS.at[3], TR.at[2 + step], tot + 2 + step, place.along_z(step))
    gq_ref[...] = sq.total()
    outs.append(local_copy(gq_ref, gq_hbm))
    for step in range(1, NZ):
        wires.landed(TR.at[2 + step], tot + 2 + step, place.along_z(step))
    picked = lax.broadcasted_iota(jnp.int32, (width, 128), 0) == me * orow + lax.broadcasted_iota(
        jnp.int32, (width, 128), 1
    )
    own = lax.dot_general(
        TS[3] + TR[3] + TR[4] + TR[5], picked.astype(F32), NN,
        precision=lax.Precision.HIGHEST, preferred_element_type=F32,
    )
    G1[...] = own[0:1, 0:orow]
    G2[...] = own[1:2, 0:orow]
    outs.append(local_copy(G1, g1_hbm))
    outs.append(local_copy(G2, g2_hbm))

    assert (wires.out, wires.used, local[0]) == (N_SEND, N_RECV, N_OWN), (wires.out, wires.used, local[0])
    wires.drain(place.partner)
    for c in outs:
        c.wait()


def fused(ctx_count, block_input, prefix, ln1_gain, w_qkv, w_out, ln2_gain, w_up, w_down, grad_y):
    width = block_input.shape[2]
    ff = w_down.shape[0] * ND
    words = 2 * WORDS
    nq = NC * WORDS // BA
    nf = ff // BQ
    orow, qrow, urow = width // NC, 3 * width // NC, ff // NC
    qrows, frows = GROWS + qrow, orow + urow + 4 * orow

    gains = jnp.concatenate([jnp.pad(g, (0, 128 - orow)) for g in (ln1_gain, ln2_gain)])
    gains = jnp.broadcast_to(gains[None], (GROWS, 256))
    x = block_input.reshape(words, width)
    dy = grad_y.reshape(words, width)

    def vm(*shape, dtype=BF16):
        return pltpu.VMEM(shape, dtype)

    def scatter_bufs(rows):
        return [
            vm(ND, NZ, NW, rows, 256),
            vm(NZ, NW, rows, 256),
            vm(3, NZ, rows // 2, 256),
            vm(3, NZ, rows // 2, 256),
            vm(2, NZ, rows // 2, 256),
            vm(NZ, rows, 256),
            vm(NZ - 1, rows, 256),
        ]

    length = NC * WORDS
    msgs = 512
    vmem = pl.BlockSpec(memory_space=pltpu.VMEM)
    hbm = pl.BlockSpec(memory_space=pl.ANY)
    out, gx, gq, g_out, g_up, g_down, g_one, g_two = pl.pallas_call(
        step_kernel,
        out_shape=(
            jax.ShapeDtypeStruct((words, width), BF16),
            jax.ShapeDtypeStruct((words, width), F32),
            jax.ShapeDtypeStruct((qrow, 256), F32),
            jax.ShapeDtypeStruct((orow, 256), F32),
            jax.ShapeDtypeStruct((256, urow), F32),
            jax.ShapeDtypeStruct((orow, 4 * 256), F32),
            jax.ShapeDtypeStruct((1, orow), F32),
            jax.ShapeDtypeStruct((1, orow), F32),
        ),
        in_specs=[pl.BlockSpec(memory_space=pltpu.SMEM)] + [hbm] * 7,
        out_specs=(hbm,) * 8,
        scratch_shapes=[
            pltpu.SemaphoreType.DMA((N_SEND,)),
            pltpu.SemaphoreType.DMA((N_RECV,)),
            pltpu.SemaphoreType.DMA((N_OWN,)),
            vm(words, width),
            vm(words, width),
            vm(256, urow),
            vm(words, width),
            vm(words, width, dtype=F32),
            vm(qrow, 256, dtype=F32),
            vm(frows, 256, dtype=F32),
            vm(256, urow, dtype=F32),
            vm(1, orow, dtype=F32),
            vm(1, orow, dtype=F32),
            vm(ND, NZ, NW, qrows, 256),
            vm(ND, NZ, NW, frows, 256),
            vm(width, words, dtype=F32),
            vm(1, words, dtype=F32),
            vm(width, words),
            vm(width, words),
            vm(NC, 3, DH, WORDS),
            vm(NC, 3, DH, WORDS),
            vm(length, DH),
            vm(length, DH),
            vm(nq, length, BA),
            vm(nq, DH, BA, dtype=F32),
            vm(nq, 1, BA, dtype=F32),
            vm(nq, nq, 1, BA, dtype=F32),
            vm(nq, 1, BA, dtype=F32),
            vm(NC, DH, WORDS),
            vm(NC, DH, WORDS),
            vm(width, words),
            vm(width, words, dtype=F32),
            vm(width, words, dtype=F32),
            vm(1, words, dtype=F32),
            vm(width, words),
            vm(nf, BQ, words),
            vm(nf, BQ, words, dtype=F32),
            vm(nf, BQ, words),
            vm(width, words, dtype=F32),
            vm(width, words, dtype=F32),
            vm(width, words),
            vm(NC, DH, WORDS),
            vm(NC, DH, WORDS),
            vm(nq, 1, BA, dtype=F32),
            vm(nq, DH, BA, dtype=F32),
            vm(NC, 3, DH, WORDS),
            vm(NC, 3, DH, WORDS),
            vm(3 * width, words),
            *scatter_bufs(frows),
            *scatter_bufs(qrow),
            vm(4, 8, width, dtype=F32),
            vm(6, 8, width, dtype=F32),
        ],
        compiler_params=pltpu.CompilerParams(
            collective_id=0, has_side_effects=True, vmem_limit_bytes=66 * 1024 * 1024 - 2 ** 21
        ),
        name="block_step",
    )(prefix, x, dy, gains, w_qkv.T, w_out.T, w_up, w_down.T)

    return (
        out.reshape(block_input.shape),
        gx.reshape(block_input.shape),
        g_one.reshape(ln1_gain.shape),
        gq.T,
        g_out.T,
        g_two.reshape(ln2_gain.shape),
        g_up,
        g_down.T,
    )


N_SEND, N_RECV, N_OWN = 47, 71, 21


def fits(mesh, block_input, w_down):
    seqs, length, width = block_input.shape
    return (
        mesh.shape["ctx"] == NC
        and mesh.shape["dp"] == ND
        and seqs == 2 * ND
        and length == NC * WORDS
        and width == H * DH
        and 2 * H == NC
        and w_down.shape[0] == 4 * width
    )


def layer_norm(values, gain):
    centred = values - jnp.mean(values, axis=-1, keepdims=True)
    spread = jnp.mean(centred * centred, axis=-1, keepdims=True)
    return centred * lax.rsqrt(spread + EPS) * gain


def row_product(left, right):
    return jnp.dot(left, right, preferred_element_type=jnp.float32)


def cross_rows(left, right):
    return lax.dot_general(
        left, right, (((0,), (0,)), ((), ())), preferred_element_type=jnp.float32
    )


def back_product(left, right):
    return lax.dot_general(
        left, right, (((1,), (1,)), ((), ())), preferred_element_type=jnp.float32
    )


def visible_mask(query_first, query_count, key_first, key_count, prefixes):
    query_pos = query_first + jnp.arange(query_count, dtype=jnp.int32)
    key_pos = key_first + jnp.arange(key_count, dtype=jnp.int32)
    causal = key_pos[None, :] <= query_pos[:, None]
    before = key_pos[None, None, :] < prefixes[:, None, None]
    return (causal[None] | before)[:, None]


def attend_forward(queries, keys_own, values_own, prefixes, my_first, scale):
    batch, rows, heads, head_dim = queries.shape
    key_first = jnp.int32(0)
    key_rows = lax.all_gather(keys_own, "ctx", axis=1, tiled=True)
    value_rows = lax.all_gather(values_own, "ctx", axis=1, tiled=True)
    count = key_rows.shape[1]
    top = jnp.full((batch, heads, rows), NEG, jnp.float32)
    summed = jnp.zeros((batch, rows, heads, head_dim), jnp.float32)
    keys_h = key_rows.reshape(batch, count, heads, head_dim)
    values_h = value_rows.reshape(batch, count, heads, head_dim)
    scores = (
        jnp.einsum("bqhd,bkhd->bhqk", queries, keys_h, preferred_element_type=jnp.float32) * scale
    )
    scores = jnp.where(visible_mask(my_first, rows, key_first, count, prefixes), scores, NEG)
    new_top = jnp.maximum(top, jnp.max(scores, axis=-1))
    factor = jnp.exp(top - new_top)
    probs = jnp.exp(scores - new_top[..., None])
    total = jnp.sum(probs, axis=-1)
    summed = summed * jnp.swapaxes(factor, 1, 2)[..., None] + jnp.einsum(
        "bhqk,bkhd->bqhd", probs.astype(jnp.bfloat16), values_h, preferred_element_type=jnp.float32
    )
    top, total, summed = (new_top, total, summed)
    attended = summed / jnp.swapaxes(total, 1, 2)[..., None]
    log_sum = top + jnp.log(total)
    return (attended.reshape(batch, rows, heads * head_dim), log_sum)


def attend_backward(
    queries, keys_own, values_own, attended, grad_att, log_sum, prefixes, my_first, scale
):
    batch, rows, heads, head_dim = queries.shape
    width = heads * head_dim
    keys_full, values_full = (
        lax.all_gather(keys_own, "ctx", axis=1, tiled=True),
        lax.all_gather(values_own, "ctx", axis=1, tiled=True),
    )
    length = keys_full.shape[1]
    key_block = math.gcd(length, 512)
    grad_h = grad_att.reshape(batch, rows, heads, head_dim)
    delta = jnp.swapaxes(
        jnp.sum(
            grad_h.astype(jnp.float32) * attended.reshape(batch, rows, heads, head_dim), axis=-1
        ),
        1,
        2,
    )

    def one_block(counter, carried):
        key_first = counter * key_block
        q_sum, k_sum, v_sum = carried
        keys_h = lax.dynamic_slice_in_dim(keys_full, key_first, key_block, 1).reshape(
            batch, key_block, heads, head_dim
        )
        values_h = lax.dynamic_slice_in_dim(values_full, key_first, key_block, 1).reshape(
            batch, key_block, heads, head_dim
        )
        scores = (
            jnp.einsum("bqhd,bkhd->bhqk", queries, keys_h, preferred_element_type=jnp.float32)
            * scale
        )
        scores = jnp.where(
            visible_mask(my_first, rows, key_first, key_block, prefixes), scores, NEG
        )
        probs = jnp.exp(scores - log_sum[..., None])
        grad_probs = jnp.einsum(
            "bqhd,bkhd->bhqk", grad_h, values_h, preferred_element_type=jnp.float32
        )
        grad_scores = (probs * (grad_probs - delta[..., None])).astype(jnp.bfloat16)
        q_sum = (
            q_sum
            + jnp.einsum("bhqk,bkhd->bqhd", grad_scores, keys_h, preferred_element_type=jnp.float32)
            * scale
        )
        v_part = jnp.einsum(
            "bhqk,bqhd->bkhd",
            probs.astype(jnp.bfloat16),
            grad_h,
            preferred_element_type=jnp.float32,
        )
        k_part = (
            jnp.einsum("bhqk,bqhd->bkhd", grad_scores, queries, preferred_element_type=jnp.float32)
            * scale
        )
        k_sum = lax.dynamic_update_slice_in_dim(
            k_sum, k_part.reshape(batch, key_block, width), key_first, 1
        )
        v_sum = lax.dynamic_update_slice_in_dim(
            v_sum, v_part.reshape(batch, key_block, width), key_first, 1
        )
        return (q_sum, k_sum, v_sum)

    initial = (
        jnp.zeros((batch, rows, heads, head_dim), jnp.float32),
        jnp.zeros((batch, length, width), jnp.float32),
        jnp.zeros((batch, length, width), jnp.float32),
    )
    q_sum, k_sum, v_sum = lax.fori_loop(0, length // key_block, one_block, initial)
    k_own, v_own = (
        lax.psum_scatter(k_sum.astype(jnp.bfloat16), "ctx", scatter_dimension=1, tiled=True).astype(
            jnp.float32
        ),
        lax.psum_scatter(v_sum.astype(jnp.bfloat16), "ctx", scatter_dimension=1, tiled=True).astype(
            jnp.float32
        ),
    )
    return (q_sum.reshape(batch, rows, width), k_own, v_own)


def local(block_input, prefix, ln1_gain, w_qkv, w_out, ln2_gain, w_up, w_down, grad_y):
    ctx_count = lax.axis_size("ctx")
    blk_rows = block_input.shape[1]
    width = block_input.shape[2]
    head_dim = width // H
    scale = head_dim ** (-0.5)
    my_first = lax.axis_index("ctx") * blk_rows
    per_micro = block_input.shape[0] // MICRO
    by_ctx = (
        lax.all_gather(w_qkv, "ctx", axis=1, tiled=True),
        lax.all_gather(w_out, "ctx", axis=1, tiled=True),
        lax.all_gather(w_up, "ctx", axis=1, tiled=True),
        lax.all_gather(w_down, "ctx", axis=1, tiled=True),
        lax.all_gather(ln1_gain, "ctx", axis=0, tiled=True),
        lax.all_gather(ln2_gain, "ctx", axis=0, tiled=True),
    )
    full_fwd = (
        lax.all_gather(by_ctx[0], "dp", axis=0, tiled=True),
        lax.all_gather(by_ctx[1], "dp", axis=0, tiled=True),
        lax.all_gather(by_ctx[2], "dp", axis=0, tiled=True),
        lax.all_gather(by_ctx[3], "dp", axis=0, tiled=True),
    )
    gain_one = by_ctx[4].astype(jnp.float32)
    gain_two = by_ctx[5].astype(jnp.float32)
    saved = []
    outputs = []
    for micro_idx in range(MICRO):
        lower_row = micro_idx * per_micro
        inputs = block_input[lower_row : lower_row + per_micro].astype(jnp.float32)
        prefixes = prefix[lower_row : lower_row + per_micro]
        flat = inputs.reshape(-1, width)
        normed = layer_norm(flat, gain_one).astype(jnp.bfloat16)
        projected = (
            row_product(normed, full_fwd[0])
            .astype(jnp.bfloat16)
            .reshape(per_micro, blk_rows, 3 * width)
        )
        queries = projected[..., :width].reshape(per_micro, blk_rows, H, head_dim)
        keys_own = projected[..., width : 2 * width]
        values_own = projected[..., 2 * width :]
        attended, log_sum = attend_forward(queries, keys_own, values_own, prefixes, my_first, scale)
        mixed_in = attended.reshape(-1, width).astype(jnp.bfloat16)
        resid = flat + row_product(mixed_in, full_fwd[1])
        normed_two = layer_norm(resid, gain_two).astype(jnp.bfloat16)
        hidden_pre = row_product(normed_two, full_fwd[2])
        activated = jax.nn.gelu(hidden_pre).astype(jnp.bfloat16)
        result = resid + row_product(activated, full_fwd[3])
        outputs.append(result.astype(jnp.bfloat16).reshape(per_micro, blk_rows, width))
        saved.append(
            (
                flat,
                normed,
                queries,
                keys_own,
                values_own,
                attended,
                log_sum,
                mixed_in,
                resid,
                normed_two,
                hidden_pre,
                activated,
                prefixes,
            )
        )
    back_ctx = (
        lax.all_gather(w_qkv, "ctx", axis=1, tiled=True),
        lax.all_gather(w_out, "ctx", axis=1, tiled=True),
        lax.all_gather(w_up, "ctx", axis=1, tiled=True),
        lax.all_gather(w_down, "ctx", axis=1, tiled=True),
    )
    w_back = (
        lax.all_gather(back_ctx[0], "dp", axis=0, tiled=True),
        lax.all_gather(back_ctx[1], "dp", axis=0, tiled=True),
        lax.all_gather(back_ctx[2], "dp", axis=0, tiled=True),
        lax.all_gather(back_ctx[3], "dp", axis=0, tiled=True),
    )
    sum_proj = jnp.zeros(w_back[0].shape, jnp.float32)
    sum_mix = jnp.zeros(w_back[1].shape, jnp.float32)
    sum_expand = jnp.zeros(w_back[2].shape, jnp.float32)
    sum_reduce = jnp.zeros(w_back[3].shape, jnp.float32)
    gain_acc_one = jnp.zeros((width,), jnp.float32)
    gain_acc_two = jnp.zeros((width,), jnp.float32)
    grad_parts = [None] * MICRO
    for micro_idx in reversed(range(MICRO)):
        (
            flat,
            normed,
            queries,
            keys_own,
            values_own,
            attended,
            log_sum,
            mixed_in,
            resid,
            normed_two,
            hidden_pre,
            activated,
            prefixes,
        ) = saved[micro_idx]
        lower_row = micro_idx * per_micro
        cot_b = grad_y[lower_row : lower_row + per_micro].reshape(-1, width)
        cotangent = cot_b.astype(jnp.float32)
        sum_reduce = sum_reduce + cross_rows(activated, cot_b)
        grad_act = back_product(cot_b, w_back[3])
        gelu_pull = jax.vjp(jax.nn.gelu, hidden_pre)[1]
        grad_hidden = gelu_pull(grad_act)[0].astype(jnp.bfloat16)
        sum_expand = sum_expand + cross_rows(normed_two, grad_hidden)
        grad_normed_two = back_product(grad_hidden, w_back[2])
        norm_pull_two = jax.vjp(layer_norm, resid, gain_two)[1]
        grad_resid_part, grad_gain_two = norm_pull_two(grad_normed_two)
        grad_resid = cotangent + grad_resid_part
        grad_mix_b = grad_resid.astype(jnp.bfloat16)
        sum_mix = sum_mix + cross_rows(mixed_in, grad_mix_b)
        grad_attended = back_product(grad_mix_b, w_back[1]).astype(jnp.bfloat16)
        q_grad, k_grad, v_grad = attend_backward(
            queries,
            keys_own,
            values_own,
            attended,
            grad_attended.reshape(per_micro, blk_rows, width),
            log_sum,
            prefixes,
            my_first,
            scale,
        )
        grad_proj = (
            jnp.concatenate([q_grad, k_grad, v_grad], axis=-1)
            .reshape(-1, 3 * width)
            .astype(jnp.bfloat16)
        )
        sum_proj = sum_proj + cross_rows(normed, grad_proj)
        grad_normed = back_product(grad_proj, w_back[0])
        norm_pull_one = jax.vjp(layer_norm, flat, gain_one)[1]
        grad_in_part, grad_gain_one = norm_pull_one(grad_normed)
        grad_parts[micro_idx] = (grad_resid + grad_in_part).reshape(per_micro, blk_rows, width)
        gain_acc_one = gain_acc_one + grad_gain_one
        gain_acc_two = gain_acc_two + grad_gain_two
    red_ctx = (
        lax.psum_scatter(
            sum_proj.astype(jnp.bfloat16), "ctx", scatter_dimension=1, tiled=True
        ).astype(jnp.float32),
        lax.psum_scatter(
            sum_mix.astype(jnp.bfloat16), "ctx", scatter_dimension=1, tiled=True
        ).astype(jnp.float32),
        lax.psum_scatter(
            sum_expand.astype(jnp.bfloat16), "ctx", scatter_dimension=1, tiled=True
        ).astype(jnp.float32),
        lax.psum_scatter(
            sum_reduce.astype(jnp.bfloat16), "ctx", scatter_dimension=1, tiled=True
        ).astype(jnp.float32),
    )
    red_dp = (
        lax.psum_scatter(
            red_ctx[0].astype(jnp.bfloat16), "dp", scatter_dimension=0, tiled=True
        ).astype(jnp.float32),
        lax.psum_scatter(
            red_ctx[1].astype(jnp.bfloat16), "dp", scatter_dimension=0, tiled=True
        ).astype(jnp.float32),
        lax.psum_scatter(
            red_ctx[2].astype(jnp.bfloat16), "dp", scatter_dimension=0, tiled=True
        ).astype(jnp.float32),
        lax.psum_scatter(
            red_ctx[3].astype(jnp.bfloat16), "dp", scatter_dimension=0, tiled=True
        ).astype(jnp.float32),
    )
    gain_total = lax.psum(jnp.stack([gain_acc_one, gain_acc_two]), ("dp", "ctx"))
    shard_width = width // ctx_count
    own_gains = lax.dynamic_slice_in_dim(
        gain_total, lax.axis_index("ctx") * shard_width, shard_width, 1
    )
    output = jnp.concatenate(outputs, axis=0)
    grad_input = jnp.concatenate(grad_parts, axis=0)
    return (
        output,
        grad_input,
        own_gains[0],
        red_dp[0],
        red_dp[1],
        own_gains[1],
        red_dp[2],
        red_dp[3],
    )


def solution(mesh):
    row, split = P("dp", "ctx"), P("dp", "ctx", None)
    in_specs = (split, P("dp"), P("ctx"), row, row, P("ctx"), row, row, split)
    out_specs = (split, split, P("ctx"), row, row, P("ctx"), row, row)

    def run(block_input, prefix, ln1_gain, w_qkv, w_out, ln2_gain, w_up, w_down, grad_y):
        body = functools.partial(fused, NC) if fits(mesh, block_input, w_down) else local
        return jax.shard_map(body, mesh=mesh, in_specs=in_specs, out_specs=out_specs, check_vma=False)(
            block_input, prefix, ln1_gain, w_qkv, w_out, ln2_gain, w_up, w_down, grad_y
        )

    return run
```

```python
import functools
import math

import jax
import jax.numpy as jnp
from jax import lax
from jax.experimental import pallas as pl
from jax.experimental.pallas import tpu as pltpu
from jax.sharding import PartitionSpec as P

H = 8
MICRO = 2


EPS = 1e-05
NEG = -1e30

MESH = pl.DeviceIdType.MESH
F32 = jnp.float32
BF16 = jnp.bfloat16
NN = (((1,), (0,)), ((), ()))
NT = (((1,), (1,)), ((), ()))
TN = (((0,), (0,)), ((), ()))
GELU_A = math.sqrt(2.0 / math.pi)
GELU_B = 0.044715

NZ, NW, ND = 4, 2 * 2, 2
NC = NZ * NW
WORDS = 128
BQ = 2 * WORDS
GROWS = 16
PACK = 4
BA = PACK * WORDS
DH = 64


def dot(a, b, dims=NN):
    return lax.dot_general(a, b, dims, preferred_element_type=F32)


def sum_rows(v):
    return jnp.sum(v, axis=0, keepdims=True)


class Wires:
    def __init__(self, send, recv):
        self.send, self.recv, self.used, self.out, self.open = send, recv, 0, 0, []

    def slots(self, count):
        first = self.used
        self.used += count
        return first

    def group(self, ref, when=None):
        self.out += 1
        self.open.append((ref, self.out - 1, when))
        return self.out - 1

    def copy(self, src, dst, slot, device, out=0):
        return pltpu.make_async_remote_copy(
            src_ref=src,
            dst_ref=dst,
            send_sem=self.send.at[out],
            recv_sem=self.recv.at[slot],
            device_id=device,
            device_id_type=MESH,
        )

    def start(self, src, dst, slot, device, out=None):
        out = self.group(src) if out is None else out
        self.copy(src, dst, slot, device, out).start()

    def landed(self, dst, slot, device):
        self.copy(dst, dst, slot, device).wait_recv()

    def drain(self, device):
        for ref, out, when in self.open:
            sent = self.copy(ref, ref, 0, device, out)
            if when is None:
                sent.wait_send()
            else:
                pl.when(when)(sent.wait_send)


class Place:
    def __init__(self):
        self.me = lax.axis_index("ctx")
        self.d = lax.axis_index("dp")
        self.z = self.me // NW
        self.w = lax.rem(self.me, NW)
        x, y = lax.rem(self.w, 2), self.w // 2
        self.w1 = y * 2 + (1 - x)
        self.w2 = (1 - y) * 2 + x
        self.w3 = (1 - y) * 2 + (1 - x)
        self.other = 1 - self.d
        self.partner = {"dp": self.other}
        self.across_x = {"ctx": self.z * NW + self.w1}
        self.across_y = {"ctx": self.z * NW + self.w2}

    def up(self, step):
        return lax.rem(self.z + step, NZ)

    def down(self, step):
        return lax.rem(self.z - step + NZ, NZ)

    def along_z(self, step):
        return {"ctx": self.up(step) * NW + self.w}


class Gather:
    def __init__(self, wires, place, buf):
        self.wires, self.at, self.buf = wires, place, buf
        self.half = buf.shape[3] // 2
        self.sz = wires.slots(NZ - 1)
        self.sx, self.sy = wires.slots(NZ), wires.slots(NZ)
        self.se, self.sf = wires.slots(NZ), wires.slots(NZ)
        self.sp = wires.slots(1)
        row = buf.at[0, 0]
        z = place.z
        self.has_up, self.has_down = z < NZ - 1, z > 0
        self.o_up = wires.group(buf.at[0, 0, 0], self.has_up)
        self.o_down = wires.group(buf.at[0, 0, 0], self.has_down)
        self.oz = wires.group(buf.at[0, 0, pl.ds(0, NZ - 1)], self.has_up & self.has_down)
        first = jnp.where(z == 0, 3, 1)
        last = jnp.where(z == 0, 1, jnp.where(z == NZ - 1, 3, 2))
        self.order = (first, 6 - first - last, last)
        self.ox, self.oy = wires.group(row), wires.group(row)
        self.oe = wires.group(buf.at[0, 0, :, pl.ds(0, self.half)])
        self.of = wires.group(buf.at[0, 0, :, pl.ds(0, self.half)])
        self.op = wires.group(buf.at[0])

    def block(self, step, w):
        return self.buf.at[self.at.d, self.at.down(step), w]

    def top(self, ref):
        return ref.at[pl.ds(0, self.half)]

    def low(self, ref):
        return ref.at[pl.ds(self.half, self.half)]

    def send_z(self, src):
        p = self.at
        dst = self.block(0, p.w)

        @pl.when(self.has_up)
        def _():
            self.wires.start(src, dst, self.sz, p.along_z(1), self.o_up)

        @pl.when(self.has_down)
        def _():
            self.wires.start(src, dst, self.sz + NZ - 2, p.along_z(NZ - 1), self.o_down)

    def wait_z(self, step):
        self.wires.landed(self.block(step, self.at.w), self.sz + step - 1, self.at.along_z(step))

    def pass_z(self, step):
        p = self.at
        self.wait_z(step)
        b = self.block(step, p.w)

        @pl.when((p.z >= step) & self.has_up)
        def _():
            self.wires.start(b, b, self.sz + step, p.along_z(1), self.oz)

        @pl.when((p.z < step) & self.has_down)
        def _():
            self.wires.start(b, b, self.sz + step - 2, p.along_z(NZ - 1), self.oz)

    def send_plane(self, step):
        p, b = self.at, self.block(step, self.at.w)
        self.wires.start(b, b, self.sx + step, p.across_x, self.ox)
        self.wires.start(b, b, self.sy + step, p.across_y, self.oy)

    def send_core(self, group, step):
        p = self.at
        b = self.block(step, (p.w, p.w1, p.w2, p.w3)[group])
        self.wires.start(b, b, self.sp, p.partner, self.op)

    def relay_plane(self, step):
        p = self.at
        bx, by = self.block(step, p.w1), self.block(step, p.w2)
        self.wires.landed(bx, self.sx + step, p.across_x)
        self.wires.start(self.top(bx), self.top(bx), self.se + step, p.across_y, self.oe)
        self.send_core(1, step)
        self.wires.landed(by, self.sy + step, p.across_y)
        self.wires.start(self.low(by), self.low(by), self.sf + step, p.across_x, self.of)
        self.send_core(2, step)

    def relay_corner(self, step):
        p, b = self.at, self.block(step, self.at.w3)
        self.wires.landed(self.top(b), self.se + step, p.across_y)
        self.wires.landed(self.low(b), self.sf + step, p.across_x)
        self.send_core(3, step)

    def wait_core(self):
        self.wires.landed(self.buf.at[self.at.other], self.sp, self.at.partner)


class Scatter:
    def __init__(self, wires, place, buf, from_core, from_x, from_y, relay, column, from_z):
        self.wires, self.at, self.buf = wires, place, buf
        self.from_core, self.from_x, self.from_y = from_core, from_x, from_y
        self.relay, self.column, self.from_z = relay, column, from_z
        self.rows = buf.shape[3]
        self.half = self.rows // 2
        self.sp = wires.slots(1)
        self.sx, self.sy = wires.slots(3), wires.slots(3)
        self.sz = wires.slots(NZ - 1)

    def part(self, w, low):
        return self.buf.at[self.at.d, :, w, pl.ds(self.half if low else 0, self.half)]

    def send_core(self):
        p = self.at
        self.wires.start(self.buf.at[p.other], self.from_core, self.sp, p.partner)

    def add_core(self):
        p = self.at
        self.wires.landed(self.from_core, self.sp, p.partner)

        def add(k, carry):
            z, w = k // NW, lax.rem(k, NW)
            mine = self.buf[p.d, z, w].astype(F32)
            self.buf[p.d, z, w] = (mine + self.from_core[z, w].astype(F32)).astype(BF16)
            return carry

        lax.fori_loop(0, NC, add, 0)

    def send_plane(self):
        p = self.at
        for k, w in enumerate((p.w3, p.w1)):
            self.wires.start(self.part(w, False), self.from_x.at[k], self.sx + k, p.across_x)
        for k, w in enumerate((p.w3, p.w2)):
            self.wires.start(self.part(w, True), self.from_y.at[k], self.sy + k, p.across_y)

    def relay_corner(self):
        p, h = self.at, self.half
        self.wires.landed(self.from_x.at[0], self.sx, p.across_x)

        def add_top(z, carry):
            mine = self.buf[p.d, z, p.w2, pl.ds(0, h)].astype(F32)
            self.relay[0, z] = (mine + self.from_x[0, z].astype(F32)).astype(BF16)
            return carry

        lax.fori_loop(0, NZ, add_top, 0)
        self.wires.start(self.relay.at[0], self.from_y.at[2], self.sy + 2, p.across_y)
        self.wires.landed(self.from_y.at[0], self.sy, p.across_y)

        def add_low(z, carry):
            mine = self.buf[p.d, z, p.w1, pl.ds(h, h)].astype(F32)
            self.relay[1, z] = (mine + self.from_y[0, z].astype(F32)).astype(BF16)
            return carry

        lax.fori_loop(0, NZ, add_low, 0)
        self.wires.start(self.relay.at[1], self.from_x.at[2], self.sx + 2, p.across_x)

    def send_z(self):
        p, h = self.at, self.half
        self.wires.landed(self.from_x.at[1], self.sx + 1, p.across_x)
        self.wires.landed(self.from_y.at[1], self.sy + 1, p.across_y)
        self.wires.landed(self.from_y.at[2], self.sy + 2, p.across_y)
        self.wires.landed(self.from_x.at[2], self.sx + 2, p.across_x)

        def add(z, carry):
            top = self.buf[p.d, z, p.w, pl.ds(0, h)].astype(F32)
            top = top + self.from_x[1, z].astype(F32) + self.from_y[2, z].astype(F32)
            self.column[z, pl.ds(0, h)] = top.astype(BF16)
            low = self.buf[p.d, z, p.w, pl.ds(h, h)].astype(F32)
            low = low + self.from_y[1, z].astype(F32) + self.from_x[2, z].astype(F32)
            self.column[z, pl.ds(h, h)] = low.astype(BF16)
            return carry

        lax.fori_loop(0, NZ, add, 0)
        for step in range(1, NZ):
            self.wires.start(
                self.column.at[p.up(step)], self.from_z.at[step - 1], self.sz + step - 1, p.along_z(step)
            )

    def total(self):
        p = self.at
        for step in range(1, NZ):
            self.wires.landed(self.from_z.at[step - 1], self.sz + step - 1, p.along_z(step))
        acc = self.column[p.z].astype(F32)
        for step in range(1, NZ):
            acc = acc + self.from_z[step - 1].astype(F32)
        return acc


class Exchange:
    def __init__(self, wires, place, src, dst, inner=None):
        self.wires, self.at, self.src, self.dst = wires, place, src, dst
        self.inner = inner
        self.slot = wires.slots(1)
        self.rest = dst.at[pl.ds(0, NC - 1)] if inner is None else dst.at[pl.ds(0, NC - 1), inner]
        self.out = wires.group(self.rest)

    def view(self, ref, k):
        return ref.at[k] if self.inner is None else ref.at[k, self.inner]

    def send(self, offset):
        to = lax.rem(self.at.me + offset, NC)
        return self.wires.copy(
            self.view(self.src, to), self.view(self.dst, self.at.me), self.slot, {"ctx": to}, self.out
        )

    def send_to(self, chip):
        offset = lax.rem(chip - self.at.me + NC, NC)

        @pl.when(offset > 0)
        def _():
            self.send(offset).start()

        @pl.when(offset == 0)
        def _():
            self.keep()

    def keep(self):
        me = self.at.me
        if self.inner is None:
            self.dst[me] = self.src[me]
        else:
            self.dst[me, self.inner] = self.src[me, self.inner]

    def send_all(self):
        for offset in range(1, NC):
            self.send(offset).start()
        self.keep()

    def wait(self):
        self.wires.landed(self.rest, self.slot, self.at.partner)


def norm_stats(v):
    centred = v - jnp.mean(v, axis=0, keepdims=True)
    rstd = lax.rsqrt(jnp.mean(centred * centred, axis=0, keepdims=True) + EPS)
    return centred * rstd, rstd


def norm_back(grad, hat, rstd, gain):
    g = grad * gain
    return rstd * (g - jnp.mean(g, axis=0, keepdims=True) - hat * jnp.mean(g * hat, axis=0, keepdims=True))


def gelu_both(p):
    t = jnp.tanh(GELU_A * (p + GELU_B * p * p * p))
    half = 0.5 * (1.0 + t)
    slope = half + 0.5 * p * (1.0 - t * t) * (GELU_A * (1.0 + 3.0 * GELU_B * p * p))
    return p * half, slope


def step_kernel(
    prefix_ref, x_hbm, dy_hbm, gains_hbm, wq_hbm, wo_hbm, wu_hbm, wd_hbm,
    out_hbm, gx_hbm, gq_hbm, go_hbm, gu_hbm, gd_hbm, g1_hbm, g2_hbm,
    send_sem, recv_sem, own_sem,
    x_ref, dy_ref, WU, out_ref, gx_ref, gq_ref, gf_ref, GU, G1, G2,
    QG, FG, HAT1, RST1, NRM, DYT,
    QS, QR, KN, VN, PR, OT, LI, TOP, LAST, AS, AR, ATT,
    RES, HAT2, RST2, NRM2, ACT, SLOPE, DPRE, ACC, DRES, DAI,
    DS, DR, DEL, DQ, DQS, DPR, DPJ,
    GF, GFC, GFX, GFY, GFR, GFS, GFZ,
    GQ, GQC, GQX, GQY, GQR, GQS, GQZ,
    TS, TR,
):
    place = Place()
    wires = Wires(send_sem, recv_sem)
    me = place.me
    width = HAT1.shape[0]
    heads = width // DH
    half = width // 2
    qrows, frows = QG.shape[3], FG.shape[3]
    nq = PR.shape[0]
    pre_blocks = nq // 2
    orow = width // NC
    urow = ACT.shape[0] * BQ // NC
    nf = ACT.shape[0]

    gq = Gather(wires, place, QG)
    gf = Gather(wires, place, FG)
    qkv_x = Exchange(wires, place, QS, QR)
    att_x = Exchange(wires, place, AS, AR)
    datt_x = Exchange(wires, place, DS, DR)
    dkv_x = Exchange(wires, place, DQS, DPR, pl.ds(1, 2))
    dq_x = Exchange(wires, place, DQS, DPR, pl.ds(0, 1))
    sf = Scatter(wires, place, GF, GFC, GFX, GFY, GFR, GFS, GFZ)
    sq = Scatter(wires, place, GQ, GQC, GQX, GQY, GQR, GQS, GQZ)
    tot = wires.slots(6)

    barrier = pltpu.get_barrier_semaphore()
    for offset in range(1, NC):
        pl.semaphore_signal(barrier, inc=1, device_id={"ctx": lax.rem(me + offset, NC)}, device_id_type=MESH)
    pl.semaphore_signal(barrier, inc=1, device_id=place.partner, device_id_type=MESH)

    mine_q, mine_f = gq.block(0, place.w), gf.block(0, place.w)
    local = [0]

    def local_copy(src, dst):
        c = pltpu.make_async_copy(src, dst, own_sem.at[local[0]])
        local[0] += 1
        c.start()
        return c

    first = [
        local_copy(gains_hbm, mine_q.at[pl.ds(0, GROWS)]),
        local_copy(wq_hbm, mine_q.at[pl.ds(GROWS, qrows - GROWS)]),
    ]
    words_in = local_copy(x_hbm, x_ref)
    up_in = local_copy(wu_hbm, WU)
    rest = [local_copy(wo_hbm, mine_f.at[pl.ds(0, orow)])]
    for c in range(4):
        rest.append(
            local_copy(wd_hbm.at[:, pl.ds(c * 256, 256)], mine_f.at[pl.ds(orow + urow + c * orow, orow)])
        )
    dy_in = local_copy(dy_hbm, dy_ref)
    for c in first:
        c.wait()
    pl.semaphore_wait(barrier, NC)

    gq.send_z(gq.block(0, place.w))
    gq.send_plane(0)
    gq.send_core(0, 0)

    up_in.wait()
    FG[place.d, place.z, place.w, pl.ds(orow, urow), :] = WU[...].astype(F32).T.astype(BF16)
    words_in.wait()
    hat, rstd = norm_stats(x_ref[...].astype(F32).T)
    HAT1[...] = hat
    RST1[...] = rstd
    for c in rest:
        c.wait()
    gf.send_plane(0)
    gf.send_core(0, 0)

    for step in gq.order:
        gq.pass_z(step)
        gq.send_plane(step)
        gq.send_core(0, step)
    gf.send_z(gf.block(0, place.w))
    dy_in.wait()
    DYT[...] = dy_ref[...].astype(F32).T.astype(BF16)
    for step in (0, *gq.order):
        gq.relay_plane(step)
    gf.pass_z(gf.order[0])
    for step in (0, *gq.order):
        gq.relay_corner(step)
    gf.pass_z(gf.order[1])
    gq.wait_core()
    gf.pass_z(gf.order[2])

    gains = QG[0, :, :, pl.ds(0, GROWS), :].reshape(NC * GROWS, 256).astype(F32).T
    gain_one, gain_two = (
        jnp.concatenate([gains[r:r + orow, k * GROWS:k * GROWS + 1] for k in range(NC)], axis=0) for r in (0, 128)
    )
    NRM[...] = (HAT1[...] * gain_one).astype(BF16)
    wrows = qrows - GROWS
    for j in range(NZ):
        proj = sum(
            dot(QG[k, j, :, pl.ds(GROWS, wrows), :].reshape(NW * wrows, 256), NRM[k * half:(k + 1) * half])
            for k in range(ND)
        )
        for t in range(NW * wrows // DH):
            kind, head = divmod(j * (NW * wrows // DH) + t, heads)
            unit = proj[t * DH:(t + 1) * DH].astype(BF16)
            if kind == 0:
                unit = (unit.astype(F32) * DH ** (-0.5)).astype(BF16)
            for b in range(2):
                QS[b * heads + head, kind] = unit[:, b * WORDS:(b + 1) * WORDS]
    qkv_x.send_all()

    for step in gf.order:
        gf.send_plane(step)
        gf.send_core(0, step)

    gf.relay_plane(0)
    qkv_x.wait()
    prefix = prefix_ref[me // heads]

    def to_rows(c, carry):
        rows = pl.ds(pl.multiple_of(c * WORDS, WORDS), WORDS)
        KN[rows, :] = QR[c, 1].astype(F32).T.astype(BF16)
        VN[rows, :] = QR[c, 2].astype(F32).T.astype(BF16)
        return carry

    lax.fori_loop(0, NC, to_rows, 0)

    def pair(ref, b, kind=None):
        parts = [ref[PACK * b + k] if kind is None else ref[PACK * b + k, kind] for k in range(PACK)]
        return jnp.concatenate(parts, axis=1)

    def rows_of(b):
        return pl.ds(pl.multiple_of(b * BA, BA), BA)

    def attend(qb, carry):
        queries = pair(QR, qb, 0)

        def step(masked, kb, state):
            top, total, acc = state
            s = dot(KN[rows_of(kb), :], queries)
            if masked:
                key = kb * BA + lax.broadcasted_iota(jnp.int32, (BA, BA), 0)
                word = qb * BA + lax.broadcasted_iota(jnp.int32, (BA, BA), 1)
                s = jnp.where((key <= word) | (key < prefix), s, NEG)
            high = jnp.max(jnp.max(s.reshape(BA // 8, 8, BA), axis=0), axis=0, keepdims=True)
            new = jnp.maximum(top, high)
            TOP[qb, kb] = new
            scale = jnp.exp(top - new)
            p = jnp.exp(s - new)
            total = total * scale + jnp.sum(p.reshape(BA // 8, 8, BA), axis=0)
            p = p.astype(BF16)
            PR[qb, rows_of(kb), :] = p
            return new, total, acc * scale + dot(pair(QR, kb, 2), p)

        state = (jnp.full((1, BA), NEG, F32), jnp.zeros((8, BA), F32), jnp.zeros((DH, BA), F32))
        state = lax.fori_loop(0, qb, functools.partial(step, False), state)
        last = jnp.maximum(qb + 1, pre_blocks)
        top, total, acc = lax.fori_loop(qb, last, functools.partial(step, True), state)
        inv = 1.0 / jnp.sum(total, axis=0, keepdims=True)
        out = acc * inv
        OT[qb] = out
        LI[qb] = inv
        LAST[qb] = top
        out = out.astype(BF16)
        for k in range(PACK):
            AS[PACK * qb + k] = out[:, k * WORDS:(k + 1) * WORDS]
            att_x.send_to(PACK * qb + k)
        return carry

    lax.fori_loop(0, 2, attend, 0)
    gf.relay_plane(gf.order[0])
    gf.relay_plane(gf.order[1])
    gf.relay_plane(gf.order[2])
    gf.relay_corner(0)
    lax.fori_loop(2, 4, attend, 0)
    gf.relay_corner(gf.order[0])
    gf.relay_corner(gf.order[1])
    gf.relay_corner(gf.order[2])

    att_x.wait()
    gf.wait_core()
    for h in range(heads):
        ATT[h * DH:(h + 1) * DH] = jnp.concatenate([AR[h], AR[heads + h]], axis=1)

    def w_out(k):
        return FG[k, :, :, pl.ds(0, orow), :].reshape(width, 256)

    def w_up(k, c):
        return FG[k, c // 2, pl.ds(2 * (c % 2), 2), pl.ds(orow, urow), :].reshape(BQ, 256)

    def w_down(c):
        rows = orow + urow + (c % 4) * orow
        return FG[c // 4, :, :, pl.ds(rows, orow), :].reshape(width, 256)

    mixed = sum(dot(w_out(k), ATT[k * half:(k + 1) * half]) for k in range(ND))
    res = x_ref[...].astype(F32).T + mixed
    RES[...] = res
    hat2, rstd2 = norm_stats(res)
    HAT2[...] = hat2
    RST2[...] = rstd2
    NRM2[...] = (hat2 * gain_two).astype(BF16)

    for c in range(nf):
        pre = sum(dot(w_up(k, c), NRM2[k * half:(k + 1) * half]) for k in range(ND))
        act, slope = gelu_both(pre)
        ACT[c] = act.astype(BF16)
        SLOPE[c] = slope
    ACC[...] = jnp.zeros_like(ACC)
    for c in range(nf):
        dact = dot(w_down(c), DYT[...], TN)
        dpre = (dact * SLOPE[c]).astype(BF16)
        DPRE[c] = dpre
        for k in range(ND):
            ACC[k * half:(k + 1) * half] += dot(w_up(k, c), dpre, TN)
    dn2 = ACC[...]
    dres = DYT[...].astype(F32) + norm_back(dn2, HAT2[...], RST2[...], gain_two)
    DRES[...] = dres
    DAI[...] = dres.astype(BF16)
    ones = jnp.ones((8, 2 * WORDS), F32)
    row_two = lax.dot_general(
        ones, dn2 * HAT2[...], NT, precision=lax.Precision.HIGHEST, preferred_element_type=F32
    )
    for k in range(ND):
        datt = dot(w_out(k), DAI[...], TN).astype(BF16)
        for t in range(half // DH):
            h = k * (half // DH) + t
            for b in range(2):
                DS[b * heads + h] = datt[t * DH:(t + 1) * DH, b * WORDS:(b + 1) * WORDS]
    datt_x.send_all()

    for c in range(nf):
        rows = orow + urow + (c % 4) * orow
        GF[c // 4, :, :, pl.ds(rows, orow), :] = dot(DYT[...], ACT[c], NT).astype(BF16).reshape(NZ, NW, orow, 256)
        for k in range(ND):
            up = dot(DPRE[c], NRM2[k * half:(k + 1) * half], NT).astype(BF16)
            GF[k, c // 2, pl.ds(2 * (c % 2), 2), pl.ds(orow, urow), :] = up.reshape(2, urow, 256)
    for k in range(ND):
        mix = dot(DAI[...], ATT[k * half:(k + 1) * half], NT).astype(BF16)
        GF[k, :, :, pl.ds(0, orow), :] = mix.reshape(NZ, NW, orow, 256)
    sf.send_core()
    for r in range(2):
        acc = RES[r * half:(r + 1) * half]
        for c in range(nf):
            rows = orow + urow + (c % 4) * orow
            w = FG[c // 4, pl.ds(2 * r, 2), :, pl.ds(rows, orow), :].reshape(half, 256)
            acc = acc + dot(w, ACT[c])
        out_ref[:, r * half:(r + 1) * half] = acc.T.astype(BF16)
    outs = [local_copy(out_ref, out_hbm)]

    datt_x.wait()

    def ready(qb, carry):
        DEL[qb] = sum_rows(pair(DR, qb).astype(F32) * OT[qb])
        DQ[qb] = jnp.zeros((DH, BA), F32)
        return carry

    lax.fori_loop(0, nq, ready, 0)

    def put(ref, b, kind, val):
        val = val.astype(BF16)
        for k in range(PACK):
            ref[PACK * b + k, kind] = val[:, k * WORDS:(k + 1) * WORDS]

    def send_dq(qb):
        put(DQS, qb, 0, DQ[qb] * DH ** (-0.5))
        for k in range(PACK):
            dq_x.send_to(PACK * qb + k)

    def attend_back(kb, carry, finish=False):
        keys, vals, keys_t = KN[rows_of(kb), :], VN[rows_of(kb), :], pair(QR, kb, 1)
        first = jnp.where(kb < pre_blocks, 0, kb)

        def one(qb, state):
            dk, dv = state
            norm = jnp.exp(TOP[qb, kb] - LAST[qb]) * LI[qb]
            datt = (pair(DR, qb).astype(F32) * norm).astype(BF16)
            dp = dot(vals, datt)
            p = PR[qb, rows_of(kb), :]
            ds = (p.astype(F32) * (dp - DEL[qb] * norm)).astype(BF16)
            DQ[qb] += dot(keys_t, ds)
            if finish:
                send_dq(qb)
            return dk + dot(pair(QR, qb, 0), ds, NT), dv + dot(datt, p, NT)

        zero = jnp.zeros((DH, BA), F32)
        dk, dv = lax.fori_loop(first, nq, one, (zero, zero))
        put(DQS, kb, 1, dk)
        put(DQS, kb, 2, dv)
        for k in range(PACK):
            dkv_x.send_to(PACK * kb + k)
        return carry

    def back_from_last(i, carry):
        return attend_back(nq - 1 - i, carry)

    lax.fori_loop(0, 1, back_from_last, 0)
    sf.add_core()
    sf.send_plane()
    lax.fori_loop(1, nq - 1, back_from_last, 0)
    attend_back(0, 0, True)
    sf.relay_corner()
    dq_x.wait()
    dkv_x.wait()

    for kind in range(3):
        for h in range(heads):
            r = (kind * heads + h) * DH
            DPJ[r:r + DH] = jnp.concatenate([DPR[h, kind], DPR[heads + h, kind]], axis=1)
    blk = NW * wrows
    for j in range(NZ):
        for k in range(ND):
            g = dot(DPJ[j * blk:(j + 1) * blk], NRM[k * half:(k + 1) * half], NT)
            GQ[k, j] = g.astype(BF16).reshape(NW, wrows, 256)
    sq.send_core()
    sf.send_z()
    ACC[...] = jnp.zeros_like(ACC)
    for k in range(ND):
        for j in range(NZ):
            w = QG[k, j, :, pl.ds(GROWS, wrows), :].reshape(blk, 256)
            ACC[k * half:(k + 1) * half] += dot(w, DPJ[j * blk:(j + 1) * blk], TN)
    dn1 = ACC[...]
    gx_ref[...] = (DRES[...] + norm_back(dn1, HAT1[...], RST1[...], gain_one)).T
    outs.append(local_copy(gx_ref, gx_hbm))
    row_one = lax.dot_general(
        ones, dn1 * HAT1[...], NT, precision=lax.Precision.HIGHEST, preferred_element_type=F32
    )

    TS[0] = jnp.where(lax.broadcasted_iota(jnp.int32, (8, width), 0) == 0, row_one, row_two)
    wires.start(TS.at[0], TR.at[0], tot, place.partner)
    sq.add_core()
    sq.send_plane()
    wires.landed(TR.at[0], tot, place.partner)
    TS[1] = TS[0] + TR[0]
    wires.start(TS.at[1], TR.at[1], tot + 1, place.across_x)
    sq.relay_corner()
    wires.landed(TR.at[1], tot + 1, place.across_x)
    TS[2] = TS[1] + TR[1]
    wires.start(TS.at[2], TR.at[2], tot + 2, place.across_y)
    gf_ref[...] = sf.total()
    GU[...] = gf_ref[pl.ds(orow, urow), :].T
    outs.append(local_copy(gf_ref.at[pl.ds(0, orow)], go_hbm))
    outs.append(local_copy(GU, gu_hbm))
    for c in range(4):
        outs.append(local_copy(gf_ref.at[pl.ds(orow + urow + c * orow, orow)], gd_hbm.at[:, pl.ds(c * 256, 256)]))
    sq.send_z()
    wires.landed(TR.at[2], tot + 2, place.across_y)
    TS[3] = TS[2] + TR[2]
    for step in range(1, NZ):
        wires.start(TS.at[3], TR.at[2 + step], tot + 2 + step, place.along_z(step))
    gq_ref[...] = sq.total()
    outs.append(local_copy(gq_ref, gq_hbm))
    for step in range(1, NZ):
        wires.landed(TR.at[2 + step], tot + 2 + step, place.along_z(step))
    picked = lax.broadcasted_iota(jnp.int32, (width, 128), 0) == me * orow + lax.broadcasted_iota(
        jnp.int32, (width, 128), 1
    )
    own = lax.dot_general(
        TS[3] + TR[3] + TR[4] + TR[5], picked.astype(F32), NN,
        precision=lax.Precision.HIGHEST, preferred_element_type=F32,
    )
    G1[...] = own[0:1, 0:orow]
    G2[...] = own[1:2, 0:orow]
    outs.append(local_copy(G1, g1_hbm))
    outs.append(local_copy(G2, g2_hbm))

    assert (wires.out, wires.used, local[0]) == (N_SEND, N_RECV, N_OWN), (wires.out, wires.used, local[0])
    wires.drain(place.partner)
    for c in outs:
        c.wait()


def fused(ctx_count, block_input, prefix, ln1_gain, w_qkv, w_out, ln2_gain, w_up, w_down, grad_y):
    width = block_input.shape[2]
    ff = w_down.shape[0] * ND
    words = 2 * WORDS
    nq = NC * WORDS // BA
    nf = ff // BQ
    orow, qrow, urow = width // NC, 3 * width // NC, ff // NC
    qrows, frows = GROWS + qrow, orow + urow + 4 * orow

    gains = jnp.concatenate([jnp.pad(g, (0, 128 - orow)) for g in (ln1_gain, ln2_gain)])
    gains = jnp.broadcast_to(gains[None], (GROWS, 256))
    x = block_input.reshape(words, width)
    dy = grad_y.reshape(words, width)

    def vm(*shape, dtype=BF16):
        return pltpu.VMEM(shape, dtype)

    def scatter_bufs(rows):
        return [
            vm(ND, NZ, NW, rows, 256),
            vm(NZ, NW, rows, 256),
            vm(3, NZ, rows // 2, 256),
            vm(3, NZ, rows // 2, 256),
            vm(2, NZ, rows // 2, 256),
            vm(NZ, rows, 256),
            vm(NZ - 1, rows, 256),
        ]

    length = NC * WORDS
    msgs = 512
    vmem = pl.BlockSpec(memory_space=pltpu.VMEM)
    hbm = pl.BlockSpec(memory_space=pl.ANY)
    out, gx, gq, g_out, g_up, g_down, g_one, g_two = pl.pallas_call(
        step_kernel,
        out_shape=(
            jax.ShapeDtypeStruct((words, width), BF16),
            jax.ShapeDtypeStruct((words, width), F32),
            jax.ShapeDtypeStruct((qrow, 256), F32),
            jax.ShapeDtypeStruct((orow, 256), F32),
            jax.ShapeDtypeStruct((256, urow), F32),
            jax.ShapeDtypeStruct((orow, 4 * 256), F32),
            jax.ShapeDtypeStruct((1, orow), F32),
            jax.ShapeDtypeStruct((1, orow), F32),
        ),
        in_specs=[pl.BlockSpec(memory_space=pltpu.SMEM)] + [hbm] * 7,
        out_specs=(hbm,) * 8,
        scratch_shapes=[
            pltpu.SemaphoreType.DMA((N_SEND,)),
            pltpu.SemaphoreType.DMA((N_RECV,)),
            pltpu.SemaphoreType.DMA((N_OWN,)),
            vm(words, width),
            vm(words, width),
            vm(256, urow),
            vm(words, width),
            vm(words, width, dtype=F32),
            vm(qrow, 256, dtype=F32),
            vm(frows, 256, dtype=F32),
            vm(256, urow, dtype=F32),
            vm(1, orow, dtype=F32),
            vm(1, orow, dtype=F32),
            vm(ND, NZ, NW, qrows, 256),
            vm(ND, NZ, NW, frows, 256),
            vm(width, words, dtype=F32),
            vm(1, words, dtype=F32),
            vm(width, words),
            vm(width, words),
            vm(NC, 3, DH, WORDS),
            vm(NC, 3, DH, WORDS),
            vm(length, DH),
            vm(length, DH),
            vm(nq, length, BA),
            vm(nq, DH, BA, dtype=F32),
            vm(nq, 1, BA, dtype=F32),
            vm(nq, nq, 1, BA, dtype=F32),
            vm(nq, 1, BA, dtype=F32),
            vm(NC, DH, WORDS),
            vm(NC, DH, WORDS),
            vm(width, words),
            vm(width, words, dtype=F32),
            vm(width, words, dtype=F32),
            vm(1, words, dtype=F32),
            vm(width, words),
            vm(nf, BQ, words),
            vm(nf, BQ, words, dtype=F32),
            vm(nf, BQ, words),
            vm(width, words, dtype=F32),
            vm(width, words, dtype=F32),
            vm(width, words),
            vm(NC, DH, WORDS),
            vm(NC, DH, WORDS),
            vm(nq, 1, BA, dtype=F32),
            vm(nq, DH, BA, dtype=F32),
            vm(NC, 3, DH, WORDS),
            vm(NC, 3, DH, WORDS),
            vm(3 * width, words),
            *scatter_bufs(frows),
            *scatter_bufs(qrow),
            vm(4, 8, width, dtype=F32),
            vm(6, 8, width, dtype=F32),
        ],
        compiler_params=pltpu.CompilerParams(
            collective_id=0, has_side_effects=True, vmem_limit_bytes=66 * 1024 * 1024 - 2 ** 21
        ),
        name="block_step",
    )(prefix, x, dy, gains, w_qkv.T, w_out.T, w_up, w_down.T)

    return (
        out.reshape(block_input.shape),
        gx.reshape(block_input.shape),
        g_one.reshape(ln1_gain.shape),
        gq.T,
        g_out.T,
        g_two.reshape(ln2_gain.shape),
        g_up,
        g_down.T,
    )


N_SEND, N_RECV, N_OWN = 47, 71, 21


def fits(mesh, block_input, w_down):
    seqs, length, width = block_input.shape
    return (
        mesh.shape["ctx"] == NC
        and mesh.shape["dp"] == ND
        and seqs == 2 * ND
        and length == NC * WORDS
        and width == H * DH
        and 2 * H == NC
        and w_down.shape[0] == 4 * width
    )


def layer_norm(values, gain):
    centred = values - jnp.mean(values, axis=-1, keepdims=True)
    spread = jnp.mean(centred * centred, axis=-1, keepdims=True)
    return centred * lax.rsqrt(spread + EPS) * gain


def row_product(left, right):
    return jnp.dot(left, right, preferred_element_type=jnp.float32)


def cross_rows(left, right):
    return lax.dot_general(
        left, right, (((0,), (0,)), ((), ())), preferred_element_type=jnp.float32
    )


def back_product(left, right):
    return lax.dot_general(
        left, right, (((1,), (1,)), ((), ())), preferred_element_type=jnp.float32
    )


def visible_mask(query_first, query_count, key_first, key_count, prefixes):
    query_pos = query_first + jnp.arange(query_count, dtype=jnp.int32)
    key_pos = key_first + jnp.arange(key_count, dtype=jnp.int32)
    causal = key_pos[None, :] <= query_pos[:, None]
    before = key_pos[None, None, :] < prefixes[:, None, None]
    return (causal[None] | before)[:, None]


def attend_forward(queries, keys_own, values_own, prefixes, my_first, scale):
    batch, rows, heads, head_dim = queries.shape
    key_first = jnp.int32(0)
    key_rows = lax.all_gather(keys_own, "ctx", axis=1, tiled=True)
    value_rows = lax.all_gather(values_own, "ctx", axis=1, tiled=True)
    count = key_rows.shape[1]
    top = jnp.full((batch, heads, rows), NEG, jnp.float32)
    summed = jnp.zeros((batch, rows, heads, head_dim), jnp.float32)
    keys_h = key_rows.reshape(batch, count, heads, head_dim)
    values_h = value_rows.reshape(batch, count, heads, head_dim)
    scores = (
        jnp.einsum("bqhd,bkhd->bhqk", queries, keys_h, preferred_element_type=jnp.float32) * scale
    )
    scores = jnp.where(visible_mask(my_first, rows, key_first, count, prefixes), scores, NEG)
    new_top = jnp.maximum(top, jnp.max(scores, axis=-1))
    factor = jnp.exp(top - new_top)
    probs = jnp.exp(scores - new_top[..., None])
    total = jnp.sum(probs, axis=-1)
    summed = summed * jnp.swapaxes(factor, 1, 2)[..., None] + jnp.einsum(
        "bhqk,bkhd->bqhd", probs.astype(jnp.bfloat16), values_h, preferred_element_type=jnp.float32
    )
    top, total, summed = (new_top, total, summed)
    attended = summed / jnp.swapaxes(total, 1, 2)[..., None]
    log_sum = top + jnp.log(total)
    return (attended.reshape(batch, rows, heads * head_dim), log_sum)


def attend_backward(
    queries, keys_own, values_own, attended, grad_att, log_sum, prefixes, my_first, scale
):
    batch, rows, heads, head_dim = queries.shape
    width = heads * head_dim
    keys_full, values_full = (
        lax.all_gather(keys_own, "ctx", axis=1, tiled=True),
        lax.all_gather(values_own, "ctx", axis=1, tiled=True),
    )
    length = keys_full.shape[1]
    key_block = math.gcd(length, 512)
    grad_h = grad_att.reshape(batch, rows, heads, head_dim)
    delta = jnp.swapaxes(
        jnp.sum(
            grad_h.astype(jnp.float32) * attended.reshape(batch, rows, heads, head_dim), axis=-1
        ),
        1,
        2,
    )

    def one_block(counter, carried):
        key_first = counter * key_block
        q_sum, k_sum, v_sum = carried
        keys_h = lax.dynamic_slice_in_dim(keys_full, key_first, key_block, 1).reshape(
            batch, key_block, heads, head_dim
        )
        values_h = lax.dynamic_slice_in_dim(values_full, key_first, key_block, 1).reshape(
            batch, key_block, heads, head_dim
        )
        scores = (
            jnp.einsum("bqhd,bkhd->bhqk", queries, keys_h, preferred_element_type=jnp.float32)
            * scale
        )
        scores = jnp.where(
            visible_mask(my_first, rows, key_first, key_block, prefixes), scores, NEG
        )
        probs = jnp.exp(scores - log_sum[..., None])
        grad_probs = jnp.einsum(
            "bqhd,bkhd->bhqk", grad_h, values_h, preferred_element_type=jnp.float32
        )
        grad_scores = (probs * (grad_probs - delta[..., None])).astype(jnp.bfloat16)
        q_sum = (
            q_sum
            + jnp.einsum("bhqk,bkhd->bqhd", grad_scores, keys_h, preferred_element_type=jnp.float32)
            * scale
        )
        v_part = jnp.einsum(
            "bhqk,bqhd->bkhd",
            probs.astype(jnp.bfloat16),
            grad_h,
            preferred_element_type=jnp.float32,
        )
        k_part = (
            jnp.einsum("bhqk,bqhd->bkhd", grad_scores, queries, preferred_element_type=jnp.float32)
            * scale
        )
        k_sum = lax.dynamic_update_slice_in_dim(
            k_sum, k_part.reshape(batch, key_block, width), key_first, 1
        )
        v_sum = lax.dynamic_update_slice_in_dim(
            v_sum, v_part.reshape(batch, key_block, width), key_first, 1
        )
        return (q_sum, k_sum, v_sum)

    initial = (
        jnp.zeros((batch, rows, heads, head_dim), jnp.float32),
        jnp.zeros((batch, length, width), jnp.float32),
        jnp.zeros((batch, length, width), jnp.float32),
    )
    q_sum, k_sum, v_sum = lax.fori_loop(0, length // key_block, one_block, initial)
    k_own, v_own = (
        lax.psum_scatter(k_sum.astype(jnp.bfloat16), "ctx", scatter_dimension=1, tiled=True).astype(
            jnp.float32
        ),
        lax.psum_scatter(v_sum.astype(jnp.bfloat16), "ctx", scatter_dimension=1, tiled=True).astype(
            jnp.float32
        ),
    )
    return (q_sum.reshape(batch, rows, width), k_own, v_own)


def local(block_input, prefix, ln1_gain, w_qkv, w_out, ln2_gain, w_up, w_down, grad_y):
    ctx_count = lax.axis_size("ctx")
    blk_rows = block_input.shape[1]
    width = block_input.shape[2]
    head_dim = width // H
    scale = head_dim ** (-0.5)
    my_first = lax.axis_index("ctx") * blk_rows
    per_micro = block_input.shape[0] // MICRO
    by_ctx = (
        lax.all_gather(w_qkv, "ctx", axis=1, tiled=True),
        lax.all_gather(w_out, "ctx", axis=1, tiled=True),
        lax.all_gather(w_up, "ctx", axis=1, tiled=True),
        lax.all_gather(w_down, "ctx", axis=1, tiled=True),
        lax.all_gather(ln1_gain, "ctx", axis=0, tiled=True),
        lax.all_gather(ln2_gain, "ctx", axis=0, tiled=True),
    )
    full_fwd = (
        lax.all_gather(by_ctx[0], "dp", axis=0, tiled=True),
        lax.all_gather(by_ctx[1], "dp", axis=0, tiled=True),
        lax.all_gather(by_ctx[2], "dp", axis=0, tiled=True),
        lax.all_gather(by_ctx[3], "dp", axis=0, tiled=True),
    )
    gain_one = by_ctx[4].astype(jnp.float32)
    gain_two = by_ctx[5].astype(jnp.float32)
    saved = []
    outputs = []
    for micro_idx in range(MICRO):
        lower_row = micro_idx * per_micro
        inputs = block_input[lower_row : lower_row + per_micro].astype(jnp.float32)
        prefixes = prefix[lower_row : lower_row + per_micro]
        flat = inputs.reshape(-1, width)
        normed = layer_norm(flat, gain_one).astype(jnp.bfloat16)
        projected = (
            row_product(normed, full_fwd[0])
            .astype(jnp.bfloat16)
            .reshape(per_micro, blk_rows, 3 * width)
        )
        queries = projected[..., :width].reshape(per_micro, blk_rows, H, head_dim)
        keys_own = projected[..., width : 2 * width]
        values_own = projected[..., 2 * width :]
        attended, log_sum = attend_forward(queries, keys_own, values_own, prefixes, my_first, scale)
        mixed_in = attended.reshape(-1, width).astype(jnp.bfloat16)
        resid = flat + row_product(mixed_in, full_fwd[1])
        normed_two = layer_norm(resid, gain_two).astype(jnp.bfloat16)
        hidden_pre = row_product(normed_two, full_fwd[2])
        activated = jax.nn.gelu(hidden_pre).astype(jnp.bfloat16)
        result = resid + row_product(activated, full_fwd[3])
        outputs.append(result.astype(jnp.bfloat16).reshape(per_micro, blk_rows, width))
        saved.append(
            (
                flat,
                normed,
                queries,
                keys_own,
                values_own,
                attended,
                log_sum,
                mixed_in,
                resid,
                normed_two,
                hidden_pre,
                activated,
                prefixes,
            )
        )
    back_ctx = (
        lax.all_gather(w_qkv, "ctx", axis=1, tiled=True),
        lax.all_gather(w_out, "ctx", axis=1, tiled=True),
        lax.all_gather(w_up, "ctx", axis=1, tiled=True),
        lax.all_gather(w_down, "ctx", axis=1, tiled=True),
    )
    w_back = (
        lax.all_gather(back_ctx[0], "dp", axis=0, tiled=True),
        lax.all_gather(back_ctx[1], "dp", axis=0, tiled=True),
        lax.all_gather(back_ctx[2], "dp", axis=0, tiled=True),
        lax.all_gather(back_ctx[3], "dp", axis=0, tiled=True),
    )
    sum_proj = jnp.zeros(w_back[0].shape, jnp.float32)
    sum_mix = jnp.zeros(w_back[1].shape, jnp.float32)
    sum_expand = jnp.zeros(w_back[2].shape, jnp.float32)
    sum_reduce = jnp.zeros(w_back[3].shape, jnp.float32)
    gain_acc_one = jnp.zeros((width,), jnp.float32)
    gain_acc_two = jnp.zeros((width,), jnp.float32)
    grad_parts = [None] * MICRO
    for micro_idx in reversed(range(MICRO)):
        (
            flat,
            normed,
            queries,
            keys_own,
            values_own,
            attended,
            log_sum,
            mixed_in,
            resid,
            normed_two,
            hidden_pre,
            activated,
            prefixes,
        ) = saved[micro_idx]
        lower_row = micro_idx * per_micro
        cot_b = grad_y[lower_row : lower_row + per_micro].reshape(-1, width)
        cotangent = cot_b.astype(jnp.float32)
        sum_reduce = sum_reduce + cross_rows(activated, cot_b)
        grad_act = back_product(cot_b, w_back[3])
        gelu_pull = jax.vjp(jax.nn.gelu, hidden_pre)[1]
        grad_hidden = gelu_pull(grad_act)[0].astype(jnp.bfloat16)
        sum_expand = sum_expand + cross_rows(normed_two, grad_hidden)
        grad_normed_two = back_product(grad_hidden, w_back[2])
        norm_pull_two = jax.vjp(layer_norm, resid, gain_two)[1]
        grad_resid_part, grad_gain_two = norm_pull_two(grad_normed_two)
        grad_resid = cotangent + grad_resid_part
        grad_mix_b = grad_resid.astype(jnp.bfloat16)
        sum_mix = sum_mix + cross_rows(mixed_in, grad_mix_b)
        grad_attended = back_product(grad_mix_b, w_back[1]).astype(jnp.bfloat16)
        q_grad, k_grad, v_grad = attend_backward(
            queries,
            keys_own,
            values_own,
            attended,
            grad_attended.reshape(per_micro, blk_rows, width),
            log_sum,
            prefixes,
            my_first,
            scale,
        )
        grad_proj = (
            jnp.concatenate([q_grad, k_grad, v_grad], axis=-1)
            .reshape(-1, 3 * width)
            .astype(jnp.bfloat16)
        )
        sum_proj = sum_proj + cross_rows(normed, grad_proj)
        grad_normed = back_product(grad_proj, w_back[0])
        norm_pull_one = jax.vjp(layer_norm, flat, gain_one)[1]
        grad_in_part, grad_gain_one = norm_pull_one(grad_normed)
        grad_parts[micro_idx] = (grad_resid + grad_in_part).reshape(per_micro, blk_rows, width)
        gain_acc_one = gain_acc_one + grad_gain_one
        gain_acc_two = gain_acc_two + grad_gain_two
    red_ctx = (
        lax.psum_scatter(
            sum_proj.astype(jnp.bfloat16), "ctx", scatter_dimension=1, tiled=True
        ).astype(jnp.float32),
        lax.psum_scatter(
            sum_mix.astype(jnp.bfloat16), "ctx", scatter_dimension=1, tiled=True
        ).astype(jnp.float32),
        lax.psum_scatter(
            sum_expand.astype(jnp.bfloat16), "ctx", scatter_dimension=1, tiled=True
        ).astype(jnp.float32),
        lax.psum_scatter(
            sum_reduce.astype(jnp.bfloat16), "ctx", scatter_dimension=1, tiled=True
        ).astype(jnp.float32),
    )
    red_dp = (
        lax.psum_scatter(
            red_ctx[0].astype(jnp.bfloat16), "dp", scatter_dimension=0, tiled=True
        ).astype(jnp.float32),
        lax.psum_scatter(
            red_ctx[1].astype(jnp.bfloat16), "dp", scatter_dimension=0, tiled=True
        ).astype(jnp.float32),
        lax.psum_scatter(
            red_ctx[2].astype(jnp.bfloat16), "dp", scatter_dimension=0, tiled=True
        ).astype(jnp.float32),
        lax.psum_scatter(
            red_ctx[3].astype(jnp.bfloat16), "dp", scatter_dimension=0, tiled=True
        ).astype(jnp.float32),
    )
    gain_total = lax.psum(jnp.stack([gain_acc_one, gain_acc_two]), ("dp", "ctx"))
    shard_width = width // ctx_count
    own_gains = lax.dynamic_slice_in_dim(
        gain_total, lax.axis_index("ctx") * shard_width, shard_width, 1
    )
    output = jnp.concatenate(outputs, axis=0)
    grad_input = jnp.concatenate(grad_parts, axis=0)
    return (
        output,
        grad_input,
        own_gains[0],
        red_dp[0],
        red_dp[1],
        own_gains[1],
        red_dp[2],
        red_dp[3],
    )


def solution(mesh):
    row, split = P("dp", "ctx"), P("dp", "ctx", None)
    in_specs = (split, P("dp"), P("ctx"), row, row, P("ctx"), row, row, split)
    out_specs = (split, split, P("ctx"), row, row, P("ctx"), row, row)

    def run(block_input, prefix, ln1_gain, w_qkv, w_out, ln2_gain, w_up, w_down, grad_y):
        body = functools.partial(fused, NC) if fits(mesh, block_input, w_down) else local
        return jax.shard_map(body, mesh=mesh, in_specs=in_specs, out_specs=out_specs, check_vma=False)(
            block_input, prefix, ln1_gain, w_qkv, w_out, ln2_gain, w_up, w_down, grad_y
        )

    return run
```
